32 devices in a mesh: gx: 4 (over z), gy: 8 (over y, x, core).
Axes of the slice: x: 2, y: 2, z: 4, core: 2. Of those that a mesh axis runs over, the one named last changes fastest.
Arguments:
- features: bfloat16 [256, 20480], P(None, ('gx', 'gy')), may hold values from 0 to 1.5
- w_first: bfloat16 [20480, 256], P(('gx', 'gy')), may hold values from -0.078125 to 0.078125
- w_label: bfloat16 [256, 90112], P(None, ('gx', 'gy')), may hold values from -42 to 42
- label_ids: int32 [256, 8], replicated, may hold values from 0 to 90111, as said below
- label_count: int32 [256], replicated, may hold values from 1 to 8
Outputs:
- grad_first: bfloat16 [20480, 256], P(('gx', 'gy'))
- grad_label: bfloat16 [256, 90112], P(None, ('gx', 'gy'))
- mean_loss: float32 [], replicated
The draws below stay inside these ranges and needn't reach their ends.
Inputs may be any that keep to these rules, and one draw needn't show every extreme that they name: `label_ids`: each document's 8 ids are distinct labels; slots at or past label_count are filled with ids that are ignored.
All inputs are finite; a program needn't handle non-finite values.
Results may differ from the reference program's by a relative error of at most 0.0085.
Values may be sent and summed in bfloat16 or wider, within the bound.
No kernel may reach another device: no remote copies, remote signals or barrier semaphores. Data moves between devices by JAX's collectives and lax.ppermute only.
A program may use at most 64 MiB of HBM per device.

```python
import jax
import jax.numpy as jnp
from jax import lax

B = 256
H = 256
LAB_DEV = 2816
MAXLAB = 8
FEAT = 20480
LABELS = 90112
N_GX = 4
N_GY = 8


def draw_w_label(key, part):
    base_key = jax.random.fold_in(jax.random.fold_in(key, 11), 0)
    values = jnp.clip(0.3 * jax.random.normal(base_key, (H, LABELS), jnp.float32), -1.8, 1.8)
    return values.astype(jnp.bfloat16)


def draw_label_ids(key, part):
    shift_key, place_key = jax.random.split(jax.random.fold_in(key, 23))
    label_gap = LABELS // MAXLAB
    shifts = jax.random.randint(shift_key, (B, 1), 0, LABELS)
    places = jax.random.randint(place_key, (B, MAXLAB), 0, label_gap)
    slots = jnp.arange(MAXLAB, dtype=jnp.int32)[None, :] * label_gap
    return ((shifts + slots + places) % LABELS).astype(jnp.int32)


def plant(result, key, smallest, largest):
    longest = result.shape.index(max(result.shape))
    spots = []
    for shift in (0, 1):
        where = [jax.random.randint(jax.random.fold_in(key, axis), (), 0, length) for axis, length in enumerate(result.shape)]
        where[longest] = (where[longest] + shift) % result.shape[longest]
        spots.append(tuple(where))
    return result.at[spots[0]].set(smallest).at[spots[1]].set(largest)


def steps_of(own_key, extent, cuts, least, top_value):
    level, own = 1.0, jax.random.fold_in(own_key, 6)
    for dim, shards_of in cuts:
        heights = jnp.exp(jax.random.uniform(jax.random.fold_in(own, dim), (shards_of,), jnp.float32, least / len(cuts), top_value / len(cuts)))
        level = level * jnp.repeat(heights, extent[dim] // shards_of).reshape([-1 if axis == dim else 1 for axis in range(len(extent))])
    return level


def scatter_about(rng, shape, deviation, reach, pieces=(), held_as=jnp.bfloat16):
    values = jax.random.normal(rng, shape, jnp.float32) * deviation
    if len(pieces) > 0:
        values = steps_of(rng, shape, pieces, -0.22, 0.18) * values
    return jnp.clip(values, min=-reach, max=reach).astype(held_as)


def setup_inputs(seed: int = 0) -> dict:
    arg_keys = jax.random.split(jax.random.key(seed), 6)
    return {
        "features": jnp.clip(1.5 * jax.random.uniform(arg_keys[0], (B, FEAT), jnp.float32) ** steps_of(arg_keys[0], (B, FEAT), ((1, 32),), -0.2, 0.2), 0.0, 1.5).astype(jnp.bfloat16),
        "w_first": scatter_about(arg_keys[1], (FEAT, H), (FEAT // 4) ** -0.5, 0.078125, ((0, 32),)),
        "w_label": draw_w_label(jax.random.fold_in(arg_keys[5], 71), 0),
        "label_ids": draw_label_ids(jax.random.fold_in(arg_keys[5], 71), 0),
        "label_count": plant(jax.random.randint(arg_keys[4], (B,), 1, 9), jax.random.fold_in(arg_keys[4], 1), 1, 8).astype(jnp.int32),
    }


def reference(features, w_first, w_label, label_ids, label_count):
    hidden_sum = jnp.dot(features, w_first, preferred_element_type=jnp.float32)
    hidden = jnp.tanh(hidden_sum).astype(jnp.bfloat16)
    block_width = LAB_DEV * N_GY
    column_blocks = w_label.reshape(H, N_GX, block_width).transpose(1, 0, 2)
    in_count = jnp.arange(MAXLAB, dtype=jnp.int32)[None, :] < label_count[:, None]
    doc_count = label_count.astype(hidden_sum.dtype)

    def scan_stats(running, column_block):
        old_max, old_sum = running
        block_logits = jnp.dot(hidden, column_block, preferred_element_type=jnp.float32)
        new_max = jnp.maximum(old_max, jnp.max(block_logits, axis=1))
        new_sum = old_sum * jnp.exp(old_max - new_max) + jnp.sum(jnp.exp(block_logits - new_max[:, None]), axis=1)
        return (new_max, new_sum), None

    start_max = jnp.full((B,), -jnp.inf, dtype=hidden_sum.dtype)
    start_sum = jnp.zeros((B,), dtype=hidden_sum.dtype)
    (row_max, norm_sum), _ = lax.scan(scan_stats, (start_max, start_sum), column_blocks)
    lse = row_max + jnp.log(norm_sum)
    chosen = w_label[:, label_ids]
    positive = jnp.einsum("bh,hbk->bk", hidden.astype(jnp.float32), chosen.astype(jnp.float32))
    picked = jnp.sum(jnp.where(in_count, positive, 0.0), axis=1)
    mean_loss = jnp.mean(lse - picked / doc_count)

    def scan_grads(grad_hidden, inputs):
        column_block, first_label = inputs
        block_logits = jnp.dot(hidden, column_block, preferred_element_type=jnp.float32)
        softmax_prob = jnp.exp(block_logits - lse[:, None])
        local_ids = first_label + jnp.arange(block_width, dtype=jnp.int32)
        matches = jnp.zeros(block_logits.shape, dtype=block_logits.dtype)
        for slot_index in range(MAXLAB):
            hit = in_count[:, slot_index:slot_index + 1] & (label_ids[:, slot_index:slot_index + 1] == local_ids[None, :])
            matches = matches + jnp.where(hit, 1.0, 0.0).astype(block_logits.dtype)
        grad_logits = (softmax_prob - matches / doc_count[:, None]).astype(jnp.bfloat16)
        grad_block = jnp.dot(hidden.T, grad_logits, preferred_element_type=jnp.float32).astype(jnp.bfloat16)
        grad_hidden = grad_hidden + jnp.dot(grad_logits, column_block.T, preferred_element_type=jnp.float32)
        return grad_hidden, grad_block

    first_labels = (jnp.arange(N_GX, dtype=jnp.int32) * block_width).astype(jnp.int32)
    grad_hidden, grad_blocks = lax.scan(scan_grads, jnp.zeros((B, H), dtype=hidden_sum.dtype), (column_blocks, first_labels))
    grad_label = grad_blocks.transpose(1, 0, 2).reshape(H, LABELS)
    hidden_wide = hidden.astype(jnp.float32)
    grad_inner = (grad_hidden * (1.0 - hidden_wide * hidden_wide)).astype(jnp.bfloat16)
    grad_first = jnp.dot(features.T, grad_inner, preferred_element_type=jnp.float32).astype(jnp.bfloat16)
    return grad_first, grad_label, mean_loss
```

```python
import jax
import jax.numpy as jnp
from jax import lax
from jax.sharding import PartitionSpec as P

AXES = ("gx", "gy")
LANES = 128


def split3(x):
    high = lax.reduce_precision(x, 8, 7)
    rest = x - high
    middle = lax.reduce_precision(rest, 8, 7)
    return [part.astype(jnp.bfloat16) for part in (high, middle, rest - middle)]


def join3(parts, at):
    wide = parts[..., at : at + 3].astype(jnp.float32)
    return wide[..., 0] + wide[..., 1] + wide[..., 2]


def lanes_of(columns):
    block = jnp.stack(columns, axis=-1)
    return jnp.pad(block, [(0, 0)] * (block.ndim - 1) + [(0, LANES - len(columns))])


def make_per_device(devices):
    def per_device(features, w_first, w_label, label_ids, label_count):
        docs, hidden_width = features.shape[0], w_first.shape[1]
        rows = max(1, docs // devices)
        cuts = devices * rows // docs
        width = hidden_width // cuts

        def by_owner(x):
            return x.reshape(docs // rows, rows, cuts, -1).swapaxes(1, 2).reshape(devices, rows, -1)

        def by_document(x):
            return x.reshape(docs // rows, cuts, rows, -1).swapaxes(1, 2).reshape(docs, -1)

        def exchange(x):
            return lax.all_to_all(x, AXES, 0, 0)

        def to_all(x):
            return exchange(jnp.broadcast_to(x[None], (devices,) + x.shape))

        place = lax.axis_index(AXES)
        first_row = (place // cuts) * rows
        doc_count = label_count.astype(jnp.float32)
        own_count = lax.dynamic_slice_in_dim(doc_count, first_row, rows)

        partial_value = jnp.dot(features, w_first, preferred_element_type=jnp.float32)
        hidden_sum = jnp.sum(exchange(by_owner(partial_value)), axis=0)
        own_hidden = jnp.tanh(hidden_sum).astype(jnp.bfloat16)
        hidden = by_document(to_all(own_hidden))

        logits = jnp.dot(hidden, w_label, preferred_element_type=jnp.float32)
        label_width = w_label.shape[1]
        local_ids = place * label_width + lax.iota(jnp.int32, label_width)
        slot_total = label_ids.shape[1]
        in_count = lax.iota(jnp.int32, slot_total)[None, :] < label_count[:, None]
        used_ids = jnp.where(in_count, label_ids, -1)
        matches = jnp.zeros(logits.shape, jnp.bool_)
        for slot_index in range(slot_total):
            matches = matches | (used_ids[:, slot_index : slot_index + 1] == local_ids[None, :])
        matches = matches.astype(jnp.bfloat16)
        local_max = jnp.max(logits, axis=1)
        powers = jnp.exp(logits - local_max[:, None])
        local_sum = jnp.sum(powers, axis=1)
        local_lse = local_max + jnp.log(local_sum)

        def times_labels(x):
            return lax.dot_general(
                x, w_label, (((1,), (1,)), ((), ())), preferred_element_type=jnp.float32
            )

        expected = times_labels(powers.astype(jnp.bfloat16)) / local_sum[:, None]
        matched = times_labels(matches)
        stats = lanes_of(split3(local_lse))
        packed = jnp.concatenate(
            [
                expected.astype(jnp.bfloat16).reshape(docs, cuts, width),
                matched.astype(jnp.bfloat16).reshape(docs, cuts, width),
                jnp.broadcast_to(stats[:, None, :], (docs, cuts, LANES)),
            ],
            axis=-1,
        )
        got = exchange(by_owner(packed.reshape(docs, -1)))
        got_expected = got[:, :, :width].astype(jnp.float32)
        got_matched = jnp.sum(got[:, :, width : 2 * width].astype(jnp.float32), axis=0)
        got_lse = join3(got, 2 * width)
        top = jnp.max(got_lse, axis=0)
        own_lse = top + jnp.log(jnp.sum(jnp.exp(got_lse - top), axis=0))
        share = jnp.exp(got_lse - own_lse)
        mean_matched = got_matched / own_count[:, None]
        grad_hidden = jnp.sum(share[:, :, None] * got_expected, axis=0) - mean_matched
        own_wide = own_hidden.astype(jnp.float32)
        grad_inner = (grad_hidden * (1.0 - own_wide * own_wide)).astype(jnp.bfloat16)
        picked = jnp.sum(own_wide * mean_matched, axis=1)
        loss_part = own_lse / cuts - picked
        back = lanes_of(split3(own_lse) + split3(loss_part))
        everyone = to_all(jnp.concatenate([grad_inner, back], axis=-1))
        grad_inner = by_document(everyone[:, :, :width])
        mean_loss = jnp.sum(join3(everyone, width + 3)) / docs
        lse = join3(everyone, width).reshape(docs // rows, cuts, rows)[:, 0].reshape(docs)
        scale = jnp.exp(local_max - lse)
        grad_logits = (powers * scale[:, None] - matches / doc_count[:, None]).astype(jnp.bfloat16)
        grad_label = lax.dot_general(
            hidden, grad_logits, (((0,), (0,)), ((), ())), preferred_element_type=jnp.float32
        ).astype(jnp.bfloat16)
        grad_first = lax.dot_general(
            features, grad_inner, (((0,), (0,)), ((), ())), preferred_element_type=jnp.float32
        ).astype(jnp.bfloat16)
        return (grad_first, grad_label, mean_loss)

    return per_device


def solution(mesh):
    placed = (P(None, AXES), P(AXES, None), P(None, AXES), P(), P())
    devices = mesh.shape["gx"] * mesh.shape["gy"]
    return jax.shard_map(
        make_per_device(devices),
        mesh=mesh,
        in_specs=placed,
        out_specs=(P(AXES, None), P(None, AXES), P()),
        check_vma=False,
    )
```

```python
import functools

import jax
import jax.numpy as jnp
from jax import lax
from jax.experimental import pallas as pl
from jax.experimental.pallas import tpu as pltpu
from jax.sharding import PartitionSpec as P

AXES = ("gx", "gy")
LANES = 128
VMEM = pl.BlockSpec(memory_space=pltpu.VMEM)
SMEM = pl.BlockSpec(memory_space=pltpu.SMEM)
F32, BF16 = jnp.float32, jnp.bfloat16


def chunks_of(length):
    size = next((s for s in (256, 128) if length % s == 0), length)
    return [slice(at, at + size) for at in range(0, length, size)]


def dot(a, b, dims):
    return lax.dot_general(a, b, (dims, ((), ())), preferred_element_type=F32)


def lane(shape):
    return lax.broadcasted_iota(jnp.int32, shape, len(shape) - 1)


def split3(x):
    high = lax.reduce_precision(x, 8, 7)
    rest = x - high
    middle = lax.reduce_precision(rest, 8, 7)
    return high, middle, rest - middle


def into_lanes(columns, shape):
    at = lane(shape)
    block = jnp.zeros(shape, F32)
    for index, column in enumerate(columns):
        block = jnp.where(at == index, column, block)
    return block.astype(BF16)


def from_lanes(block, first):
    wide = block.astype(F32)
    at = lane(wide.shape)
    return jnp.sum(jnp.where((at >= first) & (at < first + 3), wide, 0.0), axis=-1, keepdims=True)


def match_kernel(offset_ref, ids_ref, count_ref, w_label_ref, matches_ref, matched_ref):
    docs, slots = ids_ref.shape
    labels = w_label_ref.shape[1]
    step = 16

    def rows_step(index, _):
        here = pl.ds(pl.multiple_of(index * step, step), step)
        ids = ids_ref[here, :] - offset_ref[0]
        used = jnp.where(lane(ids.shape) < count_ref[here, :], ids, -1)
        wide = [jnp.broadcast_to(used[:, k : k + 1], (step, LANES)) for k in range(slots)]
        for first in range(0, labels, LANES):
            at = lane((step, LANES)) + first
            hit = jnp.zeros((step, LANES), F32)
            for k in range(slots):
                hit = jnp.where(wide[k] == at, 1.0, hit)
            matches_ref[here, first : first + LANES] = hit.astype(BF16)
        return 0

    lax.fori_loop(0, docs // step, rows_step, 0)
    matched_ref[...] = dot(matches_ref[...], w_label_ref[...], ((1,), (1,))).astype(BF16)


def softmax_kernel(hidden_ref, w_label_ref, matched_ref, powers_ref, max_ref, packed_ref):
    docs, width = hidden_ref.shape
    pieces = chunks_of(w_label_ref.shape[1])
    hidden = hidden_ref[...]
    top = None
    for piece in pieces:
        logits = dot(hidden, w_label_ref[:, piece], ((1,), (0,)))
        powers_ref[:, piece] = logits
        top = logits if top is None else jnp.maximum(top, logits)
    local_max = jnp.max(top, axis=1, keepdims=True)
    total, expected = None, None
    for piece in pieces:
        powers = jnp.exp(powers_ref[:, piece] - local_max)
        powers_ref[:, piece] = powers
        part = dot(powers.astype(BF16), w_label_ref[:, piece], ((1,), (1,)))
        total = powers if total is None else total + powers
        expected = part if expected is None else expected + part
    local_sum = jnp.sum(total, axis=1, keepdims=True)
    max_ref[...] = local_max
    packed_ref[:, :width] = (expected / local_sum).astype(BF16)
    packed_ref[:, width : 2 * width] = matched_ref[...]
    lse = local_max + jnp.log(local_sum)
    packed_ref[:, 2 * width :] = into_lanes(split3(lse), (docs, LANES))


def combine(got, own_hidden, own_count, cuts):
    width = own_hidden.shape[-1]
    expected = got[:, :, :width].astype(F32)
    matched = jnp.sum(got[:, :, width : 2 * width].astype(F32), axis=0)
    lse_parts = from_lanes(got[:, :, 2 * width :], 0)
    top = jnp.max(lse_parts, axis=0)
    lse = top + jnp.log(jnp.sum(jnp.exp(lse_parts - top), axis=0))
    mean_matched = matched / own_count
    grad_hidden = jnp.sum(jnp.exp(lse_parts - lse) * expected, axis=0) - mean_matched
    hidden = own_hidden.astype(F32)
    grad_inner = (grad_hidden * (1.0 - hidden * hidden)).astype(BF16)
    picked = jnp.sum(hidden * mean_matched, axis=-1, keepdims=True)
    columns = split3(lse) + split3(lse / cuts - picked)
    return grad_inner, into_lanes(columns, (lse.shape[0], LANES))


def combine_kernel(got_ref, own_hidden_ref, own_count_ref, back_ref):
    width = own_hidden_ref.shape[1]
    grad_inner, tail = combine(got_ref[...], own_hidden_ref[...], own_count_ref[...], 1)
    back_ref[:, :, :width] = jnp.broadcast_to(grad_inner[None], (back_ref.shape[0],) + grad_inner.shape)
    back_ref[:, :, width:] = jnp.broadcast_to(tail[None], (back_ref.shape[0],) + tail.shape)


def gradient_kernel(
    features_ref, hidden_ref, grad_inner_ref, tail_ref, powers_ref, max_ref, matches_ref, count_ref,
    grad_first_ref, grad_label_hbm, loss_ref, label_scratch, sems,
):
    docs = hidden_ref.shape[0]
    tail = tail_ref[...]
    lse = from_lanes(tail, 0)
    loss_ref[...] = jnp.sum(from_lanes(tail, 3), axis=0, keepdims=True) / docs
    scale = jnp.exp(max_ref[...] - lse)
    per_match = 1.0 / count_ref[...].astype(F32)
    hidden = hidden_ref[...]
    pieces = chunks_of(powers_ref.shape[1])
    copies = []
    for index, piece in enumerate(pieces):
        grad_logits = powers_ref[:, piece] * scale - matches_ref[:, piece].astype(F32) * per_match
        value = dot(hidden, grad_logits.astype(BF16), ((0,), (0,)))
        label_scratch[:, piece] = value.astype(BF16)
        copy = pltpu.make_async_copy(
            label_scratch.at[:, piece], grad_label_hbm.at[:, piece], sems.at[index]
        )
        copy.start()
        copies.append(copy)
    grad_first_ref[...] = dot(features_ref[...], grad_inner_ref[...], ((0,), (0,))).astype(BF16)
    for copy in copies:
        copy.wait()


def make_per_device(devices):
    def per_device(features, w_first, w_label, label_ids, label_count):
        docs, hidden_width = features.shape[0], w_first.shape[1]
        feats, labels = features.shape[1], w_label.shape[1]
        rows = max(1, docs // devices)
        cuts = devices * rows // docs
        width = hidden_width // cuts

        def by_owner(x):
            if cuts == 1:
                return x.reshape(devices, rows, -1)
            return x.reshape(docs // rows, rows, cuts, -1).swapaxes(1, 2).reshape(devices, rows, -1)

        def by_document(x):
            if cuts == 1:
                return x.reshape(docs, -1)
            return x.reshape(docs // rows, cuts, rows, -1).swapaxes(1, 2).reshape(docs, -1)

        def exchange(x):
            return lax.all_to_all(x, AXES, 0, 0)

        def to_all(x):
            return exchange(jnp.broadcast_to(x[None], (devices,) + x.shape))

        shape = jax.ShapeDtypeStruct
        place = lax.axis_index(AXES)
        first_row = (place // cuts) * rows
        count_column = label_count[:, None]
        own_count = lax.dynamic_slice_in_dim(count_column, first_row, rows).astype(F32)

        partial_value = jnp.dot(features, w_first, preferred_element_type=F32)
        hidden_sum = jnp.sum(exchange(by_owner(partial_value)), axis=0)
        own_hidden = jnp.tanh(hidden_sum).astype(BF16)
        hidden = by_document(to_all(own_hidden))

        matches, matched = pl.pallas_call(
            match_kernel,
            name="match",
            in_specs=[SMEM, VMEM, VMEM, VMEM],
            out_specs=[VMEM, VMEM],
            out_shape=[shape((docs, labels), BF16), shape((docs, hidden_width), BF16)],
        )((place * labels)[None], label_ids, count_column, w_label)

        powers, local_max, packed = pl.pallas_call(
            softmax_kernel,
            name="softmax",
            in_specs=[VMEM] * 3,
            out_specs=[VMEM] * 3,
            out_shape=[
                shape((docs, labels), F32),
                shape((docs, 1), F32),
                shape((docs, 2 * hidden_width + LANES), BF16),
            ],
        )(hidden, w_label, matched)
        if cuts > 1:
            halves = packed[:, : 2 * hidden_width].reshape(docs, 2, cuts, width)
            tail = jnp.broadcast_to(packed[:, None, 2 * hidden_width :], (docs, cuts, LANES))
            packed = jnp.concatenate([halves[:, 0], halves[:, 1], tail], axis=-1).reshape(docs, -1)
        got = exchange(by_owner(packed))
        if cuts == 1 and rows % 8 == 0:
            back = pl.pallas_call(
                combine_kernel,
                name="combine",
                in_specs=[VMEM] * 3,
                out_specs=VMEM,
                out_shape=shape((devices, rows, width + LANES), BF16),
            )(got, own_hidden, own_count)
            everyone = exchange(back)
        else:
            everyone = to_all(jnp.concatenate(combine(got, own_hidden, own_count, cuts), axis=-1))
        grad_inner = by_document(everyone[:, :, :width])
        tail = by_document(everyone[:, :, width:])
        if cuts > 1:
            tails = tail.reshape(docs, cuts, LANES)
            loss_parts = from_lanes(tails, 3)[:, :, 0]
            lse_columns = from_lanes(tails, 0)[:, 0]
            tail = into_lanes(split3(lse_columns) + split3(jnp.sum(loss_parts, 1, keepdims=True)), (docs, LANES))

        grad_first, grad_label, mean_loss = pl.pallas_call(
            gradient_kernel,
            name="gradient",
            in_specs=[VMEM] * 8,
            out_specs=[VMEM, pl.BlockSpec(memory_space=pl.ANY), VMEM],
            out_shape=[
                shape((feats, hidden_width), BF16),
                shape((hidden_width, labels), BF16),
                shape((1, 1), F32),
            ],
            scratch_shapes=[
                pltpu.VMEM((hidden_width, labels), BF16),
                pltpu.SemaphoreType.DMA((len(chunks_of(labels)),)),
            ],
        )(features, hidden, grad_inner, tail, powers, local_max, matches, count_column)
        return (grad_first, grad_label, mean_loss[0, 0])

    return per_device


def solution(mesh):
    placed = (P(None, AXES), P(AXES, None), P(None, AXES), P(), P())
    devices = mesh.shape["gx"] * mesh.shape["gy"]
    return jax.shard_map(
        make_per_device(devices),
        mesh=mesh,
        in_specs=placed,
        out_specs=(P(AXES, None), P(None, AXES), P()),
        check_vma=False,
    )
```

```python
import jax
import jax.numpy as jnp
from jax import lax
from jax.experimental import pallas as pl
from jax.experimental.pallas import tpu as pltpu
from jax.sharding import PartitionSpec as P

AXES = ("gx", "gy")
LANES = 128
GRANT = 12 * 1024 * 1024
VMEM = pl.BlockSpec(memory_space=pltpu.VMEM)
SMEM = pl.BlockSpec(memory_space=pltpu.SMEM)
F32, BF16 = jnp.float32, jnp.bfloat16


def chunks_of(length):
    size = next((s for s in (256, 128) if length % s == 0), length)
    return [slice(at, at + size) for at in range(0, length, size)]


def dot(a, b, dims):
    return lax.dot_general(a, b, (dims, ((), ())), preferred_element_type=F32)


def lane(shape):
    return lax.broadcasted_iota(jnp.int32, shape, len(shape) - 1)


def split3(x):
    high = lax.reduce_precision(x, 8, 7)
    rest = x - high
    middle = lax.reduce_precision(rest, 8, 7)
    return high, middle, rest - middle


def into_lanes(columns, shape):
    at = lane(shape)
    block = jnp.zeros(shape, F32)
    for index, column in enumerate(columns):
        block = jnp.where(at == index, column, block)
    return block.astype(BF16)


def from_lanes(block, first):
    wide = block.astype(F32)
    at = lane(wide.shape)
    return jnp.sum(jnp.where((at >= first) & (at < first + 3), wide, 0.0), axis=-1, keepdims=True)


def match_kernel(
    offset_ref, ids_ref, count_ref, w_label_ref, features_ref, matches_ref, matched_ref, turned_ref
):
    slots, docs = ids_ref.shape
    labels = w_label_ref.shape[1]
    step = 16
    ids = ids_ref[...]
    in_count = lax.broadcasted_iota(jnp.int32, ids.shape, 0) < count_ref[...]
    used = jnp.where(in_count, ids - offset_ref[0], -1).T
    for first_row in range(0, docs, step):
        here = slice(first_row, first_row + step)
        wide = [jnp.broadcast_to(used[here, k : k + 1], (step, LANES)) for k in range(slots)]
        for first in range(0, labels, LANES):
            at = lane((step, LANES)) + first
            hit = jnp.zeros((step, LANES), F32)
            for k in range(slots):
                hit = jnp.where(wide[k] == at, 1.0, hit)
            matches_ref[here, first : first + LANES] = hit.astype(BF16)
    matched_ref[...] = dot(matches_ref[...], w_label_ref[...], ((1,), (1,))).astype(BF16)
    turned_ref[...] = features_ref[...].T


def softmax_kernel(
    hidden_ref, w_label_ref, matched_ref, powers_ref, max_ref, packed_ref, turned_ref
):
    docs, width = hidden_ref.shape
    pieces = chunks_of(w_label_ref.shape[1])
    hidden = hidden_ref[...]
    top = None
    for piece in pieces:
        logits = dot(hidden, w_label_ref[:, piece], ((1,), (0,)))
        powers_ref[:, piece] = logits
        top = logits if top is None else jnp.maximum(top, logits)
    local_max = jnp.max(top, axis=1, keepdims=True)
    total, expected = None, None
    for piece in pieces:
        powers = jnp.exp(powers_ref[:, piece] - local_max)
        powers_ref[:, piece] = powers
        part = dot(powers.astype(BF16), w_label_ref[:, piece], ((1,), (1,)))
        total = powers if total is None else total + powers
        expected = part if expected is None else expected + part
    local_sum = jnp.sum(total, axis=1, keepdims=True)
    turned_ref[...] = hidden.T
    max_ref[...] = local_max
    packed_ref[:, :width] = (expected / local_sum).astype(BF16)
    packed_ref[:, width : 2 * width] = matched_ref[...]
    lse = local_max + jnp.log(local_sum)
    packed_ref[:, 2 * width :] = into_lanes(split3(lse), (docs, LANES))


def combine(got, own_hidden, own_count, cuts):
    width = own_hidden.shape[-1]
    expected = got[:, :, :width].astype(F32)
    matched = jnp.sum(got[:, :, width : 2 * width].astype(F32), axis=0)
    lse_parts = from_lanes(got[:, :, 2 * width :], 0)
    top = jnp.max(lse_parts, axis=0)
    lse = top + jnp.log(jnp.sum(jnp.exp(lse_parts - top), axis=0))
    mean_matched = matched / own_count
    grad_hidden = jnp.sum(jnp.exp(lse_parts - lse) * expected, axis=0) - mean_matched
    hidden = own_hidden.astype(F32)
    grad_inner = (grad_hidden * (1.0 - hidden * hidden)).astype(BF16)
    picked = jnp.sum(hidden * mean_matched, axis=-1, keepdims=True)
    columns = split3(lse) + split3(lse / cuts - picked)
    return grad_inner, into_lanes(columns, (lse.shape[0], LANES))


def combine_kernel(place_ref, got_ref, own_hidden_ref, count_ref, back_ref):
    rows, width = own_hidden_ref.shape
    docs = count_ref.shape[1]
    owner = lax.broadcasted_iota(jnp.int32, (rows, docs), 0) + place_ref[0] * rows
    counts = jnp.where(lane((rows, docs)) == owner, count_ref[...], 0)
    own_count = jnp.sum(counts.astype(F32), axis=1, keepdims=True)
    grad_inner, tail = combine(got_ref[...], own_hidden_ref[...], own_count, 1)
    back_ref[:, :, :width] = jnp.broadcast_to(grad_inner[None], (back_ref.shape[0],) + grad_inner.shape)
    back_ref[:, :, width:] = jnp.broadcast_to(tail[None], (back_ref.shape[0],) + tail.shape)


def gradient_kernel(
    features_ref, hidden_ref, everyone_ref, powers_ref, max_ref, matches_ref, count_ref,
    grad_first_ref, grad_label_hbm, loss_ref, label_scratch, sems,
):
    width, docs = hidden_ref.shape
    tail = everyone_ref[:, width:]
    lse = from_lanes(tail, 0)
    loss_ref[...] = jnp.sum(from_lanes(tail, 3), axis=0, keepdims=True) / docs
    scale = jnp.exp(max_ref[...] - lse)
    per_match = jnp.broadcast_to(1.0 / count_ref[...].astype(F32), (8, docs)).T[:, :1]
    hidden = hidden_ref[...]
    copies = []
    for index, piece in enumerate(chunks_of(powers_ref.shape[1])):
        grad_logits = powers_ref[:, piece] * scale - matches_ref[:, piece].astype(F32) * per_match
        label_scratch[:, piece] = dot(hidden, grad_logits.astype(BF16), ((1,), (0,))).astype(BF16)
        copy = pltpu.make_async_copy(
            label_scratch.at[:, piece], grad_label_hbm.at[:, piece], sems.at[index]
        )
        copy.start()
        copies.append(copy)
    grad_first_ref[...] = dot(features_ref[...], everyone_ref[:, :width], ((1,), (0,))).astype(BF16)
    for copy in copies:
        copy.wait()


def make_per_device(devices):
    def per_device(features, w_first, w_label, label_ids, label_count):
        docs, hidden_width = features.shape[0], w_first.shape[1]
        feats, labels = features.shape[1], w_label.shape[1]
        rows = max(1, docs // devices)
        cuts = devices * rows // docs
        width = hidden_width // cuts

        def by_owner(x):
            if cuts == 1:
                return x.reshape(devices, rows, -1)
            return x.reshape(docs // rows, rows, cuts, -1).swapaxes(1, 2).reshape(devices, rows, -1)

        def by_document(x):
            if cuts == 1:
                return x.reshape(docs, -1)
            return x.reshape(docs // rows, cuts, rows, -1).swapaxes(1, 2).reshape(docs, -1)

        def exchange(x):
            return lax.all_to_all(x, AXES, 0, 0)

        def to_all(x):
            return exchange(jnp.broadcast_to(x[None], (devices,) + x.shape))

        shape = jax.ShapeDtypeStruct
        place = lax.axis_index(AXES)
        count_row = label_count[None, :]

        partial_value = jnp.dot(features, w_first, preferred_element_type=F32)
        hidden_sum = jnp.sum(exchange(by_owner(partial_value)), axis=0)
        own_hidden = jnp.tanh(hidden_sum).astype(BF16)
        hidden = by_document(to_all(own_hidden))

        matches, matched, features_turned = kernel(
            match_kernel,
            "match",
            [SMEM] + [VMEM] * 4,
            [
                shape((docs, labels), BF16),
                shape((docs, hidden_width), BF16),
                shape((feats, docs), BF16),
            ],
        )((place * labels)[None], label_ids.T, count_row, w_label, features)

        powers, local_max, packed, hidden_turned = kernel(
            softmax_kernel,
            "softmax",
            [VMEM] * 3,
            [
                shape((docs, labels), F32),
                shape((docs, 1), F32),
                shape((docs, 2 * hidden_width + LANES), BF16),
                shape((hidden_width, docs), BF16),
            ],
        )(hidden, w_label, matched)
        if cuts > 1:
            halves = packed[:, : 2 * hidden_width].reshape(docs, 2, cuts, width)
            tail = jnp.broadcast_to(packed[:, None, 2 * hidden_width :], (docs, cuts, LANES))
            packed = jnp.concatenate([halves[:, 0], halves[:, 1], tail], axis=-1).reshape(docs, -1)
        got = exchange(by_owner(packed))
        if cuts == 1 and rows % 8 == 0:
            back = kernel(
                combine_kernel,
                "combine",
                [SMEM] + [VMEM] * 3,
                shape((devices, rows, width + LANES), BF16),
            )(place[None], got, own_hidden, count_row)
            everyone = by_document(exchange(back))
        else:
            own_count = lax.dynamic_slice_in_dim(label_count, (place // cuts) * rows, rows)
            own = combine(got, own_hidden, own_count[:, None].astype(F32), cuts)
            everyone = to_all(jnp.concatenate(own, axis=-1))
            tails = by_document(everyone[:, :, width:]).reshape(docs, cuts, LANES)
            loss_parts = jnp.sum(from_lanes(tails, 3), axis=1)
            columns = split3(from_lanes(tails, 0)[:, 0]) + split3(loss_parts)
            tail = into_lanes(columns, (docs, LANES))
            everyone = jnp.concatenate([by_document(everyone[:, :, :width]), tail], axis=-1)

        grad_first, grad_label, mean_loss = kernel(
            gradient_kernel,
            "gradient",
            [VMEM] * 7,
            [
                shape((feats, hidden_width), BF16),
                shape((hidden_width, labels), BF16),
                shape((1, 1), F32),
            ],
            out_specs=[VMEM, pl.BlockSpec(memory_space=pl.ANY), VMEM],
            scratch_shapes=[
                pltpu.VMEM((hidden_width, labels), BF16),
                pltpu.SemaphoreType.DMA((len(chunks_of(labels)),)),
            ],
        )(features_turned, hidden_turned, everyone, powers, local_max, matches, count_row)
        return (grad_first, grad_label, mean_loss[0, 0])

    return per_device


def kernel(body, name, in_specs, out_shape, **more):
    several = isinstance(out_shape, list)
    specs = {"out_specs": [VMEM] * len(out_shape) if several else VMEM}
    return pl.pallas_call(
        body,
        name=name,
        in_specs=in_specs,
        out_shape=out_shape,
        compiler_params=pltpu.CompilerParams(vmem_limit_bytes=GRANT),
        **(specs | more),
    )


def solution(mesh):
    placed = (P(None, AXES), P(AXES, None), P(None, AXES), P(), P())
    devices = mesh.shape["gx"] * mesh.shape["gy"]
    return jax.shard_map(
        make_per_device(devices),
        mesh=mesh,
        in_specs=placed,
        out_specs=(P(AXES, None), P(None, AXES), P()),
        check_vma=False,
    )
```

```python
import jax
import jax.numpy as jnp
from jax import lax
from jax.experimental import pallas as pl
from jax.experimental.pallas import tpu as pltpu
from jax.sharding import PartitionSpec as P

AXES = ("gx", "gy")
LANES = 128
GRANT = 12 * 1024 * 1024
VMEM = pl.BlockSpec(memory_space=pltpu.VMEM)
SMEM = pl.BlockSpec(memory_space=pltpu.SMEM)
F32, BF16 = jnp.float32, jnp.bfloat16


def chunks_of(length):
    size = next((s for s in (256, 128) if length % s == 0), length)
    return [slice(at, at + size) for at in range(0, length, size)]


def dot(a, b, dims):
    return lax.dot_general(a, b, (dims, ((), ())), preferred_element_type=F32)


def lane(shape):
    return lax.broadcasted_iota(jnp.int32, shape, len(shape) - 1)


def split3(x):
    high = lax.reduce_precision(x, 8, 7)
    rest = x - high
    middle = lax.reduce_precision(rest, 8, 7)
    return high, middle, rest - middle


def into_lanes(columns, shape):
    at = lane(shape)
    block = jnp.zeros(shape, F32)
    for index, column in enumerate(columns):
        block = jnp.where(at == index, column, block)
    return block.astype(BF16)


def from_lanes(block, first):
    wide = block.astype(F32)
    at = lane(wide.shape)
    return jnp.sum(jnp.where((at >= first) & (at < first + 3), wide, 0.0), axis=-1, keepdims=True)


def match_kernel(
    offset_ref, ids_ref, count_ref, w_label_ref, features_ref, matches_ref, turned_ref
):
    slots, docs = ids_ref.shape
    labels = w_label_ref.shape[1]
    step = 16
    ids = ids_ref[...]
    in_count = lax.broadcasted_iota(jnp.int32, ids.shape, 0) < count_ref[...]
    used = jnp.where(in_count, ids - offset_ref[0], -1).T
    for first_row in range(0, docs, step):
        here = slice(first_row, first_row + step)
        wide = [jnp.broadcast_to(used[here, k : k + 1], (step, LANES)) for k in range(slots)]
        for first in range(0, labels, LANES):
            at = lane((step, LANES)) + first
            hit = jnp.zeros((step, LANES), F32)
            for k in range(slots):
                hit = jnp.where(wide[k] == at, 1.0, hit)
            matches_ref[here, first : first + LANES] = hit.astype(BF16)
    matches_ref[:, labels:] = dot(
        matches_ref[:, :labels], w_label_ref[...], ((1,), (1,))
    ).astype(BF16)
    turned_ref[...] = features_ref[...].T


def softmax_kernel(
    hidden_ref, w_label_ref, matches_ref, powers_ref, max_ref, packed_ref, turned_ref
):
    docs, width = hidden_ref.shape
    pieces = chunks_of(w_label_ref.shape[1])
    hidden = hidden_ref[...]
    top = None
    for piece in pieces:
        logits = dot(hidden, w_label_ref[:, piece], ((1,), (0,)))
        powers_ref[:, piece] = logits
        top = logits if top is None else jnp.maximum(top, logits)
    local_max = jnp.max(top, axis=1, keepdims=True)
    total, expected = None, None
    for piece in pieces:
        powers = jnp.exp(powers_ref[:, piece] - local_max)
        powers_ref[:, piece] = powers
        part = dot(powers.astype(BF16), w_label_ref[:, piece], ((1,), (1,)))
        total = powers if total is None else total + powers
        expected = part if expected is None else expected + part
    local_sum = jnp.sum(total, axis=1, keepdims=True)
    turned_ref[...] = hidden.T
    max_ref[...] = local_max
    packed_ref[:, :width] = (expected / local_sum).astype(BF16)
    packed_ref[:, width : 2 * width] = matches_ref[:, w_label_ref.shape[1] :]
    lse = local_max + jnp.log(local_sum)
    packed_ref[:, 2 * width :] = into_lanes(split3(lse), (docs, LANES))


def combine(got, own_hidden, own_count, cuts):
    width = own_hidden.shape[-1]
    expected = got[:, :, :width].astype(F32)
    matched = jnp.sum(got[:, :, width : 2 * width].astype(F32), axis=0)
    lse_parts = from_lanes(got[:, :, 2 * width :], 0)
    top = jnp.max(lse_parts, axis=0)
    lse = top + jnp.log(jnp.sum(jnp.exp(lse_parts - top), axis=0))
    mean_matched = matched / own_count
    grad_hidden = jnp.sum(jnp.exp(lse_parts - lse) * expected, axis=0) - mean_matched
    hidden = own_hidden.astype(F32)
    grad_inner = (grad_hidden * (1.0 - hidden * hidden)).astype(BF16)
    picked = jnp.sum(hidden * mean_matched, axis=-1, keepdims=True)
    columns = split3(lse) + split3(lse / cuts - picked)
    return grad_inner, into_lanes(columns, (lse.shape[0], LANES))


def combine_kernel(place_ref, got_ref, own_hidden_ref, count_ref, back_ref):
    rows, width = own_hidden_ref.shape
    docs = count_ref.shape[1]
    owner = lax.broadcasted_iota(jnp.int32, (rows, docs), 0) + place_ref[0] * rows
    counts = jnp.where(lane((rows, docs)) == owner, count_ref[...], 0)
    own_count = jnp.sum(counts.astype(F32), axis=1, keepdims=True)
    grad_inner, tail = combine(got_ref[...], own_hidden_ref[...], own_count, 1)
    back_ref[:, :, :width] = jnp.broadcast_to(grad_inner[None], (back_ref.shape[0],) + grad_inner.shape)
    back_ref[:, :, width:] = jnp.broadcast_to(tail[None], (back_ref.shape[0],) + tail.shape)


def gradient_kernel(
    features_ref, hidden_ref, everyone_ref, powers_ref, max_ref, matches_ref, count_ref,
    grad_first_ref, grad_label_hbm, loss_ref, label_scratch, sems,
):
    width, docs = hidden_ref.shape
    tail = everyone_ref[:, width:]
    lse = from_lanes(tail, 0)
    loss_ref[...] = jnp.sum(from_lanes(tail, 3), axis=0, keepdims=True) / docs
    scale = jnp.exp(max_ref[...] - lse)
    per_match = jnp.broadcast_to(1.0 / count_ref[...].astype(F32), (8, docs)).T[:, :1]
    hidden = hidden_ref[...]
    copies = []
    for index, piece in enumerate(chunks_of(powers_ref.shape[1])):
        grad_logits = powers_ref[:, piece] * scale - matches_ref[:, piece].astype(F32) * per_match
        label_scratch[:, piece] = dot(hidden, grad_logits.astype(BF16), ((1,), (0,))).astype(BF16)
        copy = pltpu.make_async_copy(
            label_scratch.at[:, piece], grad_label_hbm.at[:, piece], sems.at[index]
        )
        copy.start()
        copies.append(copy)
    grad_first_ref[...] = dot(features_ref[...], everyone_ref[:, :width], ((1,), (0,))).astype(BF16)
    for copy in copies:
        copy.wait()


def make_per_device(devices):
    def per_device(features, w_first, w_label, label_ids, label_count):
        docs, hidden_width = features.shape[0], w_first.shape[1]
        feats, labels = features.shape[1], w_label.shape[1]
        rows = max(1, docs // devices)
        cuts = devices * rows // docs
        width = hidden_width // cuts

        def by_owner(x):
            if cuts == 1:
                return x.reshape(devices, rows, -1)
            return x.reshape(docs // rows, rows, cuts, -1).swapaxes(1, 2).reshape(devices, rows, -1)

        def by_document(x):
            if cuts == 1:
                return x.reshape(docs, -1)
            return x.reshape(docs // rows, cuts, rows, -1).swapaxes(1, 2).reshape(docs, -1)

        def exchange(x):
            return lax.all_to_all(x, AXES, 0, 0)

        def to_all(x):
            return exchange(jnp.broadcast_to(x[None], (devices,) + x.shape))

        shape = jax.ShapeDtypeStruct
        place = lax.axis_index(AXES)
        count_row = label_count[None, :]

        partial_value = jnp.dot(features, w_first, preferred_element_type=F32)
        matches, features_turned = kernel(
            match_kernel,
            "match",
            [SMEM] + [VMEM] * 4,
            [
                shape((docs, labels + hidden_width), BF16),
                shape((feats, docs), BF16),
            ],
        )((place * labels)[None], label_ids.T, count_row, w_label, features)

        sums = exchange(by_owner(partial_value))
        sums, matches, features_turned = lax.optimization_barrier((sums, matches, features_turned))
        own_hidden = jnp.tanh(jnp.sum(sums, axis=0)).astype(BF16)
        hidden = by_document(to_all(own_hidden))

        powers, local_max, packed, hidden_turned = kernel(
            softmax_kernel,
            "softmax",
            [VMEM] * 3,
            [
                shape((docs, labels), F32),
                shape((docs, 1), F32),
                shape((docs, 2 * hidden_width + LANES), BF16),
                shape((hidden_width, docs), BF16),
            ],
        )(hidden, w_label, matches)
        if cuts > 1:
            halves = packed[:, : 2 * hidden_width].reshape(docs, 2, cuts, width)
            tail = jnp.broadcast_to(packed[:, None, 2 * hidden_width :], (docs, cuts, LANES))
            packed = jnp.concatenate([halves[:, 0], halves[:, 1], tail], axis=-1).reshape(docs, -1)
        got = exchange(by_owner(packed))
        if cuts == 1 and rows % 8 == 0:
            back = kernel(
                combine_kernel,
                "combine",
                [SMEM] + [VMEM] * 3,
                shape((devices, rows, width + LANES), BF16),
            )(place[None], got, own_hidden, count_row)
            everyone = by_document(exchange(back))
        else:
            own_count = lax.dynamic_slice_in_dim(label_count, (place // cuts) * rows, rows)
            own = combine(got, own_hidden, own_count[:, None].astype(F32), cuts)
            everyone = to_all(jnp.concatenate(own, axis=-1))
            tails = by_document(everyone[:, :, width:]).reshape(docs, cuts, LANES)
            loss_parts = jnp.sum(from_lanes(tails, 3), axis=1)
            columns = split3(from_lanes(tails, 0)[:, 0]) + split3(loss_parts)
            tail = into_lanes(columns, (docs, LANES))
            everyone = jnp.concatenate([by_document(everyone[:, :, :width]), tail], axis=-1)

        grad_first, grad_label, mean_loss = kernel(
            gradient_kernel,
            "gradient",
            [VMEM] * 7,
            [
                shape((feats, hidden_width), BF16),
                shape((hidden_width, labels), BF16),
                shape((1, 1), F32),
            ],
            out_specs=[VMEM, pl.BlockSpec(memory_space=pl.ANY), VMEM],
            scratch_shapes=[
                pltpu.VMEM((hidden_width, labels), BF16),
                pltpu.SemaphoreType.DMA((len(chunks_of(labels)),)),
            ],
        )(features_turned, hidden_turned, everyone, powers, local_max, matches, count_row)
        return (grad_first, grad_label, mean_loss[0, 0])

    return per_device


def kernel(body, name, in_specs, out_shape, **more):
    several = isinstance(out_shape, list)
    specs = {"out_specs": [VMEM] * len(out_shape) if several else VMEM}
    return pl.pallas_call(
        body,
        name=name,
        in_specs=in_specs,
        out_shape=out_shape,
        compiler_params=pltpu.CompilerParams(vmem_limit_bytes=GRANT),
        **(specs | more),
    )


def solution(mesh):
    placed = (P(None, AXES), P(AXES, None), P(None, AXES), P(), P())
    devices = mesh.shape["gx"] * mesh.shape["gy"]
    return jax.shard_map(
        make_per_device(devices),
        mesh=mesh,
        in_specs=placed,
        out_specs=(P(AXES, None), P(None, AXES), P()),
        check_vma=False,
    )
```

```python
import jax
import jax.numpy as jnp
from jax import lax
from jax.experimental import pallas as pl
from jax.experimental.pallas import tpu as pltpu
from jax.sharding import PartitionSpec as P

AXES = ("gx", "gy")
LANES = 128
WORD = 32
GRANT = 12 * 1024 * 1024
FIRST_GRANT = 56 * 1024 * 1024
VMEM = pl.BlockSpec(memory_space=pltpu.VMEM)
HBM = pl.BlockSpec(memory_space=pltpu.HBM)
SMEM = pl.BlockSpec(memory_space=pltpu.SMEM)
F32, BF16 = jnp.float32, jnp.bfloat16


def chunks_of(length):
    size = next((s for s in (256, 128) if length % s == 0), length)
    return [slice(at, at + size) for at in range(0, length, size)]


def dot(a, b, dims):
    return lax.dot_general(a, b, (dims, ((), ())), preferred_element_type=F32)


def lane(shape):
    return lax.broadcasted_iota(jnp.int32, shape, len(shape) - 1)


def split3(x):
    high = lax.reduce_precision(x, 8, 7)
    rest = x - high
    middle = lax.reduce_precision(rest, 8, 7)
    return high, middle, rest - middle


def into_lanes(columns, shape):
    at = lane(shape)
    block = jnp.zeros(shape, F32)
    for index, column in enumerate(columns):
        block = jnp.where(at == index, column, block)
    return block.astype(BF16)


def from_lanes(block, first):
    wide = block.astype(F32)
    at = lane(wide.shape)
    return jnp.sum(jnp.where((at >= first) & (at < first + 3), wide, 0.0), axis=-1, keepdims=True)


def match_blocks(ids, counts, offset):
    slots, docs = ids.shape
    in_count = lax.broadcasted_iota(jnp.int32, ids.shape, 0) < counts
    used = jnp.where(in_count, ids - offset, -1).T
    at = lane((docs, LANES))
    blocks = []
    for slot in range(slots):
        here = jnp.broadcast_to(used[:, slot : slot + 1], (docs, LANES))
        blocks.append(jnp.where((here & (LANES - 1)) == at, here >> 7, -1))
    return blocks


def match_words(ids_ref, count_ref, offset_ref, words_ref):
    blocks = match_blocks(ids_ref[...], count_ref[...], offset_ref[0])
    for index in range(words_ref.shape[1] // LANES):
        word = jnp.zeros((words_ref.shape[0], LANES), jnp.int32)
        for block in blocks:
            bit = block - WORD * index
            word = word | jnp.where((bit >= 0) & (bit < WORD), 1 << jnp.clip(bit, 0, WORD - 1), 0)
        words_ref[:, LANES * index : LANES * (index + 1)] = word


def first_kernel(features_hbm, w_first_hbm, partial_ref, features_ref, w_first_ref, sems):
    feats = features_hbm.shape[1]
    moves = []
    for index, piece in enumerate(chunks_of(feats)):
        for source, target in (
            (features_hbm.at[:, piece], features_ref.at[:, piece]),
            (w_first_hbm.at[piece], w_first_ref.at[piece]),
        ):
            moves.append(pltpu.make_async_copy(source, target, sems.at[len(moves)]))
            moves[-1].start()
    total = None
    for index, piece in enumerate(chunks_of(feats)):
        moves[2 * index].wait()
        moves[2 * index + 1].wait()
        part = dot(features_ref[:, piece], w_first_ref[piece], ((1,), (0,)))
        total = part if total is None else total + part
    partial_ref[...] = total


def hits(words_ref, piece, yes, no):
    blocks = []
    for first in range(piece.start, piece.stop, LANES):
        word_index, bit = divmod(first // LANES, WORD)
        word = words_ref[:, LANES * word_index : LANES * (word_index + 1)]
        blocks.append(jnp.where((word & (1 << bit)) != 0, yes, no))
    return jnp.concatenate(blocks, axis=1)


def softmax_kernel(
    offset_ref, ids_ref, count_ref, hidden_ref, w_label_ref,
    powers_ref, max_ref, packed_ref, turned_ref, words_ref,
):
    docs, width = hidden_ref.shape
    pieces = chunks_of(w_label_ref.shape[1])
    hidden = hidden_ref[...]
    turned_ref[...] = hidden.T
    match_words(ids_ref, count_ref, offset_ref, words_ref)
    top = None
    for piece in pieces:
        logits = dot(hidden, w_label_ref[:, piece], ((1,), (0,)))
        powers_ref[:, piece] = logits
        top = logits if top is None else jnp.maximum(top, logits)
    local_max = jnp.max(top, axis=1, keepdims=True)
    total, sums = None, None
    for piece in pieces:
        powers = jnp.exp(powers_ref[:, piece] - local_max)
        powers_ref[:, piece] = powers
        both = [powers.astype(BF16), hits(words_ref, piece, 1.0, 0.0).astype(BF16)]
        part = dot(jnp.concatenate(both, axis=0), w_label_ref[:, piece], ((1,), (1,)))
        total = powers if total is None else total + powers
        sums = part if sums is None else sums + part
    local_sum = jnp.sum(total, axis=1, keepdims=True)
    max_ref[...] = local_max
    packed_ref[:, :width] = (sums[:docs] / local_sum).astype(BF16)
    packed_ref[:, width : 2 * width] = sums[docs:].astype(BF16)
    lse = local_max + jnp.log(local_sum)
    packed_ref[:, 2 * width :] = into_lanes(split3(lse), (docs, LANES))


def combine(got, own_hidden, own_count, cuts):
    width = own_hidden.shape[-1]
    expected = got[:, :, :width].astype(F32)
    matched = jnp.sum(got[:, :, width : 2 * width].astype(F32), axis=0)
    lse_parts = from_lanes(got[:, :, 2 * width :], 0)
    top = jnp.max(lse_parts, axis=0)
    lse = top + jnp.log(jnp.sum(jnp.exp(lse_parts - top), axis=0))
    mean_matched = matched / own_count
    grad_hidden = jnp.sum(jnp.exp(lse_parts - lse) * expected, axis=0) - mean_matched
    hidden = own_hidden.astype(F32)
    grad_inner = (grad_hidden * (1.0 - hidden * hidden)).astype(BF16)
    picked = jnp.sum(hidden * mean_matched, axis=-1, keepdims=True)
    columns = split3(lse) + split3(lse / cuts - picked)
    return grad_inner, into_lanes(columns, (lse.shape[0], LANES))


def combine_kernel(place_ref, got_ref, own_hidden_ref, count_ref, back_ref):
    rows, width = own_hidden_ref.shape
    docs = count_ref.shape[1]
    owner = lax.broadcasted_iota(jnp.int32, (rows, docs), 0) + place_ref[0] * rows
    counts = jnp.where(lane((rows, docs)) == owner, count_ref[...], 0)
    own_count = jnp.sum(counts.astype(F32), axis=1, keepdims=True)
    grad_inner, tail = combine(got_ref[...], own_hidden_ref[...], own_count, 1)
    back_ref[:, :, :width] = jnp.broadcast_to(grad_inner[None], (back_ref.shape[0],) + grad_inner.shape)
    back_ref[:, :, width:] = jnp.broadcast_to(tail[None], (back_ref.shape[0],) + tail.shape)


def gradient_kernel(
    features_ref, hidden_ref, everyone_ref, powers_ref, max_ref, words_ref, count_ref,
    grad_first_ref, grad_label_hbm, loss_ref, label_scratch, sems,
):
    width, docs = hidden_ref.shape
    tail = everyone_ref[:, width:]
    lse = from_lanes(tail, 0)
    loss_ref[...] = jnp.sum(from_lanes(tail, 3), axis=0, keepdims=True) / docs
    scale = jnp.exp(max_ref[...] - lse)
    per_match = jnp.broadcast_to(1.0 / count_ref[...].astype(F32), (8, docs)).T[:, :1]
    hidden = hidden_ref[...]
    copies = []
    for index, piece in enumerate(chunks_of(powers_ref.shape[1])):
        grad_logits = powers_ref[:, piece] * scale - hits(words_ref, piece, per_match, 0.0)
        label_scratch[:, piece] = dot(hidden, grad_logits.astype(BF16), ((1,), (0,))).astype(BF16)
        copy = pltpu.make_async_copy(
            label_scratch.at[:, piece], grad_label_hbm.at[:, piece], sems.at[index]
        )
        copy.start()
        copies.append(copy)
    grad_first_ref[...] = dot(
        features_ref[...].T, everyone_ref[:, :width], ((1,), (0,))
    ).astype(BF16)
    for copy in copies:
        copy.wait()


def make_per_device(devices):
    def per_device(features, w_first, w_label, label_ids, label_count):
        docs, hidden_width = features.shape[0], w_first.shape[1]
        feats, labels = features.shape[1], w_label.shape[1]
        rows = max(1, docs // devices)
        cuts = devices * rows // docs
        width = hidden_width // cuts

        def by_owner(x):
            if cuts == 1:
                return x.reshape(devices, rows, -1)
            return x.reshape(docs // rows, rows, cuts, -1).swapaxes(1, 2).reshape(devices, rows, -1)

        def by_document(x):
            if cuts == 1:
                return x.reshape(docs, -1)
            return x.reshape(docs // rows, cuts, rows, -1).swapaxes(1, 2).reshape(docs, -1)

        def exchange(x):
            return lax.all_to_all(x, AXES, 0, 0)

        def to_all(x):
            return exchange(jnp.broadcast_to(x[None], (devices,) + x.shape))

        shape = jax.ShapeDtypeStruct
        place = lax.axis_index(AXES)
        count_row = label_count[None, :]

        partial_value = kernel(
            first_kernel,
            "first",
            [HBM] * 2,
            shape((docs, hidden_width), F32),
            grant=FIRST_GRANT,
            scratch_shapes=[
                pltpu.VMEM((docs, feats), BF16),
                pltpu.VMEM((feats, hidden_width), BF16),
                pltpu.SemaphoreType.DMA((2 * len(chunks_of(feats)),)),
            ],
        )(features, w_first)
        sums = exchange(by_owner(partial_value))
        own_hidden = jnp.tanh(jnp.sum(sums, axis=0)).astype(BF16)
        hidden = by_document(to_all(own_hidden))

        word_lanes = LANES * pl.cdiv(labels, LANES * WORD)
        powers, local_max, packed, hidden_turned, words = kernel(
            softmax_kernel,
            "softmax",
            [SMEM] + [VMEM] * 4,
            [
                shape((docs, labels), F32),
                shape((docs, 1), F32),
                shape((docs, 2 * hidden_width + LANES), BF16),
                shape((hidden_width, docs), BF16),
                shape((docs, word_lanes), jnp.int32),
            ],
        )((place * labels)[None], label_ids.T, count_row, hidden, w_label)
        if cuts > 1:
            halves = packed[:, : 2 * hidden_width].reshape(docs, 2, cuts, width)
            tail = jnp.broadcast_to(packed[:, None, 2 * hidden_width :], (docs, cuts, LANES))
            packed = jnp.concatenate([halves[:, 0], halves[:, 1], tail], axis=-1).reshape(docs, -1)
        got = exchange(by_owner(packed))
        if cuts == 1 and rows % 8 == 0:
            back = kernel(
                combine_kernel,
                "combine",
                [SMEM] + [VMEM] * 3,
                shape((devices, rows, width + LANES), BF16),
            )(place[None], got, own_hidden, count_row)
            everyone = by_document(exchange(back))
        else:
            own_count = lax.dynamic_slice_in_dim(label_count, (place // cuts) * rows, rows)
            own = combine(got, own_hidden, own_count[:, None].astype(F32), cuts)
            everyone = to_all(jnp.concatenate(own, axis=-1))
            tails = by_document(everyone[:, :, width:]).reshape(docs, cuts, LANES)
            loss_parts = jnp.sum(from_lanes(tails, 3), axis=1)
            columns = split3(from_lanes(tails, 0)[:, 0]) + split3(loss_parts)
            tail = into_lanes(columns, (docs, LANES))
            everyone = jnp.concatenate([by_document(everyone[:, :, :width]), tail], axis=-1)

        grad_first, grad_label, mean_loss = kernel(
            gradient_kernel,
            "gradient",
            [VMEM] * 7,
            [
                shape((feats, hidden_width), BF16),
                shape((hidden_width, labels), BF16),
                shape((1, 1), F32),
            ],
            out_specs=[VMEM, HBM, VMEM],
            scratch_shapes=[
                pltpu.VMEM((hidden_width, labels), BF16),
                pltpu.SemaphoreType.DMA((len(chunks_of(labels)),)),
            ],
        )(features, hidden_turned, everyone, powers, local_max, words, count_row)
        return (grad_first, grad_label, mean_loss[0, 0])

    return per_device


def kernel(body, name, in_specs, out_shape, grant=GRANT, **more):
    several = isinstance(out_shape, list)
    specs = {"out_specs": [VMEM] * len(out_shape) if several else VMEM}
    return pl.pallas_call(
        body,
        name=name,
        in_specs=in_specs,
        out_shape=out_shape,
        compiler_params=pltpu.CompilerParams(vmem_limit_bytes=grant),
        **(specs | more),
    )


def solution(mesh):
    placed = (P(None, AXES), P(AXES, None), P(None, AXES), P(), P())
    devices = mesh.shape["gx"] * mesh.shape["gy"]
    return jax.shard_map(
        make_per_device(devices),
        mesh=mesh,
        in_specs=placed,
        out_specs=(P(AXES, None), P(None, AXES), P()),
        check_vma=False,
    )
```

```python
import jax
import jax.numpy as jnp
from jax import lax
from jax.experimental import pallas as pl
from jax.experimental.pallas import tpu as pltpu
from jax.sharding import PartitionSpec as P

AXES = ("gx", "gy")
LANES = 128
WORD = 32
GRANT = 12 * 1024 * 1024
FIRST_GRANT = 56164352
VMEM = pl.BlockSpec(memory_space=pltpu.VMEM)
HBM = pl.BlockSpec(memory_space=pltpu.HBM)
SMEM = pl.BlockSpec(memory_space=pltpu.SMEM)
F32, BF16 = jnp.float32, jnp.bfloat16


def chunks_of(length):
    size = next((s for s in (256, 128) if length % s == 0), length)
    return [slice(at, at + size) for at in range(0, length, size)]


def dot(a, b, dims):
    return lax.dot_general(a, b, (dims, ((), ())), preferred_element_type=F32)


def lane(shape):
    return lax.broadcasted_iota(jnp.int32, shape, len(shape) - 1)


def split3(x):
    high = lax.reduce_precision(x, 8, 7)
    rest = x - high
    middle = lax.reduce_precision(rest, 8, 7)
    return high, middle, rest - middle


def into_lanes(columns, shape):
    at = lane(shape)
    block = jnp.zeros(shape, F32)
    for index, column in enumerate(columns):
        block = jnp.where(at == index, column, block)
    return block.astype(BF16)


def from_lanes(block, first):
    wide = block.astype(F32)
    at = lane(wide.shape)
    return jnp.sum(jnp.where((at >= first) & (at < first + 3), wide, 0.0), axis=-1, keepdims=True)


def match_blocks(ids, counts, offset):
    slots, docs = ids.shape
    in_count = lax.broadcasted_iota(jnp.int32, ids.shape, 0) < counts
    used = jnp.where(in_count, ids - offset, -1).T
    at = lane((docs, LANES))
    blocks = []
    for slot in range(slots):
        here = jnp.broadcast_to(used[:, slot : slot + 1], (docs, LANES))
        blocks.append(jnp.where((here & (LANES - 1)) == at, here >> 7, -1))
    return blocks


def match_words(ids_ref, count_ref, offset_ref, words_ref):
    blocks = match_blocks(ids_ref[...], count_ref[...], offset_ref[0])
    for index in range(words_ref.shape[1] // LANES):
        word = jnp.zeros((words_ref.shape[0], LANES), jnp.int32)
        for block in blocks:
            bit = block - WORD * index
            word = word | jnp.where((bit >= 0) & (bit < WORD), 1 << jnp.clip(bit, 0, WORD - 1), 0)
        words_ref[:, LANES * index : LANES * (index + 1)] = word


def first_kernel(features_hbm, w_first_hbm, partial_ref, features_ref, w_first_ref, sems):
    feats = features_hbm.shape[1]
    moves = []
    for index, piece in enumerate(chunks_of(feats)):
        for source, target in (
            (features_hbm.at[:, piece], features_ref.at[:, piece]),
            (w_first_hbm.at[piece], w_first_ref.at[piece]),
        ):
            moves.append(pltpu.make_async_copy(source, target, sems.at[len(moves)]))
            moves[-1].start()
    total = None
    for index, piece in enumerate(chunks_of(feats)):
        moves[2 * index].wait()
        moves[2 * index + 1].wait()
        part = dot(features_ref[:, piece], w_first_ref[piece], ((1,), (0,)))
        total = part if total is None else total + part
    partial_ref[...] = total


def hits(words_ref, piece, yes, no):
    blocks = []
    for first in range(piece.start, piece.stop, LANES):
        word_index, bit = divmod(first // LANES, WORD)
        word = words_ref[:, LANES * word_index : LANES * (word_index + 1)]
        blocks.append(jnp.where((word & (1 << bit)) != 0, yes, no))
    return jnp.concatenate(blocks, axis=1)


def softmax_kernel(
    offset_ref, ids_ref, count_ref, hidden_ref, w_label_ref,
    powers_ref, max_ref, packed_ref, turned_ref, words_ref,
):
    docs, width = hidden_ref.shape
    pieces = chunks_of(w_label_ref.shape[1])
    hidden = hidden_ref[...]
    turned_ref[...] = hidden.T
    match_words(ids_ref, count_ref, offset_ref, words_ref)
    top = None
    for piece in pieces:
        logits = dot(hidden, w_label_ref[:, piece], ((1,), (0,)))
        powers_ref[:, piece] = logits
        top = logits if top is None else jnp.maximum(top, logits)
    local_max = jnp.max(top, axis=1, keepdims=True)
    total, sums = None, None
    for piece in pieces:
        powers = jnp.exp(powers_ref[:, piece] - local_max)
        powers_ref[:, piece] = powers
        both = [powers.astype(BF16), hits(words_ref, piece, 1.0, 0.0).astype(BF16)]
        part = dot(jnp.concatenate(both, axis=0), w_label_ref[:, piece], ((1,), (1,)))
        total = powers if total is None else total + powers
        sums = part if sums is None else sums + part
    local_sum = jnp.sum(total, axis=1, keepdims=True)
    max_ref[...] = local_max
    packed_ref[:, :width] = (sums[:docs] / local_sum).astype(BF16)
    packed_ref[:, width : 2 * width] = sums[docs:].astype(BF16)
    lse = local_max + jnp.log(local_sum)
    packed_ref[:, 2 * width :] = into_lanes(split3(lse), (docs, LANES))


def combine(got, own_hidden, own_count, cuts):
    width = own_hidden.shape[-1]
    expected = got[:, :, :width].astype(F32)
    matched = jnp.sum(got[:, :, width : 2 * width].astype(F32), axis=0)
    lse_parts = from_lanes(got[:, :, 2 * width :], 0)
    top = jnp.max(lse_parts, axis=0)
    lse = top + jnp.log(jnp.sum(jnp.exp(lse_parts - top), axis=0))
    mean_matched = matched / own_count
    grad_hidden = jnp.sum(jnp.exp(lse_parts - lse) * expected, axis=0) - mean_matched
    hidden = own_hidden.astype(F32)
    grad_inner = (grad_hidden * (1.0 - hidden * hidden)).astype(BF16)
    picked = jnp.sum(hidden * mean_matched, axis=-1, keepdims=True)
    columns = split3(lse) + split3(lse / cuts - picked)
    return grad_inner, into_lanes(columns, (lse.shape[0], LANES))


def combine_kernel(place_ref, got_ref, own_hidden_ref, count_ref, back_ref):
    rows, width = own_hidden_ref.shape
    docs = count_ref.shape[1]
    owner = lax.broadcasted_iota(jnp.int32, (rows, docs), 0) + place_ref[0] * rows
    counts = jnp.where(lane((rows, docs)) == owner, count_ref[...], 0)
    own_count = jnp.sum(counts.astype(F32), axis=1, keepdims=True)
    grad_inner, tail = combine(got_ref[...], own_hidden_ref[...], own_count, 1)
    back_ref[:, :, :width] = jnp.broadcast_to(grad_inner[None], (back_ref.shape[0],) + grad_inner.shape)
    back_ref[:, :, width:] = jnp.broadcast_to(tail[None], (back_ref.shape[0],) + tail.shape)


def gradient_kernel(
    features_ref, hidden_ref, everyone_ref, powers_ref, max_ref, words_ref, count_ref,
    grad_first_ref, grad_label_hbm, loss_ref, label_scratch, sems,
):
    width, docs = hidden_ref.shape
    tail = everyone_ref[:, width:]
    lse = from_lanes(tail, 0)
    loss_ref[...] = jnp.sum(from_lanes(tail, 3), axis=0, keepdims=True) / docs
    scale = jnp.exp(max_ref[...] - lse)
    per_match = jnp.broadcast_to(1.0 / count_ref[...].astype(F32), (8, docs)).T[:, :1]
    hidden = hidden_ref[...]
    copies = []
    for index, piece in enumerate(chunks_of(powers_ref.shape[1])):
        grad_logits = powers_ref[:, piece] * scale - hits(words_ref, piece, per_match, 0.0)
        label_scratch[:, piece] = dot(hidden, grad_logits.astype(BF16), ((1,), (0,))).astype(BF16)
        copy = pltpu.make_async_copy(
            label_scratch.at[:, piece], grad_label_hbm.at[:, piece], sems.at[index]
        )
        copy.start()
        copies.append(copy)
    grad_first_ref[...] = dot(
        features_ref[...].T, everyone_ref[:, :width], ((1,), (0,))
    ).astype(BF16)
    for copy in copies:
        copy.wait()


def make_per_device(devices):
    def per_device(features, w_first, w_label, label_ids, label_count):
        docs, hidden_width = features.shape[0], w_first.shape[1]
        feats, labels = features.shape[1], w_label.shape[1]
        rows = max(1, docs // devices)
        cuts = devices * rows // docs
        width = hidden_width // cuts

        def by_owner(x):
            if cuts == 1:
                return x.reshape(devices, rows, -1)
            return x.reshape(docs // rows, rows, cuts, -1).swapaxes(1, 2).reshape(devices, rows, -1)

        def by_document(x):
            if cuts == 1:
                return x.reshape(docs, -1)
            return x.reshape(docs // rows, cuts, rows, -1).swapaxes(1, 2).reshape(docs, -1)

        def exchange(x):
            return lax.all_to_all(x, AXES, 0, 0)

        def to_all(x):
            return exchange(jnp.broadcast_to(x[None], (devices,) + x.shape))

        shape = jax.ShapeDtypeStruct
        place = lax.axis_index(AXES)
        count_row = label_count[None, :]

        partial_value = kernel(
            first_kernel,
            "first",
            [HBM] * 2,
            shape((docs, hidden_width), F32),
            grant=FIRST_GRANT,
            scratch_shapes=[
                pltpu.VMEM((docs, feats), BF16),
                pltpu.VMEM((feats, hidden_width), BF16),
                pltpu.SemaphoreType.DMA((2 * len(chunks_of(feats)),)),
            ],
        )(features, w_first)
        offset = (place * labels)[None]
        partial_value, offset = lax.optimization_barrier((partial_value, offset))
        sums = exchange(by_owner(partial_value))
        own_hidden = jnp.tanh(jnp.sum(sums, axis=0)).astype(BF16)
        hidden = by_document(to_all(own_hidden))

        word_lanes = LANES * pl.cdiv(labels, LANES * WORD)
        powers, local_max, packed, hidden_turned, words = kernel(
            softmax_kernel,
            "softmax",
            [SMEM] + [VMEM] * 4,
            [
                shape((docs, labels), F32),
                shape((docs, 1), F32),
                shape((docs, 2 * hidden_width + LANES), BF16),
                shape((hidden_width, docs), BF16),
                shape((docs, word_lanes), jnp.int32),
            ],
        )(offset, label_ids.T, count_row, hidden, w_label)
        if cuts > 1:
            halves = packed[:, : 2 * hidden_width].reshape(docs, 2, cuts, width)
            tail = jnp.broadcast_to(packed[:, None, 2 * hidden_width :], (docs, cuts, LANES))
            packed = jnp.concatenate([halves[:, 0], halves[:, 1], tail], axis=-1).reshape(docs, -1)
        got = exchange(by_owner(packed))
        if cuts == 1 and rows % 8 == 0:
            back = kernel(
                combine_kernel,
                "combine",
                [SMEM] + [VMEM] * 3,
                shape((devices, rows, width + LANES), BF16),
            )(place[None], got, own_hidden, count_row)
            everyone = by_document(exchange(back))
        else:
            own_count = lax.dynamic_slice_in_dim(label_count, (place // cuts) * rows, rows)
            own = combine(got, own_hidden, own_count[:, None].astype(F32), cuts)
            everyone = to_all(jnp.concatenate(own, axis=-1))
            tails = by_document(everyone[:, :, width:]).reshape(docs, cuts, LANES)
            loss_parts = jnp.sum(from_lanes(tails, 3), axis=1)
            columns = split3(from_lanes(tails, 0)[:, 0]) + split3(loss_parts)
            tail = into_lanes(columns, (docs, LANES))
            everyone = jnp.concatenate([by_document(everyone[:, :, :width]), tail], axis=-1)

        grad_first, grad_label, mean_loss = kernel(
            gradient_kernel,
            "gradient",
            [VMEM] * 7,
            [
                shape((feats, hidden_width), BF16),
                shape((hidden_width, labels), BF16),
                shape((1, 1), F32),
            ],
            out_specs=[VMEM, HBM, VMEM],
            scratch_shapes=[
                pltpu.VMEM((hidden_width, labels), BF16),
                pltpu.SemaphoreType.DMA((len(chunks_of(labels)),)),
            ],
        )(features, hidden_turned, everyone, powers, local_max, words, count_row)
        return (grad_first, grad_label, mean_loss[0, 0])

    return per_device


def kernel(body, name, in_specs, out_shape, grant=GRANT, **more):
    several = isinstance(out_shape, list)
    specs = {"out_specs": [VMEM] * len(out_shape) if several else VMEM}
    return pl.pallas_call(
        body,
        name=name,
        in_specs=in_specs,
        out_shape=out_shape,
        compiler_params=pltpu.CompilerParams(vmem_limit_bytes=grant),
        **(specs | more),
    )


def solution(mesh):
    placed = (P(None, AXES), P(AXES, None), P(None, AXES), P(), P())
    devices = mesh.shape["gx"] * mesh.shape["gy"]
    return jax.shard_map(
        make_per_device(devices),
        mesh=mesh,
        in_specs=placed,
        out_specs=(P(AXES, None), P(None, AXES), P()),
        check_vma=False,
    )
```

```python
import jax
import jax.numpy as jnp
from jax import lax
from jax.experimental import pallas as pl
from jax.experimental.pallas import tpu as pltpu
from jax.sharding import PartitionSpec as P

AXES = ("gx", "gy")
LANES = 128
WORD = 32
GRANT = 12 * 1024 * 1024
FIRST_GRANT = 56164352
VMEM = pl.BlockSpec(memory_space=pltpu.VMEM)
HBM = pl.BlockSpec(memory_space=pltpu.HBM)
SMEM = pl.BlockSpec(memory_space=pltpu.SMEM)
F32, BF16 = jnp.float32, jnp.bfloat16


def chunks_of(length):
    size = next((s for s in (256, 128) if length % s == 0), length)
    return [slice(at, at + size) for at in range(0, length, size)]


def dot(a, b, dims):
    return lax.dot_general(a, b, (dims, ((), ())), preferred_element_type=F32)


def lane(shape):
    return lax.broadcasted_iota(jnp.int32, shape, len(shape) - 1)


def split3(x):
    high = lax.reduce_precision(x, 8, 7)
    rest = x - high
    middle = lax.reduce_precision(rest, 8, 7)
    return high, middle, rest - middle


def into_lanes(columns, shape):
    at = lane(shape)
    block = jnp.zeros(shape, F32)
    for index, column in enumerate(columns):
        block = jnp.where(at == index, column, block)
    return block


def column_of(row):
    return jnp.broadcast_to(row, (8, row.shape[1])).T[:, :1]


def row_of(column):
    return jnp.broadcast_to(column, (column.shape[0], 8)).T[:1]


def stats_rows(docs):
    return pl.cdiv(3 * docs // LANES + 1, 8) * 8


def stats_block(lse, scalar):
    docs = lse.shape[1]
    rows = [part[:, at : at + LANES] for part in split3(lse) for at in range(0, docs, LANES)]
    rows.append(into_lanes(split3(scalar), (1, LANES)))
    rows += [jnp.zeros((1, LANES), F32)] * (stats_rows(docs) - len(rows))
    return jnp.concatenate(rows, axis=0)


def match_blocks(ids, counts, offset):
    slots, docs = ids.shape
    in_count = lax.broadcasted_iota(jnp.int32, ids.shape, 0) < counts
    used = jnp.where(in_count, ids - offset, -1).T
    at = lane((docs, LANES))
    blocks = []
    for slot in range(slots):
        here = jnp.broadcast_to(used[:, slot : slot + 1], (docs, LANES))
        blocks.append(jnp.where((here & (LANES - 1)) == at, here >> 7, -1))
    return blocks


def match_words(ids_ref, count_ref, offset_ref, words_ref):
    blocks = match_blocks(ids_ref[...], count_ref[...], offset_ref[0])
    for index in range(words_ref.shape[1] // LANES):
        word = jnp.zeros((words_ref.shape[0], LANES), jnp.int32)
        for block in blocks:
            bit = block - WORD * index
            word = word | jnp.where((bit >= 0) & (bit < WORD), 1 << jnp.clip(bit, 0, WORD - 1), 0)
        words_ref[:, LANES * index : LANES * (index + 1)] = word


def first_kernel(features_hbm, w_first_hbm, partial_ref, features_ref, w_first_ref, sems):
    feats = features_hbm.shape[1]
    moves = []
    for index, piece in enumerate(chunks_of(feats)):
        for source, target in (
            (features_hbm.at[:, piece], features_ref.at[:, piece]),
            (w_first_hbm.at[piece], w_first_ref.at[piece]),
        ):
            moves.append(pltpu.make_async_copy(source, target, sems.at[len(moves)]))
            moves[-1].start()
    total = None
    for index, piece in enumerate(chunks_of(feats)):
        moves[2 * index].wait()
        moves[2 * index + 1].wait()
        part = dot(features_ref[:, piece], w_first_ref[piece], ((1,), (0,)))
        total = part if total is None else total + part
    partial_ref[...] = total


def hits(words_ref, piece, yes, no):
    blocks = []
    for first in range(piece.start, piece.stop, LANES):
        word_index, bit = divmod(first // LANES, WORD)
        word = words_ref[:, LANES * word_index : LANES * (word_index + 1)]
        blocks.append(jnp.where((word & (1 << bit)) != 0, yes, no))
    return jnp.concatenate(blocks, axis=1)


def softmax_kernel(
    offset_ref, ids_ref, count_ref, hidden_ref, w_label_ref,
    powers_ref, max_ref, packed_ref, turned_ref, words_ref,
):
    docs, width = hidden_ref.shape
    pieces = chunks_of(w_label_ref.shape[1])
    hidden = hidden_ref[...]
    turned_ref[...] = hidden.T
    match_words(ids_ref, count_ref, offset_ref, words_ref)
    top = None
    for piece in pieces:
        logits = dot(hidden, w_label_ref[:, piece], ((1,), (0,)))
        powers_ref[:, piece] = logits
        top = logits if top is None else jnp.maximum(top, logits)
    local_max = jnp.max(top, axis=1, keepdims=True)
    total, sums = None, None
    for piece in pieces:
        powers = jnp.exp(powers_ref[:, piece] - local_max)
        powers_ref[:, piece] = powers
        both = [powers.astype(BF16), hits(words_ref, piece, 1.0, 0.0).astype(BF16)]
        part = dot(jnp.concatenate(both, axis=0), w_label_ref[:, piece], ((1,), (1,)))
        total = powers if total is None else total + powers
        sums = part if sums is None else sums + part
    local_sum = jnp.sum(total, axis=1, keepdims=True)
    max_ref[...] = local_max
    matched = sums[docs:]
    packed_ref[:, :width] = (sums[:docs] / local_sum).astype(BF16)
    packed_ref[:, width : 2 * width] = matched.astype(BF16)
    picked = jnp.sum(hidden.astype(F32) * matched, axis=1, keepdims=True)
    picked = jnp.sum(picked / column_of(count_ref[...].astype(F32)), axis=0, keepdims=True)
    stats = stats_block(row_of(local_max + jnp.log(local_sum)), picked).astype(BF16)
    for first in range(0, docs, stats.shape[0]):
        packed_ref[first : first + stats.shape[0], 2 * width :] = stats


def combine(expected, matched, stats, own_hidden, own_count, first_row, docs):
    rows = own_hidden.shape[0]
    part = docs // LANES
    stats = stats.astype(F32)
    lse_parts = stats[:, :part] + stats[:, part : 2 * part] + stats[:, 2 * part : 3 * part]
    top = jnp.max(lse_parts, axis=0)
    lse = top + jnp.log(jnp.sum(jnp.exp(lse_parts - top), axis=0))
    picked = jnp.sum(stats[:, 3 * part : 3 * part + 1], axis=0)
    loss = jnp.sum(jnp.sum(lse, axis=0, keepdims=True) - picked, axis=1, keepdims=True) / docs
    shares = jnp.exp(lse_parts - lse)
    own = lane((rows, LANES)) - lax.broadcasted_iota(jnp.int32, (rows, LANES), 0) - first_row
    share = 0.0
    for index in range(part):
        share = share + jnp.where(own + LANES * index == 0, shares[:, index : index + 1], 0.0)
    share = jnp.sum(share, axis=-1, keepdims=True)
    mean_matched = jnp.sum(matched.astype(F32), axis=0) / own_count
    grad_hidden = jnp.sum(share * expected.astype(F32), axis=0) - mean_matched
    hidden = own_hidden.astype(F32)
    grad_inner = (grad_hidden * (1.0 - hidden * hidden)).astype(BF16)
    return grad_inner, lse, loss


def combine_kernel(place_ref, got_ref, own_hidden_ref, count_ref, back_ref, lse_ref, loss_ref):
    rows, width = own_hidden_ref.shape
    docs = count_ref.shape[1]
    first_row = place_ref[0] * rows
    owner = lax.broadcasted_iota(jnp.int32, (rows, docs), 0) + first_row
    counts = jnp.where(lane((rows, docs)) == owner, count_ref[...], 0)
    own_count = jnp.sum(counts.astype(F32), axis=1, keepdims=True)
    grad_inner, lse_ref[...], loss_ref[...] = combine(
        got_ref[:, :, :width], got_ref[:, :, width : 2 * width], got_ref[:, :, 2 * width :],
        own_hidden_ref[...], own_count, first_row, docs,
    )
    back_ref[...] = jnp.broadcast_to(grad_inner[None], back_ref.shape)


def gradient_kernel(
    features_ref, hidden_ref, grad_inner_ref, lse_ref, powers_ref, max_ref, words_ref, count_ref,
    grad_first_hbm, grad_label_hbm, first_scratch, label_scratch, sems,
):
    first_scratch[...] = dot(
        features_ref[...].T, grad_inner_ref[...], ((1,), (0,))
    ).astype(BF16)
    copies = [pltpu.make_async_copy(first_scratch, grad_first_hbm, sems.at[0])]
    copies[0].start()
    lse_row = jnp.concatenate([lse_ref[i : i + 1] for i in range(lse_ref.shape[0])], axis=1)
    scale = jnp.exp(max_ref[...] - column_of(lse_row))
    per_match = column_of(1.0 / count_ref[...].astype(F32))
    hidden = hidden_ref[...]
    for piece in chunks_of(powers_ref.shape[1]):
        grad_logits = powers_ref[:, piece] * scale - hits(words_ref, piece, per_match, 0.0)
        label_scratch[:, piece] = dot(hidden, grad_logits.astype(BF16), ((1,), (0,))).astype(BF16)
        copy = pltpu.make_async_copy(
            label_scratch.at[:, piece], grad_label_hbm.at[:, piece], sems.at[len(copies)]
        )
        copy.start()
        copies.append(copy)
    for copy in copies:
        copy.wait()


def make_per_device(devices):
    def per_device(features, w_first, w_label, label_ids, label_count):
        docs, hidden_width = features.shape[0], w_first.shape[1]
        feats, labels = features.shape[1], w_label.shape[1]
        rows = max(1, docs // devices)
        cuts = devices * rows // docs
        width = hidden_width // cuts

        def by_owner(x):
            if cuts == 1:
                return x.reshape(devices, rows, -1)
            return x.reshape(docs // rows, rows, cuts, -1).swapaxes(1, 2).reshape(devices, rows, -1)

        def by_document(x):
            if cuts == 1:
                return x.reshape(docs, -1)
            return x.reshape(docs // rows, cuts, rows, -1).swapaxes(1, 2).reshape(docs, -1)

        def exchange(x):
            return lax.all_to_all(x, AXES, 0, 0)

        def to_all(x):
            return exchange(jnp.broadcast_to(x[None], (devices,) + x.shape))

        shape = jax.ShapeDtypeStruct
        place = lax.axis_index(AXES)
        count_row = label_count[None, :]

        partial_value = kernel(
            first_kernel,
            "first",
            [HBM] * 2,
            shape((docs, hidden_width), F32),
            grant=FIRST_GRANT,
            scratch_shapes=[
                pltpu.VMEM((docs, feats), BF16),
                pltpu.VMEM((feats, hidden_width), BF16),
                pltpu.SemaphoreType.DMA((2 * len(chunks_of(feats)),)),
            ],
        )(features, w_first)
        offset = (place * labels)[None]
        partial_value, offset = lax.optimization_barrier((partial_value, offset))
        sums = exchange(by_owner(partial_value))
        own_hidden = jnp.tanh(jnp.sum(sums, axis=0)).astype(BF16)
        hidden = by_document(to_all(own_hidden))

        word_lanes = LANES * pl.cdiv(labels, LANES * WORD)
        powers, local_max, packed, hidden_turned, words = kernel(
            softmax_kernel,
            "softmax",
            [SMEM] + [VMEM] * 4,
            [
                shape((docs, labels), F32),
                shape((docs, 1), F32),
                shape((docs, 2 * hidden_width + LANES), BF16),
                shape((hidden_width, docs), BF16),
                shape((docs, word_lanes), jnp.int32),
            ],
        )(offset, label_ids.T, count_row, hidden, w_label)
        if cuts == 1 and rows == stats_rows(docs):
            back, lse, loss = kernel(
                combine_kernel,
                "combine",
                [SMEM] + [VMEM] * 3,
                [
                    shape((devices, rows, width), BF16),
                    shape((docs // LANES, LANES), F32),
                    shape((1, 1), F32),
                ],
            )(place[None], exchange(by_owner(packed)), own_hidden, count_row)
            grad_inner = by_document(exchange(back))
        else:
            stats = packed[: stats_rows(docs), 2 * hidden_width :]
            halves = by_owner(packed[:, : 2 * hidden_width].reshape(docs, 2, cuts, width).swapaxes(1, 2))
            flat = jnp.broadcast_to(stats.reshape(1, 1, -1), (devices, 1, stats.size))
            got = exchange(jnp.concatenate([halves.reshape(devices, 1, -1), flat], axis=-1))
            halves = got[:, 0, : -stats.size].reshape(devices, rows, 2, width)
            stats = got[:, 0, -stats.size :].reshape((devices,) + stats.shape)
            first_row = (place // cuts) * rows
            own_count = lax.dynamic_slice_in_dim(label_count, first_row, rows)[:, None].astype(F32)
            grad_inner, lse, loss = combine(
                halves[:, :, 0], halves[:, :, 1], stats, own_hidden, own_count, first_row, docs
            )
            grad_inner = by_document(to_all(grad_inner))

        grad_first, grad_label = kernel(
            gradient_kernel,
            "gradient",
            [VMEM] * 8,
            [shape((feats, hidden_width), BF16), shape((hidden_width, labels), BF16)],
            out_specs=[HBM] * 2,
            scratch_shapes=[
                pltpu.VMEM((feats, hidden_width), BF16),
                pltpu.VMEM((hidden_width, labels), BF16),
                pltpu.SemaphoreType.DMA((1 + len(chunks_of(labels)),)),
            ],
        )(features, hidden_turned, grad_inner, lse, powers, local_max, words, count_row)
        return (grad_first, grad_label, loss[0, 0])

    return per_device


def kernel(body, name, in_specs, out_shape, grant=GRANT, **more):
    several = isinstance(out_shape, list)
    specs = {"out_specs": [VMEM] * len(out_shape) if several else VMEM}
    return pl.pallas_call(
        body,
        name=name,
        in_specs=in_specs,
        out_shape=out_shape,
        compiler_params=pltpu.CompilerParams(vmem_limit_bytes=grant),
        **(specs | more),
    )


def solution(mesh):
    placed = (P(None, AXES), P(AXES, None), P(None, AXES), P(), P())
    devices = mesh.shape["gx"] * mesh.shape["gy"]
    return jax.shard_map(
        make_per_device(devices),
        mesh=mesh,
        in_specs=placed,
        out_specs=(P(AXES, None), P(None, AXES), P()),
        check_vma=False,
    )
```

```python
import jax
import jax.numpy as jnp
from jax import lax
from jax.experimental import pallas as pl
from jax.experimental.pallas import tpu as pltpu
from jax.sharding import PartitionSpec as P

AXES = ("gx", "gy")
LANES = 128
WORD = 32
GRANT = 12 * 1024 * 1024
FIRST_GRANT = 56164352
VMEM = pl.BlockSpec(memory_space=pltpu.VMEM)
HBM = pl.BlockSpec(memory_space=pltpu.HBM)
SMEM = pl.BlockSpec(memory_space=pltpu.SMEM)
F32, BF16 = jnp.float32, jnp.bfloat16


def chunks_of(length):
    size = next((s for s in (256, 128) if length % s == 0), length)
    return [slice(at, at + size) for at in range(0, length, size)]


def dot(a, b, dims):
    return lax.dot_general(a, b, (dims, ((), ())), preferred_element_type=F32)


def lane(shape):
    return lax.broadcasted_iota(jnp.int32, shape, len(shape) - 1)


def split3(x):
    high = lax.reduce_precision(x, 8, 7)
    rest = x - high
    middle = lax.reduce_precision(rest, 8, 7)
    return high, middle, rest - middle


def into_lanes(columns, shape):
    at = lane(shape)
    block = jnp.zeros(shape, F32)
    for index, column in enumerate(columns):
        block = jnp.where(at == index, column, block)
    return block


def column_of(row):
    return jnp.broadcast_to(row, (8, row.shape[1])).T[:, :1]


def row_of(column):
    return jnp.broadcast_to(column, (column.shape[0], 8)).T[:1]


def stats_rows(docs):
    return pl.cdiv(3 * docs // LANES + 1, 8) * 8


def stats_block(lse, scalar):
    docs = lse.shape[1]
    rows = [part[:, at : at + LANES] for part in split3(lse) for at in range(0, docs, LANES)]
    rows.append(into_lanes(split3(scalar), (1, LANES)))
    rows += [jnp.zeros((1, LANES), F32)] * (stats_rows(docs) - len(rows))
    return jnp.concatenate(rows, axis=0)


def match_blocks(ids, counts, offset):
    slots, docs = ids.shape
    in_count = lax.broadcasted_iota(jnp.int32, ids.shape, 0) < counts
    used = jnp.where(in_count, ids - offset, -1).T
    at = lane((docs, LANES))
    blocks = []
    for slot in range(slots):
        here = jnp.broadcast_to(used[:, slot : slot + 1], (docs, LANES))
        blocks.append(jnp.where((here & (LANES - 1)) == at, here >> 7, -1))
    return blocks


def match_words(ids_ref, count_ref, offset_ref, words_ref):
    blocks = match_blocks(ids_ref[...], count_ref[...], offset_ref[0])
    for index in range(words_ref.shape[1] // LANES):
        word = jnp.zeros((words_ref.shape[0], LANES), jnp.int32)
        for block in blocks:
            bit = block - WORD * index
            word = word | jnp.where((bit >= 0) & (bit < WORD), 1 << jnp.clip(bit, 0, WORD - 1), 0)
        words_ref[:, LANES * index : LANES * (index + 1)] = word


def first_kernel(
    parity_ref, features_hbm, w_first_hbm, partial_ref, send_ref, features_ref, w_first_ref, sems
):
    feats = features_hbm.shape[1]
    moves = []
    for index, piece in enumerate(chunks_of(feats)):
        for source, target in (
            (features_hbm.at[:, piece], features_ref.at[:, piece]),
            (w_first_hbm.at[piece], w_first_ref.at[piece]),
        ):
            moves.append(pltpu.make_async_copy(source, target, sems.at[len(moves)]))
            moves[-1].start()
    total = None
    for index, piece in enumerate(chunks_of(feats)):
        moves[2 * index].wait()
        moves[2 * index + 1].wait()
        part = dot(features_ref[:, piece], w_first_ref[piece], ((1,), (0,)))
        total = part if total is None else total + part
    if partial_ref.shape == total.shape:
        partial_ref[...] = total
        return
    partial_ref[...], send_ref[...] = halves_of(total, parity_ref[0], send_ref.shape[1])


def hits(words_ref, piece, yes, no):
    blocks = []
    for first in range(piece.start, piece.stop, LANES):
        word_index, bit = divmod(first // LANES, WORD)
        word = words_ref[:, LANES * word_index : LANES * (word_index + 1)]
        blocks.append(jnp.where((word & (1 << bit)) != 0, yes, no))
    return jnp.concatenate(blocks, axis=1)


def halves_of(value, parity, rows):
    split = value.reshape(-1, 2, rows, value.shape[1])
    even, odd = split[:, 0], split[:, 1]
    return jnp.where(parity == 0, even, odd), jnp.where(parity == 0, odd, even)


def softmax_kernel(
    offset_ref, parity_ref, ids_ref, count_ref, hidden_ref, w_label_ref,
    powers_ref, max_ref, turned_ref, words_ref, packed_ref, *keep_refs,
):
    docs, width = hidden_ref.shape
    pieces = chunks_of(w_label_ref.shape[1])
    hidden = hidden_ref[...]
    turned_ref[...] = hidden.T
    match_words(ids_ref, count_ref, offset_ref, words_ref)
    top = None
    for piece in pieces:
        logits = dot(hidden, w_label_ref[:, piece], ((1,), (0,)))
        powers_ref[:, piece] = logits
        top = logits if top is None else jnp.maximum(top, logits)
    local_max = jnp.max(top, axis=1, keepdims=True)
    total, sums = None, None
    for piece in pieces:
        powers = jnp.exp(powers_ref[:, piece] - local_max)
        powers_ref[:, piece] = powers
        both = [powers.astype(BF16), hits(words_ref, piece, 1.0, 0.0).astype(BF16)]
        part = dot(jnp.concatenate(both, axis=0), w_label_ref[:, piece], ((1,), (1,)))
        total = powers if total is None else total + powers
        sums = part if sums is None else sums + part
    local_sum = jnp.sum(total, axis=1, keepdims=True)
    max_ref[...] = local_max
    matched = sums[docs:]
    expected = sums[:docs] / local_sum
    picked = jnp.sum(hidden.astype(F32) * matched, axis=1, keepdims=True)
    picked = jnp.sum(picked / column_of(count_ref[...].astype(F32)), axis=0, keepdims=True)
    stats = stats_block(row_of(local_max + jnp.log(local_sum)), picked)
    if not keep_refs:
        packed_ref[:, :width] = expected.astype(BF16)
        packed_ref[:, width : 2 * width] = matched.astype(BF16)
        for first in range(0, docs, stats.shape[0]):
            packed_ref[first : first + stats.shape[0], 2 * width :] = stats.astype(BF16)
        return
    (keep_ref,) = keep_refs
    for index, value in enumerate((expected, matched)):
        mine, other = halves_of(value, parity_ref[0], packed_ref.shape[1])
        keep_ref[:, :, index * width : (index + 1) * width] = mine
        packed_ref[:, :, index * width : (index + 1) * width] = other.astype(BF16)
    wide = jnp.broadcast_to(stats[None], (keep_ref.shape[0],) + stats.shape)
    keep_ref[:, :, 2 * width :] = wide
    packed_ref[:, :, 2 * width :] = wide.astype(BF16)


def read_stats(block, docs):
    part = docs // LANES
    lse = sum(block[..., i * part : (i + 1) * part, :] for i in range(3))
    return lse, block[..., 3 * part : 3 * part + 1, :]


def pair_kernel(parity_ref, keep_ref, got_ref, packed_ref):
    half, rows, total = keep_ref.shape
    docs, width = 2 * half * rows, (total - LANES) // 2
    own_lse, own_scalar = read_stats(keep_ref[0, :, 2 * width :], docs)
    got_lse, got_scalar = read_stats(got_ref[0, :, 2 * width :].astype(F32), docs)
    top = jnp.maximum(own_lse, got_lse)
    lse = top + jnp.log(jnp.exp(own_lse - top) + jnp.exp(got_lse - top))
    expected = 0.0
    for part_lse, ref in ((own_lse, keep_ref), (got_lse, got_ref)):
        share = column_of(flat_row(jnp.exp(part_lse - lse)))
        share, _ = halves_of(share, parity_ref[0], rows)
        expected = expected + share * ref[:, :, :width].astype(F32)
    packed_ref[:, :, :width] = expected.astype(BF16)
    matched = keep_ref[:, :, width : 2 * width] + got_ref[:, :, width : 2 * width].astype(F32)
    packed_ref[:, :, width : 2 * width] = matched.astype(BF16)
    scalar = jnp.sum(own_scalar + got_scalar, axis=1, keepdims=True)
    stats = stats_block(flat_row(lse), scalar).astype(BF16)
    packed_ref[:, :, 2 * width :] = jnp.broadcast_to(stats[None], (half,) + stats.shape)


def flat_row(rows):
    return jnp.concatenate([rows[i : i + 1] for i in range(rows.shape[0])], axis=1)


def combine(expected, matched, stats, own_hidden, own_count, first_row, docs):
    rows = own_hidden.shape[0]
    part = docs // LANES
    lse_parts, picked = read_stats(stats.astype(F32), docs)
    top = jnp.max(lse_parts, axis=0)
    lse = top + jnp.log(jnp.sum(jnp.exp(lse_parts - top), axis=0))
    picked = jnp.sum(picked, axis=0)
    loss = jnp.sum(jnp.sum(lse, axis=0, keepdims=True) - picked, axis=1, keepdims=True) / docs
    shares = jnp.exp(lse_parts - lse)
    own = lane((rows, LANES)) - lax.broadcasted_iota(jnp.int32, (rows, LANES), 0) - first_row
    share = 0.0
    for index in range(part):
        share = share + jnp.where(own + LANES * index == 0, shares[:, index : index + 1], 0.0)
    share = jnp.sum(share, axis=-1, keepdims=True)
    mean_matched = jnp.sum(matched.astype(F32), axis=0) / own_count
    grad_hidden = jnp.sum(share * expected.astype(F32), axis=0) - mean_matched
    hidden = own_hidden.astype(F32)
    grad_inner = (grad_hidden * (1.0 - hidden * hidden)).astype(BF16)
    return grad_inner, lse, loss


def combine_kernel(place_ref, got_ref, own_hidden_ref, count_ref, back_ref, lse_ref, loss_ref):
    rows, width = own_hidden_ref.shape
    docs = count_ref.shape[1]
    first_row = place_ref[0] * rows
    owner = lax.broadcasted_iota(jnp.int32, (rows, docs), 0) + first_row
    counts = jnp.where(lane((rows, docs)) == owner, count_ref[...], 0)
    own_count = jnp.sum(counts.astype(F32), axis=1, keepdims=True)
    grad_inner, lse_ref[...], loss = combine(
        got_ref[:, :, :width], got_ref[:, :, width : 2 * width], got_ref[:, :, 2 * width :],
        own_hidden_ref[...], own_count, first_row, docs,
    )
    loss_ref[...] = jnp.broadcast_to(loss, loss_ref.shape)
    back_ref[...] = jnp.broadcast_to(grad_inner[None], back_ref.shape)


def gradient_kernel(
    features_ref, hidden_ref, grad_inner_ref, lse_ref, loss_ref, powers_ref, max_ref, words_ref,
    count_ref, grad_first_hbm, grad_label_hbm, loss_hbm, first_scratch, label_scratch, sems,
):
    copies = [pltpu.make_async_copy(loss_ref, loss_hbm, sems.at[0])]
    copies[0].start()
    first_scratch[...] = dot(
        features_ref[...].T, grad_inner_ref[...], ((1,), (0,))
    ).astype(BF16)
    copies.append(pltpu.make_async_copy(first_scratch, grad_first_hbm, sems.at[1]))
    copies[1].start()
    scale = jnp.exp(max_ref[...] - column_of(flat_row(lse_ref[...])))
    per_match = column_of(1.0 / count_ref[...].astype(F32))
    hidden = hidden_ref[...]
    for piece in chunks_of(powers_ref.shape[1]):
        grad_logits = powers_ref[:, piece] * scale - hits(words_ref, piece, per_match, 0.0)
        label_scratch[:, piece] = dot(hidden, grad_logits.astype(BF16), ((1,), (0,))).astype(BF16)
        copy = pltpu.make_async_copy(
            label_scratch.at[:, piece], grad_label_hbm.at[:, piece], sems.at[len(copies)]
        )
        copy.start()
        copies.append(copy)
    for copy in copies:
        copy.wait()


def make_per_device(devices):
    def per_device(features, w_first, w_label, label_ids, label_count):
        docs, hidden_width = features.shape[0], w_first.shape[1]
        feats, labels = features.shape[1], w_label.shape[1]
        rows = max(1, docs // devices)
        cuts = devices * rows // docs
        width = hidden_width // cuts
        paired = cuts == 1 and rows == stats_rows(docs)

        def by_owner(x):
            if cuts == 1:
                return x.reshape(devices, rows, -1)
            return x.reshape(docs // rows, rows, cuts, -1).swapaxes(1, 2).reshape(devices, rows, -1)

        def by_document(x):
            if cuts == 1:
                return x.reshape(docs, -1)
            return x.reshape(docs // rows, cuts, rows, -1).swapaxes(1, 2).reshape(docs, -1)

        def exchange(x):
            return lax.all_to_all(x, AXES, 0, 0)

        def exchange_halves(x):
            groups = [list(range(first, devices, 2)) for first in (0, 1)]
            return lax.all_to_all(x, AXES, 0, 0, axis_index_groups=groups)

        def to_partner(x):
            return lax.ppermute(x, AXES, [(i, i ^ 1) for i in range(devices)])

        def to_all(x):
            return exchange(jnp.broadcast_to(x[None], (devices,) + x.shape))

        shape = jax.ShapeDtypeStruct
        place = lax.axis_index(AXES)
        count_row = label_count[None, :]

        offset, parity = (place * labels)[None], (place & 1)[None]
        offset, parity = lax.optimization_barrier((offset, parity))
        half = (devices // 2, rows, hidden_width)
        partial_value, send = kernel(
            first_kernel,
            "first",
            [SMEM] + [HBM] * 2,
            [shape(half if paired else (docs, hidden_width), F32), shape(half if paired else (8, LANES), F32)],
            grant=FIRST_GRANT,
            scratch_shapes=[
                pltpu.VMEM((docs, feats), BF16),
                pltpu.VMEM((feats, hidden_width), BF16),
                pltpu.SemaphoreType.DMA((2 * len(chunks_of(feats)),)),
            ],
        )(parity, features, w_first)
        if paired:
            partial_value, offset = lax.optimization_barrier((partial_value, offset))
            sums = exchange_halves(partial_value + to_partner(send))
        else:
            sums = exchange(by_owner(partial_value))
        own_hidden = jnp.tanh(jnp.sum(sums, axis=0)).astype(BF16)
        hidden = by_document(to_all(own_hidden))

        word_lanes = LANES * pl.cdiv(labels, LANES * WORD)
        packed_width = 2 * hidden_width + LANES
        if paired:
            half = (devices // 2, rows, packed_width)
            packed_shapes = [shape(half, BF16), shape(half, F32)]
        else:
            packed_shapes = [shape((docs, packed_width), BF16)]
        powers, local_max, hidden_turned, words, packed, *keep = kernel(
            softmax_kernel,
            "softmax",
            [SMEM] * 2 + [VMEM] * 4,
            [
                shape((docs, labels), F32),
                shape((docs, 1), F32),
                shape((hidden_width, docs), BF16),
                shape((docs, word_lanes), jnp.int32),
            ]
            + packed_shapes,
        )(offset, parity, label_ids.T, count_row, hidden, w_label)
        if paired:
            packed = kernel(pair_kernel, "pair", [SMEM] + [VMEM] * 2, shape(half, BF16))(
                parity, keep[0], to_partner(packed)
            )
            back, lse, loss = kernel(
                combine_kernel,
                "combine",
                [SMEM] + [VMEM] * 3,
                [
                    shape((devices, rows, width), BF16),
                    shape((docs // LANES, LANES), F32),
                    shape((1, LANES), F32),
                ],
            )(place[None], exchange_halves(packed), own_hidden, count_row)
            grad_inner = by_document(exchange(back))
        else:
            stats = packed[: stats_rows(docs), 2 * hidden_width :]
            halves = by_owner(packed[:, : 2 * hidden_width].reshape(docs, 2, cuts, width).swapaxes(1, 2))
            flat = jnp.broadcast_to(stats.reshape(1, 1, -1), (devices, 1, stats.size))
            got = exchange(jnp.concatenate([halves.reshape(devices, 1, -1), flat], axis=-1))
            halves = got[:, 0, : -stats.size].reshape(devices, rows, 2, width)
            stats = got[:, 0, -stats.size :].reshape((devices,) + stats.shape)
            first_row = (place // cuts) * rows
            own_count = lax.dynamic_slice_in_dim(label_count, first_row, rows)[:, None].astype(F32)
            grad_inner, lse, loss = combine(
                halves[:, :, 0], halves[:, :, 1], stats, own_hidden, own_count, first_row, docs
            )
            loss = jnp.broadcast_to(loss, (1, LANES))
            grad_inner = by_document(to_all(grad_inner))

        grad_first, grad_label, mean_loss = kernel(
            gradient_kernel,
            "gradient",
            [VMEM] * 9,
            [
                shape((feats, hidden_width), BF16),
                shape((hidden_width, labels), BF16),
                shape((1, LANES), F32),
            ],
            out_specs=[HBM] * 3,
            scratch_shapes=[
                pltpu.VMEM((feats, hidden_width), BF16),
                pltpu.VMEM((hidden_width, labels), BF16),
                pltpu.SemaphoreType.DMA((2 + len(chunks_of(labels)),)),
            ],
        )(features, hidden_turned, grad_inner, lse, loss, powers, local_max, words, count_row)
        return (grad_first, grad_label, mean_loss[0, 0])

    return per_device


def kernel(body, name, in_specs, out_shape, grant=GRANT, **more):
    several = isinstance(out_shape, list)
    specs = {"out_specs": [VMEM] * len(out_shape) if several else VMEM}
    return pl.pallas_call(
        body,
        name=name,
        in_specs=in_specs,
        out_shape=out_shape,
        compiler_params=pltpu.CompilerParams(vmem_limit_bytes=grant),
        **(specs | more),
    )


def solution(mesh):
    placed = (P(None, AXES), P(AXES, None), P(None, AXES), P(), P())
    devices = mesh.shape["gx"] * mesh.shape["gy"]
    return jax.shard_map(
        make_per_device(devices),
        mesh=mesh,
        in_specs=placed,
        out_specs=(P(AXES, None), P(None, AXES), P()),
        check_vma=False,
    )
```

```python
import jax
import jax.numpy as jnp
from jax import lax
from jax.experimental import pallas as pl
from jax.experimental.pallas import tpu as pltpu
from jax.sharding import PartitionSpec as P

AXES = ("gx", "gy")
LANES, LANE_BITS = 128, 7
WORD = 31
GRANT = 12 * 1024 * 1024
FIRST_GRANT = 56164352
VMEM = pl.BlockSpec(memory_space=pltpu.VMEM)
HBM = pl.BlockSpec(memory_space=pltpu.HBM)
SMEM = pl.BlockSpec(memory_space=pltpu.SMEM)
F32, BF16 = jnp.float32, jnp.bfloat16


def chunks_of(length):
    size = next((s for s in (256, 128) if length % s == 0), length)
    return [slice(at, at + size) for at in range(0, length, size)]


def dot(a, b, dims):
    return lax.dot_general(a, b, (dims, ((), ())), preferred_element_type=F32)


def lane(shape):
    return lax.broadcasted_iota(jnp.int32, shape, len(shape) - 1)


def split3(x):
    high = lax.reduce_precision(x, 8, 7)
    rest = x - high
    middle = lax.reduce_precision(rest, 8, 7)
    return high, middle, rest - middle


def into_lanes(columns, shape):
    at = lane(shape)
    block = jnp.zeros(shape, F32)
    for index, column in enumerate(columns):
        block = jnp.where(at == index, column, block)
    return block


def column_of(row):
    return jnp.broadcast_to(row, (8, row.shape[1])).T[:, :1]


def row_of(column):
    return jnp.broadcast_to(column, (column.shape[0], 8)).T[:1]


def stats_rows(docs):
    return pl.cdiv(3 * docs // LANES + 1, 8) * 8


def stats_block(lse, scalar):
    docs = lse.shape[1]
    rows = [part[:, at : at + LANES] for part in split3(lse) for at in range(0, docs, LANES)]
    rows.append(into_lanes(split3(scalar), (1, LANES)))
    rows += [jnp.zeros((1, LANES), F32)] * (stats_rows(docs) - len(rows))
    return jnp.concatenate(rows, axis=0)


def match_words(ids_ref, count_ref, offset_ref, labels):
    slots, docs = ids_ref.shape
    ids = ids_ref[...] - offset_ref[0]
    in_count = lax.broadcasted_iota(jnp.int32, ids.shape, 0) < count_ref[...]
    used = in_count & (ids >= 0) & (ids < labels)
    words = []
    for index in range(word_lanes(labels) // LANES):
        bit = (ids >> LANE_BITS) - WORD * index
        bit = jnp.where(used & (bit >= 0) & (bit < WORD), bit, WORD)
        places = (bit * LANES + (ids & (LANES - 1))).T
        word = jnp.zeros((docs, LANES), jnp.int32)
        for slot in range(slots):
            here = jnp.broadcast_to(places[:, slot : slot + 1], (docs, LANES))
            hit = (here & (LANES - 1)) == lane((docs, LANES))
            word = word | jnp.where(hit, 1 << (here >> LANE_BITS), 0)
        words.append(word)
    return jnp.concatenate(words, axis=1)


def word_lanes(labels):
    return LANES * pl.cdiv(labels, LANES * WORD)


def first_kernel(
    parity_ref, features_hbm, w_first_hbm, partial_ref, send_ref, features_ref, w_first_ref, sems
):
    moves = [
        pltpu.make_async_copy(features_hbm, features_ref, sems.at[0]),
        pltpu.make_async_copy(w_first_hbm, w_first_ref, sems.at[1]),
    ]
    for move in moves:
        move.start()
    for move in moves:
        move.wait()
    total = dot(features_ref[...], w_first_ref[...], ((1,), (0,)))
    if partial_ref.shape == total.shape:
        partial_ref[...] = total
        return
    partial_ref[...], send_ref[...] = halves_of(total, parity_ref[0], send_ref.shape[1])


def hits(words_ref, piece, yes, no):
    blocks = []
    for first in range(piece.start, piece.stop, LANES):
        word_index, bit = divmod(first // LANES, WORD)
        word = words_ref[:, LANES * word_index : LANES * (word_index + 1)]
        blocks.append(jnp.where((word & (1 << bit)) != 0, yes, no))
    return jnp.concatenate(blocks, axis=1)


def halves_of(value, parity, rows):
    split = value.reshape(-1, 2, rows, value.shape[1])
    even, odd = split[:, 0], split[:, 1]
    return jnp.where(parity == 0, even, odd), jnp.where(parity == 0, odd, even)


def softmax_kernel(
    offset_ref, parity_ref, ids_ref, count_ref, hidden_ref, w_label_ref,
    powers_ref, max_ref, turned_ref, words_ref, packed_ref, *keep_refs,
):
    docs, width = hidden_ref.shape
    pieces = chunks_of(w_label_ref.shape[1])
    hidden = hidden_ref[...]
    turned_ref[...] = hidden.T
    words_ref[...] = match_words(ids_ref, count_ref, offset_ref, w_label_ref.shape[1])
    top = None
    for piece in pieces:
        logits = dot(hidden, w_label_ref[:, piece], ((1,), (0,)))
        powers_ref[:, piece] = logits
        top = logits if top is None else jnp.maximum(top, logits)
    local_max = jnp.max(top, axis=1, keepdims=True)
    total, sums = None, None
    for piece in pieces:
        powers = jnp.exp(powers_ref[:, piece] - local_max)
        powers_ref[:, piece] = powers
        both = [powers.astype(BF16), hits(words_ref, piece, 1.0, 0.0).astype(BF16)]
        part = dot(jnp.concatenate(both, axis=0), w_label_ref[:, piece], ((1,), (1,)))
        total = powers if total is None else total + powers
        sums = part if sums is None else sums + part
    local_sum = jnp.sum(total, axis=1, keepdims=True)
    max_ref[...] = local_max
    matched = sums[docs:]
    expected = sums[:docs] / local_sum
    picked = jnp.sum(hidden.astype(F32) * matched, axis=1, keepdims=True)
    picked = jnp.sum(picked / column_of(count_ref[...].astype(F32)), axis=0, keepdims=True)
    stats = stats_block(row_of(local_max + jnp.log(local_sum)), picked)
    if not keep_refs:
        packed_ref[:, :width] = expected.astype(BF16)
        packed_ref[:, width : 2 * width] = matched.astype(BF16)
        for first in range(0, docs, stats.shape[0]):
            packed_ref[first : first + stats.shape[0], 2 * width :] = stats.astype(BF16)
        return
    (keep_ref,) = keep_refs
    for index, value in enumerate((expected, matched)):
        mine, other = halves_of(value, parity_ref[0], packed_ref.shape[1])
        keep_ref[:, :, index * width : (index + 1) * width] = mine
        packed_ref[:, :, index * width : (index + 1) * width] = other.astype(BF16)
    wide = jnp.broadcast_to(stats[None], (keep_ref.shape[0],) + stats.shape)
    keep_ref[:, :, 2 * width :] = wide
    packed_ref[:, :, 2 * width :] = wide.astype(BF16)


def read_stats(block, docs):
    part = docs // LANES
    lse = sum(block[..., i * part : (i + 1) * part, :] for i in range(3))
    return lse, block[..., 3 * part : 3 * part + 1, :]


def pair_kernel(parity_ref, keep_ref, got_ref, packed_ref):
    half, rows, total = keep_ref.shape
    docs, width = 2 * half * rows, (total - LANES) // 2
    own_lse, own_scalar = read_stats(keep_ref[0, :, 2 * width :], docs)
    got_lse, got_scalar = read_stats(got_ref[0, :, 2 * width :].astype(F32), docs)
    top = jnp.maximum(own_lse, got_lse)
    lse = top + jnp.log(jnp.exp(own_lse - top) + jnp.exp(got_lse - top))
    expected = 0.0
    for part_lse, ref in ((own_lse, keep_ref), (got_lse, got_ref)):
        share = column_of(flat_row(jnp.exp(part_lse - lse)))
        share, _ = halves_of(share, parity_ref[0], rows)
        expected = expected + share * ref[:, :, :width].astype(F32)
    packed_ref[:, :, :width] = expected.astype(BF16)
    matched = keep_ref[:, :, width : 2 * width] + got_ref[:, :, width : 2 * width].astype(F32)
    packed_ref[:, :, width : 2 * width] = matched.astype(BF16)
    scalar = jnp.sum(own_scalar + got_scalar, axis=1, keepdims=True)
    stats = stats_block(flat_row(lse), scalar).astype(BF16)
    packed_ref[:, :, 2 * width :] = jnp.broadcast_to(stats[None], (half,) + stats.shape)


def flat_row(rows):
    return jnp.concatenate([rows[i : i + 1] for i in range(rows.shape[0])], axis=1)


def combine(expected, matched, stats, own_hidden, own_count, first_row, docs):
    rows = own_hidden.shape[0]
    part = docs // LANES
    lse_parts, picked = read_stats(stats.astype(F32), docs)
    top = jnp.max(lse_parts, axis=0)
    lse = top + jnp.log(jnp.sum(jnp.exp(lse_parts - top), axis=0))
    picked = jnp.sum(picked, axis=0)
    loss = jnp.sum(jnp.sum(lse, axis=0, keepdims=True) - picked, axis=1, keepdims=True) / docs
    shares = jnp.exp(lse_parts - lse)
    own = lane((rows, LANES)) - lax.broadcasted_iota(jnp.int32, (rows, LANES), 0) - first_row
    share = 0.0
    for index in range(part):
        share = share + jnp.where(own + LANES * index == 0, shares[:, index : index + 1], 0.0)
    share = jnp.sum(share, axis=-1, keepdims=True)
    mean_matched = jnp.sum(matched.astype(F32), axis=0) / own_count
    grad_hidden = jnp.sum(share * expected.astype(F32), axis=0) - mean_matched
    hidden = own_hidden.astype(F32)
    grad_inner = (grad_hidden * (1.0 - hidden * hidden)).astype(BF16)
    return grad_inner, lse, loss


def combine_kernel(place_ref, got_ref, own_hidden_ref, count_ref, back_ref, lse_ref, loss_ref):
    rows, width = own_hidden_ref.shape
    docs = count_ref.shape[1]
    first_row = place_ref[0] * rows
    owner = lax.broadcasted_iota(jnp.int32, (rows, docs), 0) + first_row
    counts = jnp.where(lane((rows, docs)) == owner, count_ref[...], 0)
    own_count = jnp.sum(counts.astype(F32), axis=1, keepdims=True)
    grad_inner, lse_ref[...], loss = combine(
        got_ref[:, :, :width], got_ref[:, :, width : 2 * width], got_ref[:, :, 2 * width :],
        own_hidden_ref[...], own_count, first_row, docs,
    )
    loss_ref[...] = jnp.broadcast_to(loss, loss_ref.shape)
    back_ref[...] = jnp.broadcast_to(grad_inner[None], back_ref.shape)


def gradient_kernel(
    features_ref, hidden_ref, grad_inner_ref, lse_ref, loss_ref, powers_ref, max_ref, words_ref,
    count_ref, grad_first_hbm, grad_label_hbm, loss_hbm, first_scratch, label_scratch, sems,
):
    copies = [pltpu.make_async_copy(loss_ref, loss_hbm, sems.at[0])]
    copies[0].start()
    first_scratch[...] = dot(
        features_ref[...].T, grad_inner_ref[...], ((1,), (0,))
    ).astype(BF16)
    copies.append(pltpu.make_async_copy(first_scratch, grad_first_hbm, sems.at[1]))
    copies[1].start()
    scale = jnp.exp(max_ref[...] - column_of(flat_row(lse_ref[...])))
    per_match = column_of(1.0 / count_ref[...].astype(F32))
    hidden = hidden_ref[...]
    for piece in chunks_of(powers_ref.shape[1]):
        grad_logits = powers_ref[:, piece] * scale - hits(words_ref, piece, per_match, 0.0)
        label_scratch[:, piece] = dot(hidden, grad_logits.astype(BF16), ((1,), (0,))).astype(BF16)
        copy = pltpu.make_async_copy(
            label_scratch.at[:, piece], grad_label_hbm.at[:, piece], sems.at[len(copies)]
        )
        copy.start()
        copies.append(copy)
    for copy in copies:
        copy.wait()


def make_per_device(devices):
    def per_device(features, w_first, w_label, label_ids, label_count):
        docs, hidden_width = features.shape[0], w_first.shape[1]
        feats, labels = features.shape[1], w_label.shape[1]
        rows = max(1, docs // devices)
        cuts = devices * rows // docs
        width = hidden_width // cuts
        paired = cuts == 1 and rows == stats_rows(docs)

        def by_owner(x):
            if cuts == 1:
                return x.reshape(devices, rows, -1)
            return x.reshape(docs // rows, rows, cuts, -1).swapaxes(1, 2).reshape(devices, rows, -1)

        def by_document(x):
            if cuts == 1:
                return x.reshape(docs, -1)
            return x.reshape(docs // rows, cuts, rows, -1).swapaxes(1, 2).reshape(docs, -1)

        def exchange(x):
            return lax.all_to_all(x, AXES, 0, 0)

        def exchange_halves(x):
            groups = [list(range(first, devices, 2)) for first in (0, 1)]
            return lax.all_to_all(x, AXES, 0, 0, axis_index_groups=groups)

        def to_partner(x):
            return lax.ppermute(x, AXES, [(i, i ^ 1) for i in range(devices)])

        def to_all(x):
            return exchange(jnp.broadcast_to(x[None], (devices,) + x.shape))

        shape = jax.ShapeDtypeStruct
        place = lax.axis_index(AXES)
        count_row = label_count[None, :]

        offset, parity = (place * labels)[None], (place & 1)[None]
        offset, parity = lax.optimization_barrier((offset, parity))
        half = (devices // 2, rows, hidden_width)
        partial_value, send = kernel(
            first_kernel,
            "first",
            [SMEM] + [HBM] * 2,
            [shape(half if paired else (docs, hidden_width), F32), shape(half if paired else (8, LANES), F32)],
            grant=FIRST_GRANT,
            scratch_shapes=[
                pltpu.VMEM((docs, feats), BF16),
                pltpu.VMEM((feats, hidden_width), BF16),
                pltpu.SemaphoreType.DMA((2,)),
            ],
        )(parity, features, w_first)
        if paired:
            sums = exchange_halves(partial_value + to_partner(send))
        else:
            sums = exchange(by_owner(partial_value))
        own_hidden = jnp.tanh(jnp.sum(sums, axis=0)).astype(BF16)
        hidden = by_document(to_all(own_hidden))

        packed_width = 2 * hidden_width + LANES
        if paired:
            half = (devices // 2, rows, packed_width)
            packed_shapes = [shape(half, BF16), shape(half, F32)]
        else:
            packed_shapes = [shape((docs, packed_width), BF16)]
        powers, local_max, hidden_turned, words, packed, *keep = kernel(
            softmax_kernel,
            "softmax",
            [SMEM] * 2 + [VMEM] * 4,
            [
                shape((docs, labels), F32),
                shape((docs, 1), F32),
                shape((hidden_width, docs), BF16),
                shape((docs, word_lanes(labels)), jnp.int32),
            ]
            + packed_shapes,
        )(offset, parity, label_ids.T, count_row, hidden, w_label)
        if paired:
            packed = kernel(pair_kernel, "pair", [SMEM] + [VMEM] * 2, shape(half, BF16))(
                parity, keep[0], to_partner(packed)
            )
            back, lse, loss = kernel(
                combine_kernel,
                "combine",
                [SMEM] + [VMEM] * 3,
                [
                    shape((devices, rows, width), BF16),
                    shape((docs // LANES, LANES), F32),
                    shape((1, LANES), F32),
                ],
            )(place[None], exchange_halves(packed), own_hidden, count_row)
            grad_inner = by_document(exchange(back))
        else:
            stats = packed[: stats_rows(docs), 2 * hidden_width :]
            halves = by_owner(packed[:, : 2 * hidden_width].reshape(docs, 2, cuts, width).swapaxes(1, 2))
            flat = jnp.broadcast_to(stats.reshape(1, 1, -1), (devices, 1, stats.size))
            got = exchange(jnp.concatenate([halves.reshape(devices, 1, -1), flat], axis=-1))
            halves = got[:, 0, : -stats.size].reshape(devices, rows, 2, width)
            stats = got[:, 0, -stats.size :].reshape((devices,) + stats.shape)
            first_row = (place // cuts) * rows
            own_count = lax.dynamic_slice_in_dim(label_count, first_row, rows)[:, None].astype(F32)
            grad_inner, lse, loss = combine(
                halves[:, :, 0], halves[:, :, 1], stats, own_hidden, own_count, first_row, docs
            )
            loss = jnp.broadcast_to(loss, (1, LANES))
            grad_inner = by_document(to_all(grad_inner))

        grad_first, grad_label, mean_loss = kernel(
            gradient_kernel,
            "gradient",
            [VMEM] * 9,
            [
                shape((feats, hidden_width), BF16),
                shape((hidden_width, labels), BF16),
                shape((1, LANES), F32),
            ],
            out_specs=[HBM] * 3,
            scratch_shapes=[
                pltpu.VMEM((feats, hidden_width), BF16),
                pltpu.VMEM((hidden_width, labels), BF16),
                pltpu.SemaphoreType.DMA((2 + len(chunks_of(labels)),)),
            ],
        )(features, hidden_turned, grad_inner, lse, loss, powers, local_max, words, count_row)
        return (grad_first, grad_label, mean_loss[0, 0])

    return per_device


def kernel(body, name, in_specs, out_shape, grant=GRANT, **more):
    several = isinstance(out_shape, list)
    specs = {"out_specs": [VMEM] * len(out_shape) if several else VMEM}
    return pl.pallas_call(
        body,
        name=name,
        in_specs=in_specs,
        out_shape=out_shape,
        compiler_params=pltpu.CompilerParams(vmem_limit_bytes=grant),
        **(specs | more),
    )


def solution(mesh):
    placed = (P(None, AXES), P(AXES, None), P(None, AXES), P(), P())
    devices = mesh.shape["gx"] * mesh.shape["gy"]
    return jax.shard_map(
        make_per_device(devices),
        mesh=mesh,
        in_specs=placed,
        out_specs=(P(AXES, None), P(None, AXES), P()),
        check_vma=False,
    )
```

```python
import jax
import jax.numpy as jnp
from jax import lax
from jax.experimental import pallas as pl
from jax.experimental.pallas import tpu as pltpu
from jax.sharding import PartitionSpec as P

AXES = ("gx", "gy")
LANES, LANE_BITS = 128, 7
WORD = 31
GRANT = 12 * 1024 * 1024
FIRST_GRANT = 56164352
VMEM = pl.BlockSpec(memory_space=pltpu.VMEM)
HBM = pl.BlockSpec(memory_space=pltpu.HBM)
SMEM = pl.BlockSpec(memory_space=pltpu.SMEM)
F32, BF16 = jnp.float32, jnp.bfloat16


def chunks_of(length):
    size = next((s for s in (256, 128) if length % s == 0), length)
    return [slice(at, at + size) for at in range(0, length, size)]


def dot(a, b, dims):
    return lax.dot_general(a, b, (dims, ((), ())), preferred_element_type=F32)


def lane(shape):
    return lax.broadcasted_iota(jnp.int32, shape, len(shape) - 1)


def split3(x):
    high = lax.reduce_precision(x, 8, 7)
    rest = x - high
    middle = lax.reduce_precision(rest, 8, 7)
    return high, middle, rest - middle


def into_lanes(columns, shape):
    at = lane(shape)
    block = jnp.zeros(shape, F32)
    for index, column in enumerate(columns):
        block = jnp.where(at == index, column, block)
    return block


def column_of(row):
    return jnp.broadcast_to(row, (8, row.shape[1])).T[:, :1]


def row_of(column):
    return jnp.broadcast_to(column, (column.shape[0], 8)).T[:1]


def stats_rows(docs):
    return pl.cdiv(3 * docs // LANES + 1, 8) * 8


def stats_block(lse, scalar):
    docs = lse.shape[1]
    rows = [part[:, at : at + LANES] for part in split3(lse) for at in range(0, docs, LANES)]
    rows.append(into_lanes(split3(scalar), (1, LANES)))
    rows += [jnp.zeros((1, LANES), F32)] * (stats_rows(docs) - len(rows))
    return jnp.concatenate(rows, axis=0)


def match_words(ids_ref, count_ref, offset_ref, labels):
    slots, docs = ids_ref.shape
    ids = ids_ref[...] - offset_ref[0]
    in_count = lax.broadcasted_iota(jnp.int32, ids.shape, 0) < count_ref[...]
    used = in_count & (ids >= 0) & (ids < labels)
    words = []
    for index in range(word_lanes(labels) // LANES):
        bit = (ids >> LANE_BITS) - WORD * index
        bit = jnp.where(used & (bit >= 0) & (bit < WORD), bit, WORD)
        places = (bit * LANES + (ids & (LANES - 1))).T
        word = jnp.zeros((docs, LANES), jnp.int32)
        for slot in range(slots):
            here = jnp.broadcast_to(places[:, slot : slot + 1], (docs, LANES))
            hit = (here & (LANES - 1)) == lane((docs, LANES))
            word = word | jnp.where(hit, 1 << (here >> LANE_BITS), 0)
        words.append(word)
    return jnp.concatenate(words, axis=1)


def word_lanes(labels):
    return LANES * pl.cdiv(labels, LANES * WORD)


def first_kernel(
    parity_ref, features_hbm, w_first_hbm, partial_ref, send_ref, features_ref, w_first_ref, sems
):
    moves = [
        pltpu.make_async_copy(features_hbm, features_ref, sems.at[0]),
        pltpu.make_async_copy(w_first_hbm, w_first_ref, sems.at[1]),
    ]
    for move in moves:
        move.start()
    for move in moves:
        move.wait()
    total = dot(features_ref[...], w_first_ref[...], ((1,), (0,)))
    if partial_ref.shape == total.shape:
        partial_ref[...] = total
        return
    partial_ref[...], send_ref[...] = halves_of(total, parity_ref[0], send_ref.shape[1])


def hits(words_ref, piece, yes, no):
    blocks = []
    for first in range(piece.start, piece.stop, LANES):
        word_index, bit = divmod(first // LANES, WORD)
        word = words_ref[:, LANES * word_index : LANES * (word_index + 1)]
        blocks.append(jnp.where((word & (1 << bit)) != 0, yes, no))
    return jnp.concatenate(blocks, axis=1)


def halves_of(value, parity, rows):
    split = value.reshape(-1, 2, rows, value.shape[1])
    even, odd = split[:, 0], split[:, 1]
    return jnp.where(parity == 0, even, odd), jnp.where(parity == 0, odd, even)


def softmax_kernel(
    offset_ref, parity_ref, ids_ref, count_ref, hidden_ref, w_label_ref,
    powers_ref, max_ref, turned_ref, words_ref, packed_ref, *keep_refs,
):
    docs, width = hidden_ref.shape
    pieces = chunks_of(w_label_ref.shape[1])
    hidden = hidden_ref[...]
    turned_ref[...] = hidden.T
    words_ref[...] = match_words(ids_ref, count_ref, offset_ref, w_label_ref.shape[1])
    top = None
    for piece in pieces:
        logits = dot(hidden, w_label_ref[:, piece], ((1,), (0,)))
        powers_ref[:, piece] = logits
        top = logits if top is None else jnp.maximum(top, logits)
    local_max = jnp.max(top, axis=1, keepdims=True)
    total, sums = None, None
    for piece in pieces:
        powers = jnp.exp(powers_ref[:, piece] - local_max)
        powers_ref[:, piece] = powers
        both = [powers.astype(BF16), hits(words_ref, piece, 1.0, 0.0).astype(BF16)]
        part = dot(jnp.concatenate(both, axis=0), w_label_ref[:, piece], ((1,), (1,)))
        total = powers if total is None else total + powers
        sums = part if sums is None else sums + part
    local_sum = jnp.sum(total, axis=1, keepdims=True)
    max_ref[...] = local_max
    matched = sums[docs:]
    expected = sums[:docs] / local_sum
    picked = jnp.sum(hidden.astype(F32) * matched, axis=1, keepdims=True)
    picked = jnp.sum(picked / column_of(count_ref[...].astype(F32)), axis=0, keepdims=True)
    stats = stats_block(row_of(local_max + jnp.log(local_sum)), picked)
    if not keep_refs:
        packed_ref[:, :width] = expected.astype(BF16)
        packed_ref[:, width : 2 * width] = matched.astype(BF16)
        for first in range(0, docs, stats.shape[0]):
            packed_ref[first : first + stats.shape[0], 2 * width :] = stats.astype(BF16)
        return
    (keep_ref,) = keep_refs
    for index, value in enumerate((expected, matched)):
        mine, other = halves_of(value, parity_ref[0], packed_ref.shape[1])
        keep_ref[:, :, index * width : (index + 1) * width] = mine
        packed_ref[:, :, index * width : (index + 1) * width] = other.astype(BF16)
    wide = jnp.broadcast_to(stats[None], (keep_ref.shape[0],) + stats.shape)
    keep_ref[:, :, 2 * width :] = wide
    packed_ref[:, :, 2 * width :] = wide.astype(BF16)


def read_stats(block, docs):
    part = docs // LANES
    lse = sum(block[..., i * part : (i + 1) * part, :] for i in range(3))
    return lse, block[..., 3 * part : 3 * part + 1, :]


def pair_kernel(parity_ref, keep_ref, got_ref, packed_ref):
    half, rows, total = keep_ref.shape
    docs, width = 2 * half * rows, (total - LANES) // 2
    own_lse, own_scalar = read_stats(keep_ref[0, :, 2 * width :], docs)
    got_lse, got_scalar = read_stats(got_ref[0, :, 2 * width :].astype(F32), docs)
    top = jnp.maximum(own_lse, got_lse)
    lse = top + jnp.log(jnp.exp(own_lse - top) + jnp.exp(got_lse - top))
    expected = 0.0
    for part_lse, ref in ((own_lse, keep_ref), (got_lse, got_ref)):
        share = column_of(flat_row(jnp.exp(part_lse - lse)))
        share, _ = halves_of(share, parity_ref[0], rows)
        expected = expected + share * ref[:, :, :width].astype(F32)
    packed_ref[:, :, :width] = expected.astype(BF16)
    matched = keep_ref[:, :, width : 2 * width] + got_ref[:, :, width : 2 * width].astype(F32)
    packed_ref[:, :, width : 2 * width] = matched.astype(BF16)
    scalar = jnp.sum(own_scalar + got_scalar, axis=1, keepdims=True)
    stats = stats_block(flat_row(lse), scalar).astype(BF16)
    packed_ref[:, :, 2 * width :] = jnp.broadcast_to(stats[None], (half,) + stats.shape)


def flat_row(rows):
    return jnp.concatenate([rows[i : i + 1] for i in range(rows.shape[0])], axis=1)


def combine(expected, matched, stats, own_hidden, own_count, first_row, docs):
    rows = own_hidden.shape[0]
    part = docs // LANES
    lse_parts, picked = read_stats(stats.astype(F32), docs)
    top = jnp.max(lse_parts, axis=0)
    lse = top + jnp.log(jnp.sum(jnp.exp(lse_parts - top), axis=0))
    picked = jnp.sum(picked, axis=0)
    loss = jnp.sum(jnp.sum(lse, axis=0, keepdims=True) - picked, axis=1, keepdims=True) / docs
    shares = jnp.exp(lse_parts - lse)
    own = lane((rows, LANES)) - lax.broadcasted_iota(jnp.int32, (rows, LANES), 0) - first_row
    share = 0.0
    for index in range(part):
        share = share + jnp.where(own + LANES * index == 0, shares[:, index : index + 1], 0.0)
    share = jnp.sum(share, axis=-1, keepdims=True)
    mean_matched = jnp.sum(matched.astype(F32), axis=0) / own_count
    grad_hidden = jnp.sum(share * expected.astype(F32), axis=0) - mean_matched
    hidden = own_hidden.astype(F32)
    grad_inner = (grad_hidden * (1.0 - hidden * hidden)).astype(BF16)
    return grad_inner, lse, loss


def combine_kernel(place_ref, got_ref, own_hidden_ref, count_ref, back_ref, lse_ref, loss_ref):
    rows, width = own_hidden_ref.shape
    docs = count_ref.shape[1]
    first_row = place_ref[0] * rows
    owner = lax.broadcasted_iota(jnp.int32, (rows, docs), 0) + first_row
    counts = jnp.where(lane((rows, docs)) == owner, count_ref[...], 0)
    own_count = jnp.sum(counts.astype(F32), axis=1, keepdims=True)
    grad_inner, lse_ref[...], loss = combine(
        got_ref[:, :, :width], got_ref[:, :, width : 2 * width], got_ref[:, :, 2 * width :],
        own_hidden_ref[...], own_count, first_row, docs,
    )
    loss_ref[...] = jnp.broadcast_to(loss, loss_ref.shape)
    half = width // 2
    for parity in (0, 1):
        part = grad_inner[:, parity * half : (parity + 1) * half]
        for index in range(parity, back_ref.shape[0], 2):
            back_ref[index] = part


def label_kernel(hidden_ref, lse_ref, powers_ref, max_ref, words_ref, count_ref, grad_label_ref):
    scale = jnp.exp(max_ref[...] - column_of(flat_row(lse_ref[...])))
    per_match = column_of(1.0 / count_ref[...].astype(F32))
    hidden = hidden_ref[...]
    for piece in chunks_of(powers_ref.shape[1]):
        grad_logits = powers_ref[:, piece] * scale - hits(words_ref, piece, per_match, 0.0)
        grad_label_ref[:, piece] = dot(hidden, grad_logits.astype(BF16), ((1,), (0,))).astype(BF16)


def last_kernel(
    parity_ref, features_ref, label_ref, loss_ref, *refs,
):
    *grad_inner_refs, grad_first_hbm, grad_label_hbm, loss_hbm, first_scratch, sems = refs
    copies = [
        pltpu.make_async_copy(label_ref, grad_label_hbm, sems.at[0]),
        pltpu.make_async_copy(loss_ref, loss_hbm, sems.at[1]),
        pltpu.make_async_copy(first_scratch, grad_first_hbm, sems.at[2]),
    ]
    copies[0].start()
    copies[1].start()
    if len(grad_inner_refs) == 1:
        grad_inner = grad_inner_refs[0][...]
    else:
        own, other = (ref[...].astype(F32) for ref in grad_inner_refs)
        even = parity_ref[0] == 0
        both = [jnp.where(even, own, other), jnp.where(even, other, own)]
        grad_inner = jnp.concatenate(both, axis=1).astype(BF16)
    first_scratch[...] = dot(features_ref[...].T, grad_inner, ((1,), (0,))).astype(BF16)
    copies[2].start()
    for copy in copies:
        copy.wait()


def make_per_device(devices):
    def per_device(features, w_first, w_label, label_ids, label_count):
        docs, hidden_width = features.shape[0], w_first.shape[1]
        feats, labels = features.shape[1], w_label.shape[1]
        rows = max(1, docs // devices)
        cuts = devices * rows // docs
        width = hidden_width // cuts
        paired = cuts == 1 and rows == stats_rows(docs) and width % (2 * LANES) == 0

        def by_owner(x):
            if cuts == 1:
                return x.reshape(devices, rows, -1)
            return x.reshape(docs // rows, rows, cuts, -1).swapaxes(1, 2).reshape(devices, rows, -1)

        def by_document(x):
            if cuts == 1:
                return x.reshape(docs, -1)
            return x.reshape(docs // rows, cuts, rows, -1).swapaxes(1, 2).reshape(docs, -1)

        def exchange(x):
            return lax.all_to_all(x, AXES, 0, 0)

        def exchange_halves(x):
            groups = [list(range(first, devices, 2)) for first in (0, 1)]
            return lax.all_to_all(x, AXES, 0, 0, axis_index_groups=groups)

        def to_partner(x):
            return lax.ppermute(x, AXES, [(i, i ^ 1) for i in range(devices)])

        def to_all(x):
            return exchange(jnp.broadcast_to(x[None], (devices,) + x.shape))

        shape = jax.ShapeDtypeStruct
        place = lax.axis_index(AXES)
        count_row = label_count[None, :]

        offset, parity = (place * labels)[None], (place & 1)[None]
        offset, parity = lax.optimization_barrier((offset, parity))
        half = (devices // 2, rows, hidden_width)
        partial_value, send = kernel(
            first_kernel,
            "first",
            [SMEM] + [HBM] * 2,
            [shape(half if paired else (docs, hidden_width), F32), shape(half if paired else (8, LANES), F32)],
            grant=FIRST_GRANT,
            scratch_shapes=[
                pltpu.VMEM((docs, feats), BF16),
                pltpu.VMEM((feats, hidden_width), BF16),
                pltpu.SemaphoreType.DMA((2,)),
            ],
        )(parity, features, w_first)
        if paired:
            sums = exchange_halves(partial_value + to_partner(send))
        else:
            sums = exchange(by_owner(partial_value))
        own_hidden = jnp.tanh(jnp.sum(sums, axis=0)).astype(BF16)
        hidden = by_document(to_all(own_hidden))

        packed_width = 2 * hidden_width + LANES
        if paired:
            half = (devices // 2, rows, packed_width)
            packed_shapes = [shape(half, BF16), shape(half, F32)]
        else:
            packed_shapes = [shape((docs, packed_width), BF16)]
        powers, local_max, hidden_turned, words, packed, *keep = kernel(
            softmax_kernel,
            "softmax",
            [SMEM] * 2 + [VMEM] * 4,
            [
                shape((docs, labels), F32),
                shape((docs, 1), F32),
                shape((hidden_width, docs), BF16),
                shape((docs, word_lanes(labels)), jnp.int32),
            ]
            + packed_shapes,
        )(offset, parity, label_ids.T, count_row, hidden, w_label)
        if paired:
            packed = kernel(pair_kernel, "pair", [SMEM] + [VMEM] * 2, shape(half, BF16))(
                parity, keep[0], to_partner(packed)
            )
            back, lse, loss = kernel(
                combine_kernel,
                "combine",
                [SMEM] + [VMEM] * 3,
                [
                    shape((devices, rows, width // 2), BF16),
                    shape((docs // LANES, LANES), F32),
                    shape((1, LANES), F32),
                ],
            )(place[None], exchange_halves(packed), own_hidden, count_row)
            own_inner = by_document(exchange(back))
            grad_inner = [own_inner, to_partner(own_inner)]
        else:
            stats = packed[: stats_rows(docs), 2 * hidden_width :]
            halves = by_owner(packed[:, : 2 * hidden_width].reshape(docs, 2, cuts, width).swapaxes(1, 2))
            flat = jnp.broadcast_to(stats.reshape(1, 1, -1), (devices, 1, stats.size))
            got = exchange(jnp.concatenate([halves.reshape(devices, 1, -1), flat], axis=-1))
            halves = got[:, 0, : -stats.size].reshape(devices, rows, 2, width)
            stats = got[:, 0, -stats.size :].reshape((devices,) + stats.shape)
            first_row = (place // cuts) * rows
            own_count = lax.dynamic_slice_in_dim(label_count, first_row, rows)[:, None].astype(F32)
            grad_inner, lse, loss = combine(
                halves[:, :, 0], halves[:, :, 1], stats, own_hidden, own_count, first_row, docs
            )
            loss = jnp.broadcast_to(loss, (1, LANES))
            grad_inner = [by_document(to_all(grad_inner))]

        grad_label = kernel(
            label_kernel, "label", [VMEM] * 6, shape((hidden_width, labels), BF16)
        )(hidden_turned, lse, powers, local_max, words, count_row)
        grad_first, grad_label, mean_loss = kernel(
            last_kernel,
            "last",
            [SMEM] + [VMEM] * (3 + len(grad_inner)),
            [
                shape((feats, hidden_width), BF16),
                shape((hidden_width, labels), BF16),
                shape((1, LANES), F32),
            ],
            out_specs=[HBM] * 3,
            scratch_shapes=[pltpu.VMEM((feats, hidden_width), BF16), pltpu.SemaphoreType.DMA((3,))],
        )(parity, features, grad_label, loss, *grad_inner)
        return (grad_first, grad_label, mean_loss[0, 0])

    return per_device


def kernel(body, name, in_specs, out_shape, grant=GRANT, **more):
    several = isinstance(out_shape, list)
    specs = {"out_specs": [VMEM] * len(out_shape) if several else VMEM}
    return pl.pallas_call(
        body,
        name=name,
        in_specs=in_specs,
        out_shape=out_shape,
        compiler_params=pltpu.CompilerParams(vmem_limit_bytes=grant),
        **(specs | more),
    )


def solution(mesh):
    placed = (P(None, AXES), P(AXES, None), P(None, AXES), P(), P())
    devices = mesh.shape["gx"] * mesh.shape["gy"]
    return jax.shard_map(
        make_per_device(devices),
        mesh=mesh,
        in_specs=placed,
        out_specs=(P(AXES, None), P(None, AXES), P()),
        check_vma=False,
    )
```

```python
import jax
import jax.numpy as jnp
from jax import lax
from jax.experimental import pallas as pl
from jax.experimental.pallas import tpu as pltpu
from jax.sharding import PartitionSpec as P

AXES = ("gx", "gy")
LANES, LANE_BITS = 128, 7
WORD = 31
GRANT = 12 * 1024 * 1024
FIRST_GRANT = 56164352
VMEM = pl.BlockSpec(memory_space=pltpu.VMEM)
HBM = pl.BlockSpec(memory_space=pltpu.HBM)
SMEM = pl.BlockSpec(memory_space=pltpu.SMEM)
F32, BF16 = jnp.float32, jnp.bfloat16


def chunks_of(length):
    size = next((s for s in (256, 128) if length % s == 0), length)
    return [slice(at, at + size) for at in range(0, length, size)]


def dot(a, b, dims):
    return lax.dot_general(a, b, (dims, ((), ())), preferred_element_type=F32)


def lane(shape):
    return lax.broadcasted_iota(jnp.int32, shape, len(shape) - 1)


def split3(x):
    high = lax.reduce_precision(x, 8, 7)
    rest = x - high
    middle = lax.reduce_precision(rest, 8, 7)
    return high, middle, rest - middle


def into_lanes(columns, shape):
    at = lane(shape)
    block = jnp.zeros(shape, F32)
    for index, column in enumerate(columns):
        block = jnp.where(at == index, column, block)
    return block


def column_of(row):
    return jnp.broadcast_to(row, (8, row.shape[1])).T[:, :1]


def row_of(column):
    return jnp.broadcast_to(column, (column.shape[0], 8)).T[:1]


def stats_rows(docs):
    return pl.cdiv(3 * docs // LANES + 1, 8) * 8


def stats_block(lse, scalar):
    docs = lse.shape[1]
    rows = [part[:, at : at + LANES] for part in split3(lse) for at in range(0, docs, LANES)]
    rows.append(into_lanes(split3(scalar), (1, LANES)))
    rows += [jnp.zeros((1, LANES), F32)] * (stats_rows(docs) - len(rows))
    return jnp.concatenate(rows, axis=0)


def match_words(ids_ref, count_ref, offset_ref, labels):
    slots, docs = ids_ref.shape
    ids = ids_ref[...] - offset_ref[0]
    in_count = lax.broadcasted_iota(jnp.int32, ids.shape, 0) < count_ref[...]
    used = in_count & (ids >= 0) & (ids < labels)
    words = []
    for index in range(word_lanes(labels) // LANES):
        bit = (ids >> LANE_BITS) - WORD * index
        bit = jnp.where(used & (bit >= 0) & (bit < WORD), bit, WORD)
        places = (bit * LANES + (ids & (LANES - 1))).T
        word = jnp.zeros((docs, LANES), jnp.int32)
        for slot in range(slots):
            here = jnp.broadcast_to(places[:, slot : slot + 1], (docs, LANES))
            hit = (here & (LANES - 1)) == lane((docs, LANES))
            word = word | jnp.where(hit, 1 << (here >> LANE_BITS), 0)
        words.append(word)
    return jnp.concatenate(words, axis=1)


def word_lanes(labels):
    return LANES * pl.cdiv(labels, LANES * WORD)


def first_kernel(
    parity_ref, features_hbm, w_first_hbm, partial_ref, send_ref, features_ref, w_first_ref, sems
):
    moves = [
        pltpu.make_async_copy(features_hbm, features_ref, sems.at[0]),
        pltpu.make_async_copy(w_first_hbm, w_first_ref, sems.at[1]),
    ]
    for move in moves:
        move.start()
    for move in moves:
        move.wait()
    total = dot(features_ref[...], w_first_ref[...], ((1,), (0,)))
    if partial_ref.shape == total.shape:
        partial_ref[...] = total
        return
    partial_ref[...], send_ref[...] = halves_of(total, parity_ref[0], send_ref.shape[1])


def hits(words_ref, piece, yes, no):
    blocks = []
    for first in range(piece.start, piece.stop, LANES):
        word_index, bit = divmod(first // LANES, WORD)
        word = words_ref[:, LANES * word_index : LANES * (word_index + 1)]
        blocks.append(jnp.where((word & (1 << bit)) != 0, yes, no))
    return jnp.concatenate(blocks, axis=1)


def halves_of(value, parity, rows):
    split = value.reshape(-1, 2, rows, value.shape[1])
    even, odd = split[:, 0], split[:, 1]
    return jnp.where(parity == 0, even, odd), jnp.where(parity == 0, odd, even)


def softmax_kernel(
    offset_ref, parity_ref, ids_ref, count_ref, hidden_ref, w_label_ref,
    powers_ref, max_ref, words_ref, packed_ref, *keep_refs,
):
    docs, width = hidden_ref.shape
    pieces = chunks_of(w_label_ref.shape[1])
    hidden = hidden_ref[...]
    words_ref[...] = match_words(ids_ref, count_ref, offset_ref, w_label_ref.shape[1])
    top = None
    for piece in pieces:
        logits = dot(hidden, w_label_ref[:, piece], ((1,), (0,)))
        powers_ref[:, piece] = logits
        top = logits if top is None else jnp.maximum(top, logits)
    local_max = jnp.max(top, axis=1, keepdims=True)
    paired = bool(keep_refs)
    total, sums = None, None
    for piece in pieces:
        powers = jnp.exp(powers_ref[:, piece] - local_max)
        powers_ref[:, piece] = powers
        total = powers if total is None else total + powers
        if paired:
            _, powers = halves_of(powers, parity_ref[0], packed_ref.shape[1])
            powers = powers.reshape(-1, powers.shape[-1])
        both = [powers.astype(BF16), hits(words_ref, piece, 1.0, 0.0).astype(BF16)]
        part = dot(jnp.concatenate(both, axis=0), w_label_ref[:, piece], ((1,), (1,)))
        sums = part if sums is None else sums + part
    local_sum = jnp.sum(total, axis=1, keepdims=True)
    max_ref[...] = local_max
    matched = sums[-docs:]
    expected = sums[:-docs]
    picked = jnp.sum(hidden.astype(F32) * matched, axis=1, keepdims=True)
    picked = jnp.sum(picked / column_of(count_ref[...].astype(F32)), axis=0, keepdims=True)
    stats = stats_block(row_of(local_max + jnp.log(local_sum)), picked)
    if not paired:
        packed_ref[:, :width] = (expected / local_sum).astype(BF16)
        packed_ref[:, width : 2 * width] = matched.astype(BF16)
        for first in range(0, docs, stats.shape[0]):
            packed_ref[first : first + stats.shape[0], 2 * width :] = stats.astype(BF16)
        return
    keep_ref, sum_ref = keep_refs
    rows = packed_ref.shape[1]
    sum_ref[...], other_sum = halves_of(local_sum, parity_ref[0], rows)
    keep_ref[:, :, :width], other = halves_of(matched, parity_ref[0], rows)
    packed_ref[:, :, :width] = (expected.reshape(-1, rows, width) / other_sum).astype(BF16)
    packed_ref[:, :, width : 2 * width] = other.astype(BF16)
    wide = jnp.broadcast_to(stats[None], (keep_ref.shape[0],) + stats.shape)
    keep_ref[:, :, width:] = wide
    packed_ref[:, :, 2 * width :] = wide.astype(BF16)


def own_kernel(parity_ref, hidden_ref, features_ref, powers_ref, sum_ref, w_label_ref, *refs):
    expected_ref, hidden_turned_ref, features_turned_ref = refs
    half, rows, width = expected_ref.shape
    total = None
    for piece in chunks_of(w_label_ref.shape[1]):
        powers, _ = halves_of(powers_ref[:, piece], parity_ref[0], rows)
        powers = powers.reshape(half * rows, -1).astype(BF16)
        part = dot(powers, w_label_ref[:, piece], ((1,), (1,)))
        total = part if total is None else total + part
    expected_ref[...] = total.reshape(half, rows, width) / sum_ref[...]
    turn_kernel(hidden_ref, features_ref, hidden_turned_ref, features_turned_ref)


def read_stats(block, docs):
    part = docs // LANES
    lse = sum(block[..., i * part : (i + 1) * part, :] for i in range(3))
    return lse, block[..., 3 * part : 3 * part + 1, :]


def pair_kernel(parity_ref, expected_ref, keep_ref, got_ref, packed_ref):
    half, rows, width = expected_ref.shape
    docs = 2 * half * rows
    own_lse, own_scalar = read_stats(keep_ref[0, :, width:], docs)
    got_lse, got_scalar = read_stats(got_ref[0, :, 2 * width :].astype(F32), docs)
    top = jnp.maximum(own_lse, got_lse)
    lse = top + jnp.log(jnp.exp(own_lse - top) + jnp.exp(got_lse - top))
    expected = 0.0
    for part_lse, ref in ((own_lse, expected_ref), (got_lse, got_ref)):
        share = column_of(flat_row(jnp.exp(part_lse - lse)))
        share, _ = halves_of(share, parity_ref[0], rows)
        expected = expected + share * ref[:, :, :width].astype(F32)
    packed_ref[:, :, :width] = expected.astype(BF16)
    matched = keep_ref[:, :, :width] + got_ref[:, :, width : 2 * width].astype(F32)
    packed_ref[:, :, width : 2 * width] = matched.astype(BF16)
    scalar = jnp.sum(own_scalar + got_scalar, axis=1, keepdims=True)
    stats = stats_block(flat_row(lse), scalar).astype(BF16)
    packed_ref[:, :, 2 * width :] = jnp.broadcast_to(stats[None], (half,) + stats.shape)


def flat_row(rows):
    return jnp.concatenate([rows[i : i + 1] for i in range(rows.shape[0])], axis=1)


def combine(expected, matched, stats, own_hidden, own_count, first_row, docs):
    rows = own_hidden.shape[0]
    part = docs // LANES
    lse_parts, picked = read_stats(stats.astype(F32), docs)
    top = jnp.max(lse_parts, axis=0)
    lse = top + jnp.log(jnp.sum(jnp.exp(lse_parts - top), axis=0))
    picked = jnp.sum(picked, axis=0)
    loss = jnp.sum(jnp.sum(lse, axis=0, keepdims=True) - picked, axis=1, keepdims=True) / docs
    shares = jnp.exp(lse_parts - lse)
    own = lane((rows, LANES)) - lax.broadcasted_iota(jnp.int32, (rows, LANES), 0) - first_row
    share = 0.0
    for index in range(part):
        share = share + jnp.where(own + LANES * index == 0, shares[:, index : index + 1], 0.0)
    share = jnp.sum(share, axis=-1, keepdims=True)
    mean_matched = jnp.sum(matched.astype(F32), axis=0) / own_count
    grad_hidden = jnp.sum(share * expected.astype(F32), axis=0) - mean_matched
    hidden = own_hidden.astype(F32)
    grad_inner = (grad_hidden * (1.0 - hidden * hidden)).astype(BF16)
    return grad_inner, lse, loss


def combine_kernel(place_ref, got_ref, own_hidden_ref, count_ref, back_ref, lse_ref, loss_ref):
    rows, width = own_hidden_ref.shape
    docs = count_ref.shape[1]
    first_row = place_ref[0] * rows
    owner = lax.broadcasted_iota(jnp.int32, (rows, docs), 0) + first_row
    counts = jnp.where(lane((rows, docs)) == owner, count_ref[...], 0)
    own_count = jnp.sum(counts.astype(F32), axis=1, keepdims=True)
    grad_inner, lse_ref[...], loss = combine(
        got_ref[:, :, :width], got_ref[:, :, width : 2 * width], got_ref[:, :, 2 * width :],
        own_hidden_ref[...], own_count, first_row, docs,
    )
    loss_ref[...] = jnp.broadcast_to(loss, loss_ref.shape)
    half = width // 2
    for parity in (0, 1):
        part = grad_inner[:, parity * half : (parity + 1) * half]
        for index in range(parity, back_ref.shape[0], 2):
            back_ref[index] = part


def turn_kernel(hidden_ref, features_ref, hidden_turned_ref, features_turned_ref):
    hidden_turned_ref[...] = hidden_ref[...].T
    features_turned_ref[...] = features_ref[...].T


def label_kernel(hidden_ref, lse_ref, powers_ref, max_ref, words_ref, count_ref, grad_label_ref):
    scale = jnp.exp(max_ref[...] - column_of(flat_row(lse_ref[...])))
    per_match = column_of(1.0 / count_ref[...].astype(F32))
    hidden = hidden_ref[...]
    for piece in chunks_of(powers_ref.shape[1]):
        grad_logits = powers_ref[:, piece] * scale - hits(words_ref, piece, per_match, 0.0)
        grad_label_ref[:, piece] = dot(hidden, grad_logits.astype(BF16), ((1,), (0,))).astype(BF16)


def last_kernel(
    parity_ref, features_ref, label_ref, loss_ref, *refs,
):
    *grad_inner_refs, grad_first_hbm, grad_label_hbm, loss_hbm, first_scratch, sems = refs
    copies = [
        pltpu.make_async_copy(label_ref, grad_label_hbm, sems.at[0]),
        pltpu.make_async_copy(loss_ref, loss_hbm, sems.at[1]),
        pltpu.make_async_copy(first_scratch, grad_first_hbm, sems.at[2]),
    ]
    copies[0].start()
    copies[1].start()
    if len(grad_inner_refs) == 1:
        grad_inner = grad_inner_refs[0][...]
    else:
        own, other = (ref[...].astype(F32) for ref in grad_inner_refs)
        even = parity_ref[0] == 0
        both = [jnp.where(even, own, other), jnp.where(even, other, own)]
        grad_inner = jnp.concatenate(both, axis=1).astype(BF16)
    first_scratch[...] = dot(features_ref[...], grad_inner, ((1,), (0,))).astype(BF16)
    copies[2].start()
    for copy in copies:
        copy.wait()


def make_per_device(devices):
    def per_device(features, w_first, w_label, label_ids, label_count):
        docs, hidden_width = features.shape[0], w_first.shape[1]
        feats, labels = features.shape[1], w_label.shape[1]
        rows = max(1, docs // devices)
        cuts = devices * rows // docs
        width = hidden_width // cuts
        paired = cuts == 1 and rows == stats_rows(docs) and width % (2 * LANES) == 0

        def by_owner(x):
            if cuts == 1:
                return x.reshape(devices, rows, -1)
            return x.reshape(docs // rows, rows, cuts, -1).swapaxes(1, 2).reshape(devices, rows, -1)

        def by_document(x):
            if cuts == 1:
                return x.reshape(docs, -1)
            return x.reshape(docs // rows, cuts, rows, -1).swapaxes(1, 2).reshape(docs, -1)

        def exchange(x):
            return lax.all_to_all(x, AXES, 0, 0)

        def exchange_halves(x):
            groups = [list(range(first, devices, 2)) for first in (0, 1)]
            return lax.all_to_all(x, AXES, 0, 0, axis_index_groups=groups)

        def to_partner(x):
            return lax.ppermute(x, AXES, [(i, i ^ 1) for i in range(devices)])

        def to_all(x):
            return exchange(jnp.broadcast_to(x[None], (devices,) + x.shape))

        shape = jax.ShapeDtypeStruct
        place = lax.axis_index(AXES)
        count_row = label_count[None, :]

        offset, parity = (place * labels)[None], (place & 1)[None]
        offset, parity = lax.optimization_barrier((offset, parity))
        half = (devices // 2, rows, hidden_width)
        partial_value, send = kernel(
            first_kernel,
            "first",
            [SMEM] + [HBM] * 2,
            [shape(half if paired else (docs, hidden_width), F32), shape(half if paired else (8, LANES), F32)],
            grant=FIRST_GRANT,
            scratch_shapes=[
                pltpu.VMEM((docs, feats), BF16),
                pltpu.VMEM((feats, hidden_width), BF16),
                pltpu.SemaphoreType.DMA((2,)),
            ],
        )(parity, features, w_first)
        if paired:
            sums = exchange_halves(partial_value + to_partner(send))
        else:
            sums = exchange(by_owner(partial_value))
        own_hidden = jnp.tanh(jnp.sum(sums, axis=0)).astype(BF16)
        hidden = by_document(to_all(own_hidden))

        packed_width = 2 * hidden_width + LANES
        if paired:
            half = (devices // 2, rows, packed_width)
            packed_shapes = [
                shape(half, BF16),
                shape((devices // 2, rows, hidden_width + LANES), F32),
                shape((devices // 2, rows, 1), F32),
            ]
        else:
            packed_shapes = [shape((docs, packed_width), BF16)]
        powers, local_max, words, packed, *keep = kernel(
            softmax_kernel,
            "softmax",
            [SMEM] * 2 + [VMEM] * 4,
            [
                shape((docs, labels), F32),
                shape((docs, 1), F32),
                shape((docs, word_lanes(labels)), jnp.int32),
            ]
            + packed_shapes,
        )(offset, parity, label_ids.T, count_row, hidden, w_label)
        turned = [shape((hidden_width, docs), BF16), shape((feats, docs), BF16)]
        if paired:
            keep, own_sum = keep
            got = to_partner(packed)
            expected, *turned = kernel(
                own_kernel,
                "own",
                [SMEM] + [VMEM] * 5,
                [shape((devices // 2, rows, hidden_width), F32)] + turned,
            )(parity, hidden, features, powers, own_sum, w_label)
            got, expected, turned = lax.optimization_barrier((got, expected, turned))
            packed = kernel(pair_kernel, "pair", [SMEM] + [VMEM] * 3, shape(half, BF16))(
                parity, expected, keep, got
            )
            back, lse, loss = kernel(
                combine_kernel,
                "combine",
                [SMEM] + [VMEM] * 3,
                [
                    shape((devices, rows, width // 2), BF16),
                    shape((docs // LANES, LANES), F32),
                    shape((1, LANES), F32),
                ],
            )(place[None], exchange_halves(packed), own_hidden, count_row)
            own_inner = by_document(exchange(back))
            grad_inner = [own_inner, to_partner(own_inner)]
        else:
            turned = kernel(turn_kernel, "turn", [VMEM] * 2, turned)(hidden, features)
            stats = packed[: stats_rows(docs), 2 * hidden_width :]
            halves = by_owner(packed[:, : 2 * hidden_width].reshape(docs, 2, cuts, width).swapaxes(1, 2))
            flat = jnp.broadcast_to(stats.reshape(1, 1, -1), (devices, 1, stats.size))
            got = exchange(jnp.concatenate([halves.reshape(devices, 1, -1), flat], axis=-1))
            halves = got[:, 0, : -stats.size].reshape(devices, rows, 2, width)
            stats = got[:, 0, -stats.size :].reshape((devices,) + stats.shape)
            first_row = (place // cuts) * rows
            own_count = lax.dynamic_slice_in_dim(label_count, first_row, rows)[:, None].astype(F32)
            grad_inner, lse, loss = combine(
                halves[:, :, 0], halves[:, :, 1], stats, own_hidden, own_count, first_row, docs
            )
            loss = jnp.broadcast_to(loss, (1, LANES))
            grad_inner = [by_document(to_all(grad_inner))]

        hidden_turned, features_turned = turned
        grad_label = kernel(
            label_kernel, "label", [VMEM] * 6, shape((hidden_width, labels), BF16)
        )(hidden_turned, lse, powers, local_max, words, count_row)
        grad_first, grad_label, mean_loss = kernel(
            last_kernel,
            "last",
            [SMEM] + [VMEM] * (3 + len(grad_inner)),
            [
                shape((feats, hidden_width), BF16),
                shape((hidden_width, labels), BF16),
                shape((1, LANES), F32),
            ],
            out_specs=[HBM] * 3,
            scratch_shapes=[pltpu.VMEM((feats, hidden_width), BF16), pltpu.SemaphoreType.DMA((3,))],
        )(parity, features_turned, grad_label, loss, *grad_inner)
        return (grad_first, grad_label, mean_loss[0, 0])

    return per_device


def kernel(body, name, in_specs, out_shape, grant=GRANT, **more):
    several = isinstance(out_shape, list)
    specs = {"out_specs": [VMEM] * len(out_shape) if several else VMEM}
    return pl.pallas_call(
        body,
        name=name,
        in_specs=in_specs,
        out_shape=out_shape,
        compiler_params=pltpu.CompilerParams(vmem_limit_bytes=grant),
        **(specs | more),
    )


def solution(mesh):
    placed = (P(None, AXES), P(AXES, None), P(None, AXES), P(), P())
    devices = mesh.shape["gx"] * mesh.shape["gy"]
    return jax.shard_map(
        make_per_device(devices),
        mesh=mesh,
        in_specs=placed,
        out_specs=(P(AXES, None), P(None, AXES), P()),
        check_vma=False,
    )
```

```python
import jax
import jax.numpy as jnp
from jax import lax
from jax.experimental import pallas as pl
from jax.experimental.pallas import tpu as pltpu
from jax.sharding import PartitionSpec as P

AXES = ("gx", "gy")
LANES, LANE_BITS = 128, 7
WORD = 31
GRANT = 12 * 1024 * 1024
FIRST_GRANT = 56164352
VMEM = pl.BlockSpec(memory_space=pltpu.VMEM)
HBM = pl.BlockSpec(memory_space=pltpu.HBM)
SMEM = pl.BlockSpec(memory_space=pltpu.SMEM)
F32, BF16 = jnp.float32, jnp.bfloat16


def chunks_of(length):
    size = next((s for s in (256, 128) if length % s == 0), length)
    return [slice(at, at + size) for at in range(0, length, size)]


def dot(a, b, dims):
    return lax.dot_general(a, b, (dims, ((), ())), preferred_element_type=F32)


def lane(shape):
    return lax.broadcasted_iota(jnp.int32, shape, len(shape) - 1)


def split3(x):
    high = lax.reduce_precision(x, 8, 7)
    rest = x - high
    middle = lax.reduce_precision(rest, 8, 7)
    return high, middle, rest - middle


def into_lanes(columns, shape):
    at = lane(shape)
    block = jnp.zeros(shape, F32)
    for index, column in enumerate(columns):
        block = jnp.where(at == index, column, block)
    return block


def column_of(row):
    return jnp.broadcast_to(row, (8, row.shape[1])).T[:, :1]


def row_of(column):
    return jnp.broadcast_to(column, (column.shape[0], 8)).T[:1]


def stats_rows(docs):
    return pl.cdiv(3 * docs // LANES + 1, 8) * 8


def stats_block(lse, scalar):
    docs = lse.shape[1]
    rows = [part[:, at : at + LANES] for part in split3(lse) for at in range(0, docs, LANES)]
    rows.append(into_lanes(split3(scalar), (1, LANES)))
    rows += [jnp.zeros((1, LANES), F32)] * (stats_rows(docs) - len(rows))
    return jnp.concatenate(rows, axis=0)


def match_words(ids_ref, count_ref, offset_ref, labels):
    slots, docs = ids_ref.shape
    ids = ids_ref[...] - offset_ref[0]
    in_count = lax.broadcasted_iota(jnp.int32, ids.shape, 0) < count_ref[...]
    used = in_count & (ids >= 0) & (ids < labels)
    words = []
    for index in range(word_lanes(labels) // LANES):
        bit = (ids >> LANE_BITS) - WORD * index
        bit = jnp.where(used & (bit >= 0) & (bit < WORD), bit, WORD)
        places = (bit * LANES + (ids & (LANES - 1))).T
        word = jnp.zeros((docs, LANES), jnp.int32)
        for slot in range(slots):
            here = jnp.broadcast_to(places[:, slot : slot + 1], (docs, LANES))
            hit = (here & (LANES - 1)) == lane((docs, LANES))
            word = word | jnp.where(hit, 1 << (here >> LANE_BITS), 0)
        words.append(word)
    return jnp.concatenate(words, axis=1)


def word_lanes(labels):
    return LANES * pl.cdiv(labels, LANES * WORD)


def first_kernel(
    parity_ref, features_hbm, w_first_hbm, partial_ref, send_ref, features_ref, w_first_ref, sems
):
    moves = [
        pltpu.make_async_copy(features_hbm, features_ref, sems.at[0]),
        pltpu.make_async_copy(w_first_hbm, w_first_ref, sems.at[1]),
    ]
    for move in moves:
        move.start()
    for move in moves:
        move.wait()
    total = dot(features_ref[...], w_first_ref[...], ((1,), (0,)))
    if partial_ref.shape == total.shape:
        partial_ref[...] = total
        return
    partial_ref[...], send_ref[...] = halves_of(total, parity_ref[0], send_ref.shape[1])


def hits(words_ref, piece, yes, no):
    blocks = []
    for first in range(piece.start, piece.stop, LANES):
        word_index, bit = divmod(first // LANES, WORD)
        word = words_ref[:, LANES * word_index : LANES * (word_index + 1)]
        blocks.append(jnp.where((word & (1 << bit)) != 0, yes, no))
    return jnp.concatenate(blocks, axis=1)


def halves_of(value, parity, rows):
    split = value.reshape(-1, 2, rows, value.shape[1])
    even, odd = split[:, 0], split[:, 1]
    return jnp.where(parity == 0, even, odd), jnp.where(parity == 0, odd, even)


def softmax_kernel(
    offset_ref, parity_ref, ids_ref, count_ref, hidden_ref, w_label_ref,
    powers_ref, max_ref, words_ref, packed_ref, *keep_refs,
):
    docs, width = hidden_ref.shape
    pieces = chunks_of(w_label_ref.shape[1])
    hidden = hidden_ref[...]
    words_ref[...] = match_words(ids_ref, count_ref, offset_ref, w_label_ref.shape[1])
    top = None
    for piece in pieces:
        logits = dot(hidden, w_label_ref[:, piece], ((1,), (0,)))
        powers_ref[:, piece] = logits
        top = logits if top is None else jnp.maximum(top, logits)
    local_max = jnp.max(top, axis=1, keepdims=True)
    paired = bool(keep_refs)
    total, sums = None, None
    for piece in pieces:
        powers = jnp.exp(powers_ref[:, piece] - local_max)
        powers_ref[:, piece] = powers
        total = powers if total is None else total + powers
        if paired:
            _, powers = halves_of(powers, parity_ref[0], packed_ref.shape[1])
            powers = powers.reshape(-1, powers.shape[-1])
        both = [powers.astype(BF16), hits(words_ref, piece, 1.0, 0.0).astype(BF16)]
        part = dot(jnp.concatenate(both, axis=0), w_label_ref[:, piece], ((1,), (1,)))
        sums = part if sums is None else sums + part
    local_sum = jnp.sum(total, axis=1, keepdims=True)
    max_ref[...] = local_max
    matched = sums[-docs:]
    expected = sums[:-docs]
    picked = jnp.sum(hidden.astype(F32) * matched, axis=1, keepdims=True)
    picked = jnp.sum(picked / column_of(count_ref[...].astype(F32)), axis=0, keepdims=True)
    stats = stats_block(row_of(local_max + jnp.log(local_sum)), picked)
    if not paired:
        packed_ref[:, :width] = (expected / local_sum).astype(BF16)
        packed_ref[:, width : 2 * width] = matched.astype(BF16)
        for first in range(0, docs, stats.shape[0]):
            packed_ref[first : first + stats.shape[0], 2 * width :] = stats.astype(BF16)
        return
    keep_ref, sum_ref = keep_refs
    rows = packed_ref.shape[1]
    sum_ref[...], other_sum = halves_of(local_sum, parity_ref[0], rows)
    keep_ref[:, :, :width], other = halves_of(matched, parity_ref[0], rows)
    packed_ref[:, :, :width] = (expected.reshape(-1, rows, width) / other_sum).astype(BF16)
    packed_ref[:, :, width : 2 * width] = other.astype(BF16)
    wide = jnp.broadcast_to(stats[None], (keep_ref.shape[0],) + stats.shape)
    keep_ref[:, :, width:] = wide
    packed_ref[:, :, 2 * width :] = wide.astype(BF16)


def own_kernel(parity_ref, hidden_ref, features_ref, powers_ref, sum_ref, w_label_ref, *refs):
    expected_ref, hidden_turned_ref, features_turned_ref = refs
    half, rows, width = expected_ref.shape
    total = None
    for piece in chunks_of(w_label_ref.shape[1]):
        powers, _ = halves_of(powers_ref[:, piece], parity_ref[0], rows)
        powers = powers.reshape(half * rows, -1).astype(BF16)
        part = dot(powers, w_label_ref[:, piece], ((1,), (1,)))
        total = part if total is None else total + part
    expected_ref[...] = total.reshape(half, rows, width) / sum_ref[...]
    turn_kernel(hidden_ref, features_ref, hidden_turned_ref, features_turned_ref)


def read_stats(block, docs):
    part = docs // LANES
    lse = sum(block[..., i * part : (i + 1) * part, :] for i in range(3))
    return lse, block[..., 3 * part : 3 * part + 1, :]


def pair_kernel(parity_ref, expected_ref, keep_ref, got_ref, packed_ref):
    half, rows, width = expected_ref.shape
    docs = 2 * half * rows
    own_lse, own_scalar = read_stats(keep_ref[0, :, width:], docs)
    got_lse, got_scalar = read_stats(got_ref[0, :, 2 * width :].astype(F32), docs)
    top = jnp.maximum(own_lse, got_lse)
    lse = top + jnp.log(jnp.exp(own_lse - top) + jnp.exp(got_lse - top))
    expected = 0.0
    shares = [flat_row(jnp.exp(part_lse - lse)) for part_lse in (own_lse, got_lse)]
    columns = jnp.concatenate(shares * 4, axis=0).T
    columns, _ = halves_of(columns, parity_ref[0], rows)
    for index, ref in enumerate((expected_ref, got_ref)):
        expected = expected + columns[:, :, index : index + 1] * ref[:, :, :width].astype(F32)
    packed_ref[:, :, :width] = expected.astype(BF16)
    matched = keep_ref[:, :, :width] + got_ref[:, :, width : 2 * width].astype(F32)
    packed_ref[:, :, width : 2 * width] = matched.astype(BF16)
    scalar = jnp.sum(own_scalar + got_scalar, axis=1, keepdims=True)
    stats = stats_block(flat_row(lse), scalar).astype(BF16)
    packed_ref[:, :, 2 * width :] = jnp.broadcast_to(stats[None], (half,) + stats.shape)


def flat_row(rows):
    return jnp.concatenate([rows[i : i + 1] for i in range(rows.shape[0])], axis=1)


def combine(expected, matched, stats, own_hidden, own_count, first_row, docs):
    rows = own_hidden.shape[0]
    part = docs // LANES
    lse_parts, picked = read_stats(stats.astype(F32), docs)
    top = jnp.max(lse_parts, axis=0)
    lse = top + jnp.log(jnp.sum(jnp.exp(lse_parts - top), axis=0))
    picked = jnp.sum(picked, axis=0)
    loss = jnp.sum(jnp.sum(lse, axis=0, keepdims=True) - picked, axis=1, keepdims=True) / docs
    shares = jnp.exp(lse_parts - lse)
    own = lane((rows, LANES)) - lax.broadcasted_iota(jnp.int32, (rows, LANES), 0) - first_row
    share = 0.0
    for index in range(part):
        share = share + jnp.where(own + LANES * index == 0, shares[:, index : index + 1], 0.0)
    share = jnp.sum(share, axis=-1, keepdims=True)
    mean_matched = jnp.sum(matched.astype(F32), axis=0) / own_count
    grad_hidden = jnp.sum(share * expected.astype(F32), axis=0) - mean_matched
    hidden = own_hidden.astype(F32)
    grad_inner = (grad_hidden * (1.0 - hidden * hidden)).astype(BF16)
    return grad_inner, lse, loss


def combine_kernel(place_ref, got_ref, own_hidden_ref, count_ref, back_ref, lse_ref, loss_ref):
    rows, width = own_hidden_ref.shape
    docs = count_ref.shape[1]
    first_row = place_ref[0] * rows
    owner = lax.broadcasted_iota(jnp.int32, (rows, docs), 0) + first_row
    counts = jnp.where(lane((rows, docs)) == owner, count_ref[...], 0)
    own_count = jnp.sum(counts.astype(F32), axis=1, keepdims=True)
    grad_inner, lse_ref[...], loss = combine(
        got_ref[:, :, :width], got_ref[:, :, width : 2 * width], got_ref[:, :, 2 * width :],
        own_hidden_ref[...], own_count, first_row, docs,
    )
    loss_ref[...] = jnp.broadcast_to(loss, loss_ref.shape)
    half = width // 2
    for parity in (0, 1):
        part = grad_inner[:, parity * half : (parity + 1) * half]
        for index in range(parity, back_ref.shape[0], 2):
            back_ref[index] = part


def turn_kernel(hidden_ref, features_ref, hidden_turned_ref, features_turned_ref):
    hidden_turned_ref[...] = hidden_ref[...].T
    features_turned_ref[...] = features_ref[...].T


def label_kernel(hidden_ref, lse_ref, powers_ref, max_ref, words_ref, count_ref, grad_label_ref):
    scale = jnp.exp(max_ref[...] - column_of(flat_row(lse_ref[...])))
    per_match = column_of(1.0 / count_ref[...].astype(F32))
    hidden = hidden_ref[...]
    for piece in chunks_of(powers_ref.shape[1]):
        grad_logits = powers_ref[:, piece] * scale - hits(words_ref, piece, per_match, 0.0)
        grad_label_ref[:, piece] = dot(hidden, grad_logits.astype(BF16), ((1,), (0,))).astype(BF16)


def last_kernel(
    parity_ref, features_ref, label_ref, loss_ref, *refs,
):
    *grad_inner_refs, grad_first_hbm, grad_label_hbm, loss_hbm, first_scratch, sems = refs
    copies = [
        pltpu.make_async_copy(label_ref, grad_label_hbm, sems.at[0]),
        pltpu.make_async_copy(loss_ref, loss_hbm, sems.at[1]),
        pltpu.make_async_copy(first_scratch, grad_first_hbm, sems.at[2]),
    ]
    copies[0].start()
    copies[1].start()
    if len(grad_inner_refs) == 1:
        grad_inner = grad_inner_refs[0][...]
    else:
        own, other = (ref[...].astype(F32) for ref in grad_inner_refs)
        even = parity_ref[0] == 0
        both = [jnp.where(even, own, other), jnp.where(even, other, own)]
        grad_inner = jnp.concatenate(both, axis=1).astype(BF16)
    first_scratch[...] = dot(features_ref[...], grad_inner, ((1,), (0,))).astype(BF16)
    copies[2].start()
    for copy in copies:
        copy.wait()


def make_per_device(devices):
    def per_device(features, w_first, w_label, label_ids, label_count):
        docs, hidden_width = features.shape[0], w_first.shape[1]
        feats, labels = features.shape[1], w_label.shape[1]
        rows = max(1, docs // devices)
        cuts = devices * rows // docs
        width = hidden_width // cuts
        paired = cuts == 1 and rows == stats_rows(docs) and width % (2 * LANES) == 0

        def by_owner(x):
            if cuts == 1:
                return x.reshape(devices, rows, -1)
            return x.reshape(docs // rows, rows, cuts, -1).swapaxes(1, 2).reshape(devices, rows, -1)

        def by_document(x):
            if cuts == 1:
                return x.reshape(docs, -1)
            return x.reshape(docs // rows, cuts, rows, -1).swapaxes(1, 2).reshape(docs, -1)

        def exchange(x):
            return lax.all_to_all(x, AXES, 0, 0)

        def exchange_halves(x):
            groups = [list(range(first, devices, 2)) for first in (0, 1)]
            return lax.all_to_all(x, AXES, 0, 0, axis_index_groups=groups)

        def to_partner(x):
            return lax.ppermute(x, AXES, [(i, i ^ 1) for i in range(devices)])

        def to_all(x):
            return exchange(jnp.broadcast_to(x[None], (devices,) + x.shape))

        shape = jax.ShapeDtypeStruct
        place = lax.axis_index(AXES)
        count_row = label_count[None, :]

        offset, parity = (place * labels)[None], (place & 1)[None]
        offset, parity = lax.optimization_barrier((offset, parity))
        half = (devices // 2, rows, hidden_width)
        partial_value, send = kernel(
            first_kernel,
            "first",
            [SMEM] + [HBM] * 2,
            [shape(half if paired else (docs, hidden_width), F32), shape(half if paired else (8, LANES), F32)],
            grant=FIRST_GRANT,
            scratch_shapes=[
                pltpu.VMEM((docs, feats), BF16),
                pltpu.VMEM((feats, hidden_width), BF16),
                pltpu.SemaphoreType.DMA((2,)),
            ],
        )(parity, features, w_first)
        if paired:
            sums = exchange_halves(partial_value + to_partner(send))
        else:
            sums = exchange(by_owner(partial_value))
        own_hidden = jnp.tanh(jnp.sum(sums, axis=0)).astype(BF16)
        hidden = by_document(to_all(own_hidden))

        packed_width = 2 * hidden_width + LANES
        if paired:
            half = (devices // 2, rows, packed_width)
            packed_shapes = [
                shape(half, BF16),
                shape((devices // 2, rows, hidden_width + LANES), F32),
                shape((devices // 2, rows, 1), F32),
            ]
        else:
            packed_shapes = [shape((docs, packed_width), BF16)]
        powers, local_max, words, packed, *keep = kernel(
            softmax_kernel,
            "softmax",
            [SMEM] * 2 + [VMEM] * 4,
            [
                shape((docs, labels), F32),
                shape((docs, 1), F32),
                shape((docs, word_lanes(labels)), jnp.int32),
            ]
            + packed_shapes,
        )(offset, parity, label_ids.T, count_row, hidden, w_label)
        turned = [shape((hidden_width, docs), BF16), shape((feats, docs), BF16)]
        if paired:
            keep, own_sum = keep
            got = to_partner(packed)
            expected, *turned = kernel(
                own_kernel,
                "own",
                [SMEM] + [VMEM] * 5,
                [shape((devices // 2, rows, hidden_width), F32)] + turned,
            )(parity, hidden, features, powers, own_sum, w_label)
            got, expected, turned = lax.optimization_barrier((got, expected, turned))
            packed = kernel(pair_kernel, "pair", [SMEM] + [VMEM] * 3, shape(half, BF16))(
                parity, expected, keep, got
            )
            back, lse, loss = kernel(
                combine_kernel,
                "combine",
                [SMEM] + [VMEM] * 3,
                [
                    shape((devices, rows, width // 2), BF16),
                    shape((docs // LANES, LANES), F32),
                    shape((1, LANES), F32),
                ],
            )(place[None], exchange_halves(packed), own_hidden, count_row)
            own_inner = by_document(exchange(back))
            grad_inner = [own_inner, to_partner(own_inner)]
        else:
            turned = kernel(turn_kernel, "turn", [VMEM] * 2, turned)(hidden, features)
            stats = packed[: stats_rows(docs), 2 * hidden_width :]
            halves = by_owner(packed[:, : 2 * hidden_width].reshape(docs, 2, cuts, width).swapaxes(1, 2))
            flat = jnp.broadcast_to(stats.reshape(1, 1, -1), (devices, 1, stats.size))
            got = exchange(jnp.concatenate([halves.reshape(devices, 1, -1), flat], axis=-1))
            halves = got[:, 0, : -stats.size].reshape(devices, rows, 2, width)
            stats = got[:, 0, -stats.size :].reshape((devices,) + stats.shape)
            first_row = (place // cuts) * rows
            own_count = lax.dynamic_slice_in_dim(label_count, first_row, rows)[:, None].astype(F32)
            grad_inner, lse, loss = combine(
                halves[:, :, 0], halves[:, :, 1], stats, own_hidden, own_count, first_row, docs
            )
            loss = jnp.broadcast_to(loss, (1, LANES))
            grad_inner = [by_document(to_all(grad_inner))]

        hidden_turned, features_turned = turned
        grad_label = kernel(
            label_kernel, "label", [VMEM] * 6, shape((hidden_width, labels), BF16)
        )(hidden_turned, lse, powers, local_max, words, count_row)
        grad_first, grad_label, mean_loss = kernel(
            last_kernel,
            "last",
            [SMEM] + [VMEM] * (3 + len(grad_inner)),
            [
                shape((feats, hidden_width), BF16),
                shape((hidden_width, labels), BF16),
                shape((1, LANES), F32),
            ],
            out_specs=[HBM] * 3,
            scratch_shapes=[pltpu.VMEM((feats, hidden_width), BF16), pltpu.SemaphoreType.DMA((3,))],
        )(parity, features_turned, grad_label, loss, *grad_inner)
        return (grad_first, grad_label, mean_loss[0, 0])

    return per_device


def kernel(body, name, in_specs, out_shape, grant=GRANT, **more):
    several = isinstance(out_shape, list)
    specs = {"out_specs": [VMEM] * len(out_shape) if several else VMEM}
    return pl.pallas_call(
        body,
        name=name,
        in_specs=in_specs,
        out_shape=out_shape,
        compiler_params=pltpu.CompilerParams(vmem_limit_bytes=grant),
        **(specs | more),
    )


def solution(mesh):
    placed = (P(None, AXES), P(AXES, None), P(None, AXES), P(), P())
    devices = mesh.shape["gx"] * mesh.shape["gy"]
    return jax.shard_map(
        make_per_device(devices),
        mesh=mesh,
        in_specs=placed,
        out_specs=(P(AXES, None), P(None, AXES), P()),
        check_vma=False,
    )
```

```python
import jax
import jax.numpy as jnp
from jax import lax
from jax.experimental import pallas as pl
from jax.experimental.pallas import tpu as pltpu
from jax.sharding import PartitionSpec as P

AXES = ("gx", "gy")
LANES, LANE_BITS = 128, 7
WORD = 31
GRANT = 12 * 1024 * 1024
FIRST_GRANT = 56164352
VMEM = pl.BlockSpec(memory_space=pltpu.VMEM)
HBM = pl.BlockSpec(memory_space=pltpu.HBM)
SMEM = pl.BlockSpec(memory_space=pltpu.SMEM)
F32, BF16 = jnp.float32, jnp.bfloat16


def chunks_of(length):
    size = next((s for s in (256, 128) if length % s == 0), length)
    return [slice(at, at + size) for at in range(0, length, size)]


def dot(a, b, dims):
    return lax.dot_general(a, b, (dims, ((), ())), preferred_element_type=F32)


def lane(shape):
    return lax.broadcasted_iota(jnp.int32, shape, len(shape) - 1)


def split3(x):
    high = lax.reduce_precision(x, 8, 7)
    rest = x - high
    middle = lax.reduce_precision(rest, 8, 7)
    return high, middle, rest - middle


def into_lanes(columns, shape):
    at = lane(shape)
    block = jnp.zeros(shape, F32)
    for index, column in enumerate(columns):
        block = jnp.where(at == index, column, block)
    return block


def column_of(row):
    return jnp.broadcast_to(row, (8, row.shape[1])).T[:, :1]


def row_of(column):
    return jnp.broadcast_to(column, (column.shape[0], 8)).T[:1]


def stats_rows(docs):
    return pl.cdiv(3 * docs // LANES + 1, 8) * 8


def stats_block(lse, scalar):
    docs = lse.shape[1]
    rows = [part[:, at : at + LANES] for part in split3(lse) for at in range(0, docs, LANES)]
    rows.append(into_lanes(split3(scalar), (1, LANES)))
    rows += [jnp.zeros((1, LANES), F32)] * (stats_rows(docs) - len(rows))
    return jnp.concatenate(rows, axis=0)


def match_words(ids_ref, count_ref, offset_ref, labels):
    slots, docs = ids_ref.shape
    ids = ids_ref[...] - offset_ref[0]
    in_count = lax.broadcasted_iota(jnp.int32, ids.shape, 0) < count_ref[...]
    used = in_count & (ids >= 0) & (ids < labels)
    words = []
    for index in range(word_lanes(labels) // LANES):
        bit = (ids >> LANE_BITS) - WORD * index
        bit = jnp.where(used & (bit >= 0) & (bit < WORD), bit, WORD)
        places = (bit * LANES + (ids & (LANES - 1))).T
        word = jnp.zeros((docs, LANES), jnp.int32)
        for slot in range(slots):
            here = jnp.broadcast_to(places[:, slot : slot + 1], (docs, LANES))
            hit = (here & (LANES - 1)) == lane((docs, LANES))
            word = word | jnp.where(hit, 1 << (here >> LANE_BITS), 0)
        words.append(word)
    return jnp.concatenate(words, axis=1)


def word_lanes(labels):
    return LANES * pl.cdiv(labels, LANES * WORD)


def first_kernel(
    parity_ref, features_hbm, w_first_hbm, partial_ref, send_ref, features_ref, w_first_ref, sems
):
    moves = [
        pltpu.make_async_copy(w_first_hbm, w_first_ref, sems.at[0]),
        pltpu.make_async_copy(features_hbm, features_ref, sems.at[1]),
    ]
    for move in moves:
        move.start()
    for move in moves:
        move.wait()
    total = dot(features_ref[...], w_first_ref[...], ((1,), (0,)))
    if partial_ref.shape == total.shape:
        partial_ref[...] = total
        return
    partial_ref[...], send_ref[...] = halves_of(total, parity_ref[0], send_ref.shape[1])


def hits(words_ref, piece, yes, no):
    blocks = []
    for first in range(piece.start, piece.stop, LANES):
        word_index, bit = divmod(first // LANES, WORD)
        word = words_ref[:, LANES * word_index : LANES * (word_index + 1)]
        blocks.append(jnp.where((word & (1 << bit)) != 0, yes, no))
    return jnp.concatenate(blocks, axis=1)


def halves_of(value, parity, rows):
    split = value.reshape(-1, 2, rows, value.shape[1])
    even, odd = split[:, 0], split[:, 1]
    return jnp.where(parity == 0, even, odd), jnp.where(parity == 0, odd, even)


def softmax_kernel(
    offset_ref, parity_ref, ids_ref, count_ref, hidden_ref, w_label_ref,
    powers_ref, max_ref, words_ref, packed_ref, *keep_refs,
):
    docs, width = hidden_ref.shape
    pieces = chunks_of(w_label_ref.shape[1])
    hidden = hidden_ref[...]
    words_ref[...] = match_words(ids_ref, count_ref, offset_ref, w_label_ref.shape[1])
    top = None
    for piece in pieces:
        logits = dot(hidden, w_label_ref[:, piece], ((1,), (0,)))
        powers_ref[:, piece] = logits
        top = logits if top is None else jnp.maximum(top, logits)
    local_max = jnp.max(top, axis=1, keepdims=True)
    paired = bool(keep_refs)
    total, sums = None, None
    for piece in pieces:
        powers = jnp.exp(powers_ref[:, piece] - local_max)
        powers_ref[:, piece] = powers
        total = powers if total is None else total + powers
        if paired:
            _, powers = halves_of(powers, parity_ref[0], packed_ref.shape[1])
            powers = powers.reshape(-1, powers.shape[-1])
        both = [powers.astype(BF16), hits(words_ref, piece, 1.0, 0.0).astype(BF16)]
        part = dot(jnp.concatenate(both, axis=0), w_label_ref[:, piece], ((1,), (1,)))
        sums = part if sums is None else sums + part
    local_sum = jnp.sum(total, axis=1, keepdims=True)
    max_ref[...] = local_max
    matched = sums[-docs:]
    expected = sums[:-docs]
    picked = jnp.sum(hidden.astype(F32) * matched, axis=1, keepdims=True)
    picked = jnp.sum(picked / column_of(count_ref[...].astype(F32)), axis=0, keepdims=True)
    stats = stats_block(row_of(local_max + jnp.log(local_sum)), picked)
    if not paired:
        packed_ref[:, :width] = (expected / local_sum).astype(BF16)
        packed_ref[:, width : 2 * width] = matched.astype(BF16)
        for first in range(0, docs, stats.shape[0]):
            packed_ref[first : first + stats.shape[0], 2 * width :] = stats.astype(BF16)
        return
    keep_ref, sum_ref = keep_refs
    rows = packed_ref.shape[1]
    sum_ref[...], other_sum = halves_of(local_sum, parity_ref[0], rows)
    keep_ref[:, :, :width], other = halves_of(matched, parity_ref[0], rows)
    packed_ref[:, :, :width] = (expected.reshape(-1, rows, width) / other_sum).astype(BF16)
    packed_ref[:, :, width : 2 * width] = other.astype(BF16)
    wide = jnp.broadcast_to(stats[None], (keep_ref.shape[0],) + stats.shape)
    keep_ref[:, :, width:] = wide
    packed_ref[:, :, 2 * width :] = wide.astype(BF16)


def own_kernel(parity_ref, hidden_ref, features_ref, powers_ref, sum_ref, w_label_ref, *refs):
    expected_ref, hidden_turned_ref, features_turned_ref = refs
    half, rows, width = expected_ref.shape
    total = None
    for piece in chunks_of(w_label_ref.shape[1]):
        powers, _ = halves_of(powers_ref[:, piece], parity_ref[0], rows)
        powers = powers.reshape(half * rows, -1).astype(BF16)
        part = dot(powers, w_label_ref[:, piece], ((1,), (1,)))
        total = part if total is None else total + part
    expected_ref[...] = total.reshape(half, rows, width) / sum_ref[...]
    turn_kernel(hidden_ref, features_ref, hidden_turned_ref, features_turned_ref)


def read_stats(block, docs):
    part = docs // LANES
    lse = sum(block[..., i * part : (i + 1) * part, :] for i in range(3))
    return lse, block[..., 3 * part : 3 * part + 1, :]


def pair_kernel(parity_ref, expected_ref, keep_ref, got_ref, packed_ref):
    half, rows, width = expected_ref.shape
    docs = 2 * half * rows
    own_lse, own_scalar = read_stats(keep_ref[0, :, width:], docs)
    got_lse, got_scalar = read_stats(got_ref[0, :, 2 * width :].astype(F32), docs)
    top = jnp.maximum(own_lse, got_lse)
    lse = top + jnp.log(jnp.exp(own_lse - top) + jnp.exp(got_lse - top))
    expected = 0.0
    shares = [flat_row(jnp.exp(part_lse - lse)) for part_lse in (own_lse, got_lse)]
    columns = jnp.concatenate(shares * 4, axis=0).T
    columns, _ = halves_of(columns, parity_ref[0], rows)
    for index, ref in enumerate((expected_ref, got_ref)):
        expected = expected + columns[:, :, index : index + 1] * ref[:, :, :width].astype(F32)
    packed_ref[:, :, :width] = expected.astype(BF16)
    matched = keep_ref[:, :, :width] + got_ref[:, :, width : 2 * width].astype(F32)
    packed_ref[:, :, width : 2 * width] = matched.astype(BF16)
    scalar = jnp.sum(own_scalar + got_scalar, axis=1, keepdims=True)
    stats = stats_block(flat_row(lse), scalar).astype(BF16)
    packed_ref[:, :, 2 * width :] = jnp.broadcast_to(stats[None], (half,) + stats.shape)


def flat_row(rows):
    return jnp.concatenate([rows[i : i + 1] for i in range(rows.shape[0])], axis=1)


def combine(expected, matched, stats, own_hidden, own_count, first_row, docs):
    rows = own_hidden.shape[0]
    part = docs // LANES
    lse_parts, picked = read_stats(stats.astype(F32), docs)
    top = jnp.max(lse_parts, axis=0)
    lse = top + jnp.log(jnp.sum(jnp.exp(lse_parts - top), axis=0))
    picked = jnp.sum(picked, axis=0)
    loss = jnp.sum(jnp.sum(lse, axis=0, keepdims=True) - picked, axis=1, keepdims=True) / docs
    shares = jnp.exp(lse_parts - lse)
    own = lane((rows, LANES)) - lax.broadcasted_iota(jnp.int32, (rows, LANES), 0) - first_row
    share = 0.0
    for index in range(part):
        share = share + jnp.where(own + LANES * index == 0, shares[:, index : index + 1], 0.0)
    share = jnp.sum(share, axis=-1, keepdims=True)
    mean_matched = jnp.sum(matched.astype(F32), axis=0) / own_count
    grad_hidden = jnp.sum(share * expected.astype(F32), axis=0) - mean_matched
    hidden = own_hidden.astype(F32)
    grad_inner = (grad_hidden * (1.0 - hidden * hidden)).astype(BF16)
    return grad_inner, lse, loss


def combine_kernel(place_ref, got_ref, own_hidden_ref, count_ref, back_ref, lse_ref, loss_ref):
    rows, width = own_hidden_ref.shape
    docs = count_ref.shape[1]
    first_row = place_ref[0] * rows
    owner = lax.broadcasted_iota(jnp.int32, (rows, docs), 0) + first_row
    counts = jnp.where(lane((rows, docs)) == owner, count_ref[...], 0)
    own_count = jnp.sum(counts.astype(F32), axis=1, keepdims=True)
    grad_inner, lse_ref[...], loss = combine(
        got_ref[:, :, :width], got_ref[:, :, width : 2 * width], got_ref[:, :, 2 * width :],
        own_hidden_ref[...], own_count, first_row, docs,
    )
    loss_ref[...] = jnp.broadcast_to(loss, loss_ref.shape)
    half = width // 2
    for parity in (0, 1):
        part = grad_inner[:, parity * half : (parity + 1) * half]
        for index in range(parity, back_ref.shape[0], 2):
            back_ref[index] = part


def turn_kernel(hidden_ref, features_ref, hidden_turned_ref, features_turned_ref):
    hidden_turned_ref[...] = hidden_ref[...].T
    features_turned_ref[...] = features_ref[...].T


def label_kernel(hidden_ref, lse_ref, powers_ref, max_ref, words_ref, count_ref, grad_label_ref):
    scale = jnp.exp(max_ref[...] - column_of(flat_row(lse_ref[...])))
    per_match = column_of(1.0 / count_ref[...].astype(F32))
    hidden = hidden_ref[...]
    for piece in chunks_of(powers_ref.shape[1]):
        grad_logits = powers_ref[:, piece] * scale - hits(words_ref, piece, per_match, 0.0)
        grad_label_ref[:, piece] = dot(hidden, grad_logits.astype(BF16), ((1,), (0,))).astype(BF16)


def last_kernel(
    parity_ref, features_ref, label_ref, loss_ref, *refs,
):
    *grad_inner_refs, grad_first_hbm, grad_label_hbm, loss_hbm, first_scratch, sems = refs
    copies = [
        pltpu.make_async_copy(label_ref, grad_label_hbm, sems.at[0]),
        pltpu.make_async_copy(loss_ref, loss_hbm, sems.at[1]),
        pltpu.make_async_copy(first_scratch, grad_first_hbm, sems.at[2]),
    ]
    copies[0].start()
    copies[1].start()
    if len(grad_inner_refs) == 1:
        grad_inner = grad_inner_refs[0][...]
    else:
        own, other = (ref[...].astype(F32) for ref in grad_inner_refs)
        even = parity_ref[0] == 0
        both = [jnp.where(even, own, other), jnp.where(even, other, own)]
        grad_inner = jnp.concatenate(both, axis=1).astype(BF16)
    first_scratch[...] = dot(features_ref[...], grad_inner, ((1,), (0,))).astype(BF16)
    copies[2].start()
    for copy in copies:
        copy.wait()


def make_per_device(devices):
    def per_device(features, w_first, w_label, label_ids, label_count):
        docs, hidden_width = features.shape[0], w_first.shape[1]
        feats, labels = features.shape[1], w_label.shape[1]
        rows = max(1, docs // devices)
        cuts = devices * rows // docs
        width = hidden_width // cuts
        paired = cuts == 1 and rows == stats_rows(docs) and width % (2 * LANES) == 0

        def by_owner(x):
            if cuts == 1:
                return x.reshape(devices, rows, -1)
            return x.reshape(docs // rows, rows, cuts, -1).swapaxes(1, 2).reshape(devices, rows, -1)

        def by_document(x):
            if cuts == 1:
                return x.reshape(docs, -1)
            return x.reshape(docs // rows, cuts, rows, -1).swapaxes(1, 2).reshape(docs, -1)

        def exchange(x):
            return lax.all_to_all(x, AXES, 0, 0)

        def exchange_halves(x):
            groups = [list(range(first, devices, 2)) for first in (0, 1)]
            return lax.all_to_all(x, AXES, 0, 0, axis_index_groups=groups)

        def to_partner(x):
            return lax.ppermute(x, AXES, [(i, i ^ 1) for i in range(devices)])

        def to_all(x):
            return exchange(jnp.broadcast_to(x[None], (devices,) + x.shape))

        shape = jax.ShapeDtypeStruct
        place = lax.axis_index(AXES)
        count_row = label_count[None, :]

        offset, parity = (place * labels)[None], (place & 1)[None]
        offset, parity = lax.optimization_barrier((offset, parity))
        half = (devices // 2, rows, hidden_width)
        partial_value, send = kernel(
            first_kernel,
            "first",
            [SMEM] + [HBM] * 2,
            [shape(half if paired else (docs, hidden_width), F32), shape(half if paired else (8, LANES), F32)],
            grant=FIRST_GRANT,
            scratch_shapes=[
                pltpu.VMEM((docs, feats), BF16),
                pltpu.VMEM((feats, hidden_width), BF16),
                pltpu.SemaphoreType.DMA((2,)),
            ],
        )(parity, features, w_first)
        if paired:
            sums = exchange_halves(partial_value + to_partner(send))
        else:
            sums = exchange(by_owner(partial_value))
        own_hidden = jnp.tanh(jnp.sum(sums, axis=0)).astype(BF16)
        hidden = by_document(to_all(own_hidden))

        packed_width = 2 * hidden_width + LANES
        if paired:
            half = (devices // 2, rows, packed_width)
            packed_shapes = [
                shape(half, BF16),
                shape((devices // 2, rows, hidden_width + LANES), F32),
                shape((devices // 2, rows, 1), F32),
            ]
        else:
            packed_shapes = [shape((docs, packed_width), BF16)]
        powers, local_max, words, packed, *keep = kernel(
            softmax_kernel,
            "softmax",
            [SMEM] * 2 + [VMEM] * 4,
            [
                shape((docs, labels), F32),
                shape((docs, 1), F32),
                shape((docs, word_lanes(labels)), jnp.int32),
            ]
            + packed_shapes,
        )(offset, parity, label_ids.T, count_row, hidden, w_label)
        turned = [shape((hidden_width, docs), BF16), shape((feats, docs), BF16)]
        if paired:
            keep, own_sum = keep
            got = to_partner(packed)
            expected, *turned = kernel(
                own_kernel,
                "own",
                [SMEM] + [VMEM] * 5,
                [shape((devices // 2, rows, hidden_width), F32)] + turned,
            )(parity, hidden, features, powers, own_sum, w_label)
            got, expected, turned = lax.optimization_barrier((got, expected, turned))
            packed = kernel(pair_kernel, "pair", [SMEM] + [VMEM] * 3, shape(half, BF16))(
                parity, expected, keep, got
            )
            back, lse, loss = kernel(
                combine_kernel,
                "combine",
                [SMEM] + [VMEM] * 3,
                [
                    shape((devices, rows, width // 2), BF16),
                    shape((docs // LANES, LANES), F32),
                    shape((1, LANES), F32),
                ],
            )(place[None], exchange_halves(packed), own_hidden, count_row)
            own_inner = by_document(exchange(back))
            grad_inner = [own_inner, to_partner(own_inner)]
        else:
            turned = kernel(turn_kernel, "turn", [VMEM] * 2, turned)(hidden, features)
            stats = packed[: stats_rows(docs), 2 * hidden_width :]
            halves = by_owner(packed[:, : 2 * hidden_width].reshape(docs, 2, cuts, width).swapaxes(1, 2))
            flat = jnp.broadcast_to(stats.reshape(1, 1, -1), (devices, 1, stats.size))
            got = exchange(jnp.concatenate([halves.reshape(devices, 1, -1), flat], axis=-1))
            halves = got[:, 0, : -stats.size].reshape(devices, rows, 2, width)
            stats = got[:, 0, -stats.size :].reshape((devices,) + stats.shape)
            first_row = (place // cuts) * rows
            own_count = lax.dynamic_slice_in_dim(label_count, first_row, rows)[:, None].astype(F32)
            grad_inner, lse, loss = combine(
                halves[:, :, 0], halves[:, :, 1], stats, own_hidden, own_count, first_row, docs
            )
            loss = jnp.broadcast_to(loss, (1, LANES))
            grad_inner = [by_document(to_all(grad_inner))]

        hidden_turned, features_turned = turned
        grad_label = kernel(
            label_kernel, "label", [VMEM] * 6, shape((hidden_width, labels), BF16)
        )(hidden_turned, lse, powers, local_max, words, count_row)
        grad_first, grad_label, mean_loss = kernel(
            last_kernel,
            "last",
            [SMEM] + [VMEM] * (3 + len(grad_inner)),
            [
                shape((feats, hidden_width), BF16),
                shape((hidden_width, labels), BF16),
                shape((1, LANES), F32),
            ],
            out_specs=[HBM] * 3,
            scratch_shapes=[pltpu.VMEM((feats, hidden_width), BF16), pltpu.SemaphoreType.DMA((3,))],
        )(parity, features_turned, grad_label, loss, *grad_inner)
        return (grad_first, grad_label, mean_loss[0, 0])

    return per_device


def kernel(body, name, in_specs, out_shape, grant=GRANT, **more):
    several = isinstance(out_shape, list)
    specs = {"out_specs": [VMEM] * len(out_shape) if several else VMEM}
    return pl.pallas_call(
        body,
        name=name,
        in_specs=in_specs,
        out_shape=out_shape,
        compiler_params=pltpu.CompilerParams(vmem_limit_bytes=grant),
        **(specs | more),
    )


def solution(mesh):
    placed = (P(None, AXES), P(AXES, None), P(None, AXES), P(), P())
    devices = mesh.shape["gx"] * mesh.shape["gy"]
    return jax.shard_map(
        make_per_device(devices),
        mesh=mesh,
        in_specs=placed,
        out_specs=(P(AXES, None), P(None, AXES), P()),
        check_vma=False,
    )
```
